32 devices in a mesh: enc: 2 (over x), batch: 16 (over z, y, core).
Axes of the slice: x: 2, y: 2, z: 4, core: 2. Of those that a mesh axis runs over, the one named last changes fastest.
Arguments:
- tokens: bfloat16 [2, 16384, 768], P('enc', 'batch'), may hold values from -6 to 6
- cotangent: bfloat16 [2, 16384, 768], P('enc', 'batch'), may hold values from -6 to 6
- question_lengths: int32 [16, 8], P('batch'), may hold values from 1 to 64, 320 in all within a row
- passage_lengths: int32 [16, 8], P('batch'), may hold values from 1 to 256, 1024 in all within a row
- attend_weight: bfloat16 [2, 768, 2304], P('enc'), may hold values from -0.21875 to 0.21875
- query_bias: bfloat16 [2, 768], P('enc'), may hold values from -1 to 1
- value_bias: bfloat16 [2, 768], P('enc'), may hold values from -1 to 1
- output_weight: bfloat16 [2, 768, 768], P('enc'), may hold values from -0.875 to 0.875
- output_bias: bfloat16 [2, 768], P('enc'), may hold values from -1 to 1
- first_gain: bfloat16 [2, 768], P('enc'), may hold values from 0.5 to 1.5
- first_shift: bfloat16 [2, 768], P('enc'), may hold values from -1 to 1
- expand_weight: bfloat16 [2, 768, 3072], P('enc'), may hold values from -0.21875 to 0.21875
- expand_bias: bfloat16 [2, 3072], P('enc'), may hold values from -1 to 1
- reduce_weight: bfloat16 [2, 3072, 768], P('enc'), may hold values from -0.109375 to 0.109375
- reduce_bias: bfloat16 [2, 768], P('enc'), may hold values from -1 to 1
- second_gain: bfloat16 [2, 768], P('enc'), may hold values from 0.5 to 1.5
- second_shift: bfloat16 [2, 768], P('enc'), may hold values from -1 to 1
Outputs:
- layer_output: bfloat16 [2, 16384, 768], P('enc', 'batch')
- tokens_gradient: bfloat16 [2, 16384, 768], P('enc', 'batch')
- attend_weight_gradient: float32 [2, 768, 2304], P('enc', 'batch')
- query_bias_gradient: float32 [2, 768], P('enc', 'batch')
- value_bias_gradient: float32 [2, 768], P('enc', 'batch')
- output_weight_gradient: float32 [2, 768, 768], P('enc', 'batch')
- output_bias_gradient: float32 [2, 768], P('enc', 'batch')
- first_gain_gradient: float32 [2, 768], P('enc', 'batch')
- first_shift_gradient: float32 [2, 768], P('enc', 'batch')
- expand_weight_gradient: float32 [2, 768, 3072], P('enc', 'batch')
- expand_bias_gradient: float32 [2, 3072], P('enc', 'batch')
- reduce_weight_gradient: float32 [2, 3072, 768], P('enc', 'batch')
- reduce_bias_gradient: float32 [2, 768], P('enc', 'batch')
- second_gain_gradient: float32 [2, 768], P('enc', 'batch')
- second_shift_gradient: float32 [2, 768], P('enc', 'batch')
The draws below stay inside these ranges and needn't reach their ends.
Inputs may be any that keep to these rules, and one draw needn't show every extreme that they name: `question_lengths`: each row sums to 320; the longest question of each row has exactly 64 tokens. `passage_lengths`: each row sums to 1024; the longest passage of each row has exactly 256 tokens.
All inputs are finite; a program needn't handle non-finite values.
Results may differ from the reference program's by a relative error of at most 0.013.
Values may be sent and summed in bfloat16 or wider, within the bound.
No kernel may reach another device: no remote copies, remote signals or barrier semaphores. Data moves between devices by JAX's collectives and lax.ppermute only.
A program may use at most 256 MiB of HBM per device.

```python
import math
import jax
import jax.numpy as jnp
import numpy as np
from jax import lax

D = 768
HEADS = 12
HEAD_DIM = 64
FF = 3072
SEQ_DEV = 8
QLEN = 64
TOK_DEV = 1024
PLEN = 256
Q_TOK = 320
TOKENS = 16384
SEQS = 128
N_BATCH = 16


def strengthened(entries, key, source, target, blocks, factor):
    owner, partner = [(jnp.arange(entries.shape[dim]) // (entries.shape[dim] // blocks)).reshape([-1 if axis == dim else 1 for axis in range(entries.ndim)]) for dim in (source, target)]
    chosen = jax.random.permutation(key, blocks)[partner]
    strong = (owner == chosen) | (owner == (partner + blocks // 2) % blocks)
    return jnp.where(strong, factor * entries, entries)


def levels(rng, shape, cuts, least, high):
    gain, own = 1.0, jax.random.fold_in(rng, 6)
    for position, blocks in cuts:
        steps = jnp.exp(jax.random.uniform(jax.random.fold_in(own, position), (blocks,), jnp.float32, least / len(cuts), high / len(cuts)))
        gain = gain * jnp.repeat(steps, shape[position] // blocks).reshape([-1 if axis == position else 1 for axis in range(len(shape))])
    return gain


def length_profile(count, total, bound, lean):
    loads = [(1 << 20) // math.isqrt(grade ** lean) + 1 for grade in range(2, count + 1)]
    rest, counts = total - bound - (count - 1), [1] * (count - 1)
    while rest > 0:
        free = [i for i in range(count - 1) if counts[i] < bound]
        mass, left = sum([loads[i] for i in free]), rest
        for i in free:
            extra = min(bound - counts[i], max(1, left * loads[i] // mass), rest)
            counts[i] = counts[i] + extra
            rest = rest - extra
    return np.array([bound] + counts)


def uneven(rng, amount, total, most, lean):
    if amount == 2:
        one = jax.random.randint(rng, (), max(1, total - most), min(most, total - 1) + 1)
        return jnp.stack([one, total - one])
    tallies = jnp.asarray(length_profile(amount, total, most, lean), jnp.int32)
    pairs = (amount - 1) // 2
    source_of, sink = tallies[1:1 + 2 * pairs:2], tallies[2:2 + 2 * pairs:2]
    room = jnp.minimum(source_of - 1, most - sink)
    passed = jax.random.randint(jax.random.fold_in(rng, 1), (pairs,), 0, 1 << 20) % (room + 1)
    tallies = tallies.at[1:1 + 2 * pairs:2].set(source_of - passed).at[2:2 + 2 * pairs:2].set(sink + passed)
    return tallies[jax.random.permutation(jax.random.fold_in(rng, 2), amount)]


def normal_values(key, shape, scale, most, cuts=(), kind=jnp.bfloat16):
    entries = scale * jax.random.normal(key, shape, jnp.float32)
    if cuts:
        entries = entries * levels(key, shape, cuts, -0.22, 0.18)
    return jnp.clip(entries, -most, most).astype(kind)


def noise_with(stream_key, dims, spread, bound, split, heavy, kind=jnp.bfloat16):
    drawn = spread * jax.random.normal(stream_key, dims, jnp.float32)
    if split:
        drawn = drawn * levels(stream_key, dims, split, -0.22, 0.18)
    return jnp.clip(strengthened(drawn, jax.random.fold_in(stream_key, 3), *heavy), -bound, bound).astype(kind)


def setup_inputs(seed: int = 0) -> dict:
    arg_keys = jax.random.split(jax.random.key(seed), 18)
    return {
        "tokens": normal_values(arg_keys[0], (2, TOKENS, D), 1.0, 6.0, ((0, 2), (1, 16))),
        "cotangent": noise_with(arg_keys[1], (2, TOKENS, D), 1.0, 6.0, ((0, 2), (1, 16)), (1, 2, 16, 2.0)),
        "question_lengths": jax.vmap(lambda own: uneven(own, SEQ_DEV, Q_TOK, QLEN, 2))(jax.random.split(arg_keys[2], N_BATCH)).reshape((N_BATCH, SEQ_DEV)).astype(jnp.int32),
        "passage_lengths": jax.vmap(lambda own: uneven(own, SEQ_DEV, TOK_DEV, PLEN, 2))(jax.random.split(arg_keys[3], N_BATCH)).reshape((N_BATCH, SEQ_DEV)).astype(jnp.int32),
        "attend_weight": normal_values(arg_keys[4], (2, D, 3 * D), D ** -0.5, 0.21875, ((0, 2),)),
        "query_bias": normal_values(arg_keys[5], (2, D), 0.2, 1.0, ((0, 2),)),
        "value_bias": normal_values(arg_keys[6], (2, D), 0.2, 1.0, ((0, 2),)),
        "output_weight": normal_values(arg_keys[7], (2, D, D), (D // 16) ** -0.5, 0.875, ((0, 2),)),
        "output_bias": normal_values(arg_keys[8], (2, D), 0.2, 1.0, ((0, 2),)),
        "first_gain": jnp.clip(1.0 + 0.1 * jax.random.normal(arg_keys[9], (2, D), jnp.float32), 0.5, 1.5).astype(jnp.bfloat16),
        "first_shift": normal_values(arg_keys[10], (2, D), 0.2, 1.0, ((0, 2),)),
        "expand_weight": normal_values(arg_keys[11], (2, D, FF), D ** -0.5, 0.21875, ((0, 2),)),
        "expand_bias": normal_values(arg_keys[12], (2, FF), 0.2, 1.0, ((0, 2),)),
        "reduce_weight": normal_values(arg_keys[13], (2, FF, D), FF ** -0.5, 0.109375, ((0, 2),)),
        "reduce_bias": normal_values(arg_keys[14], (2, D), 0.2, 1.0, ((0, 2),)),
        "second_gain": jnp.clip(1.0 + 0.1 * jax.random.normal(arg_keys[15], (2, D), jnp.float32), 0.5, 1.5).astype(jnp.bfloat16),
        "second_shift": normal_values(arg_keys[16], (2, D), 0.2, 1.0, ((0, 2),)),
    }


EPSILON = 1e-12
SCORE_SCALE = 0.125
MASKED = -1000000000.0
LOSS_WEIGHT = 16.0
INV_ROOT_TWO = 0.7071067811865476

@jax.custom_vjp
def low(v):
    return lax.optimization_barrier(v.astype(jnp.bfloat16)).astype(jnp.float32)

@jax.custom_vjp
def low_back(v):
    return v

def low_keep(v):
    return (low(v), None)

def low_pass(kept, grad):
    return (grad,)

def back_keep(v):
    return (v, None)

def back_low(kept, grad):
    return (low(grad),)
low.defvjp(low_keep, low_pass)
low_back.defvjp(back_keep, back_low)

def matmul(left_side, right_side):
    return jnp.dot(left_side, right_side, precision=lax.Precision.HIGHEST)

def layer_norm(values, scale_row, shift_row):
    centred = values - lax.optimization_barrier(jnp.mean(values, axis=-1, keepdims=True))
    variance = lax.optimization_barrier(jnp.mean(centred * centred, axis=-1, keepdims=True))
    return centred * lax.rsqrt(variance + EPSILON) * scale_row + shift_row

def segment_ids(lengths_row):
    row_ends = jnp.cumsum(lengths_row).astype(jnp.int32)
    slot_index = jnp.arange(TOK_DEV, dtype=jnp.int32)
    return lax.optimization_barrier(jnp.sum((slot_index[:, None] >= row_ends[None, :]).astype(jnp.int32), axis=1)).astype(jnp.int32)

def encoder_layer(params, block_inputs, segments):
    attend_matrix, query_offset, value_offset, output_matrix, output_offset, first_scale, first_offset, expand_matrix, expand_offset, reduce_matrix, reduce_offset, second_scale, second_offset = params
    slot_count = block_inputs.shape[0]
    bias_full = jnp.concatenate([query_offset, jnp.zeros_like(query_offset), value_offset])
    projected = low(low_back(matmul(block_inputs, attend_matrix) + bias_full))
    query_rows = projected[:, :D].reshape(slot_count, HEADS, HEAD_DIM)
    key_rows = projected[:, D:2 * D].reshape(slot_count, HEADS, HEAD_DIM)
    value_rows = projected[:, 2 * D:].reshape(slot_count, HEADS, HEAD_DIM)
    scores = jnp.einsum('qhe,khe->hqk', query_rows, key_rows, precision=lax.Precision.HIGHEST) * SCORE_SCALE
    same_segment = segments[:, None] == segments[None, :]
    scores = low_back(jnp.where(same_segment[None], scores, MASKED))
    totals = jax.nn.logsumexp(scores, axis=-1, keepdims=True)
    weights_soft = low(jnp.exp(scores - totals))
    context = jnp.einsum('hqk,khe->qhe', weights_soft, value_rows, precision=lax.Precision.HIGHEST)
    context = low(low_back(context.reshape(slot_count, D)))
    branch = low_back(matmul(context, output_matrix) + output_offset)
    hidden = layer_norm(block_inputs + branch, first_scale, first_offset)
    inner = low_back(matmul(low(hidden), expand_matrix) + expand_offset)
    active = low(0.5 * inner * (1.0 + lax.erf(inner * INV_ROOT_TWO)))
    second = low_back(matmul(active, reduce_matrix) + reduce_offset)
    return layer_norm(hidden + second, second_scale, second_offset)

def pick_rows(block_out, row_starts):
    return jnp.take(block_out, row_starts, axis=0)

def forward(params, inputs, segments_all, starts_all):
    outputs_all = []
    for encoder_side in range(2):
        side_params = tuple((parameter[encoder_side] for parameter in params))

        def run_block(block_pair):
            return encoder_layer(side_params, block_pair[0], block_pair[1])
        outputs_all.append(lax.map(jax.checkpoint(run_block), (inputs[encoder_side], segments_all[encoder_side])))
    question_heads = jax.vmap(pick_rows)(outputs_all[0], starts_all[0]).reshape(SEQS, D)
    passage_heads = jax.vmap(pick_rows)(outputs_all[1], starts_all[1]).reshape(SEQS, D)
    question_summary = low(low_back(question_heads))
    passage_summary = low(passage_heads)
    logits = low_back(matmul(question_summary, passage_summary.T) * (2.0 / math.sqrt(D)))
    loss_value = jnp.sum(jax.nn.logsumexp(logits, axis=1) - jnp.diagonal(logits))
    return (jnp.stack(outputs_all), loss_value)

def reference(tokens, cotangent, question_lengths, passage_lengths, attend_weight, query_bias, value_bias, output_weight, output_bias, first_gain, first_shift, expand_weight, expand_bias, reduce_weight, reduce_bias, second_gain, second_shift):
    params = tuple((parameter.astype(jnp.float32) for parameter in (attend_weight, query_bias, value_bias, output_weight, output_bias, first_gain, first_shift, expand_weight, expand_bias, reduce_weight, reduce_bias, second_gain, second_shift)))
    inputs = tokens.astype(jnp.float32).reshape(2, N_BATCH, TOK_DEV, D)
    lengths_all = jnp.stack([question_lengths, passage_lengths]).astype(jnp.int32)
    segments_all = jax.vmap(jax.vmap(segment_ids))(lengths_all)
    ends_all = jnp.cumsum(lengths_all, axis=2).astype(jnp.int32)
    starts_all = (ends_all - lengths_all).astype(jnp.int32)
    slot_index = jnp.arange(TOK_DEV, dtype=jnp.int32)
    live = (slot_index[None, None, :] < ends_all[:, :, -1:]).astype(jnp.float32)

    def objective(param_set, input_set):
        return forward(param_set, input_set, segments_all, starts_all)
    (outputs, loss_value), pullback = jax.vjp(objective, params, inputs)
    upstream = cotangent.astype(jnp.float32).reshape(2, N_BATCH, TOK_DEV, D) * live[..., None]
    param_grads, input_grads = pullback((upstream, jnp.ones_like(loss_value) * LOSS_WEIGHT))
    attend_gradient, query_gradient, value_gradient, output_gradient, output_bias_gradient, first_gain_gradient, first_shift_gradient, expand_gradient, expand_bias_gradient, reduce_gradient, reduce_bias_gradient, second_gain_gradient, second_shift_gradient = param_grads
    return (outputs.reshape(2, TOKENS, D).astype(jnp.bfloat16), input_grads.reshape(2, TOKENS, D).astype(jnp.bfloat16), attend_gradient, query_gradient, value_gradient, output_gradient, output_bias_gradient, first_gain_gradient, first_shift_gradient, expand_gradient, expand_bias_gradient, reduce_gradient, reduce_bias_gradient, second_gain_gradient, second_shift_gradient)
```

```python
import math

import jax
import jax.numpy as jnp
from jax import lax
from jax.sharding import PartitionSpec as P

D = 768
HEADS = 12
HEAD_DIM = 64


EPSILON = 1e-12
SCORE_SCALE = 0.125
MASKED = -1000000000.0
LOSS_WEIGHT = 16.0
INV_ROOT_TWO = 0.7071067811865476
INV_ROOT_TAU = 0.3989422804014327


def exchanged(value, axes, distance):
    count = math.prod(lax.axis_size(axis) for axis in axes)
    return lax.ppermute(value, axes, [(source, source ^ distance) for source in range(count)])


def gathered_summaries(summary):
    count = lax.axis_size("batch")
    if count != 16:
        everything = lax.all_gather(summary, ("enc", "batch"), axis=0, tiled=False)
        own = lax.axis_index("enc")
        everything = everything.reshape((2, count) + summary.shape)
        mine = lax.dynamic_index_in_dim(everything, own, 0, keepdims=False)
        other = lax.dynamic_index_in_dim(everything, 1 - own, 0, keepdims=False)
        return mine, other, lax.axis_index("batch")
    both = ("enc", "batch")
    pair = jnp.stack([summary, exchanged(summary, both, 1)])
    mine = [pair, exchanged(pair, both, 2)]
    other = [exchanged(pair, both, 16), exchanged(pair, both, 18)]
    plane = jnp.concatenate(mine + other)
    parts = [plane] + [exchanged(plane, both, distance) for distance in (4, 8, 12)]
    size = plane.shape[0] // 2
    return (
        jnp.concatenate([part[:size] for part in parts]),
        jnp.concatenate([part[size:] for part in parts]),
        0,
    )


def scattered_sum(pieces):
    count = lax.axis_size("batch")
    if count & (count - 1):
        return lax.psum_scatter(pieces, "batch", scatter_dimension=0, tiled=False).astype(
            jnp.float32
        )
    own = lax.axis_index("batch")
    bits = count.bit_length() - 1
    rest = pieces.shape[1:]
    terms = [pieces.reshape((2,) * bits + rest)]
    for bit in range(bits):
        side = (own >> bit) & 1
        axis = bits - 1 - bit
        sent = sum(
            lax.dynamic_index_in_dim(term, 1 - side, axis, keepdims=False).astype(jnp.float32)
            for term in terms
        ).astype(pieces.dtype)
        terms = [lax.dynamic_index_in_dim(term, side, axis, keepdims=False) for term in terms]
        terms.append(exchanged(sent, ("batch",), 1 << bit))
    return sum(term.astype(jnp.float32) for term in terms)


def product(left_side, right_side):
    return jnp.dot(left_side, right_side, preferred_element_type=jnp.float32)


def contract_rows(left_side, right_side):
    return lax.dot_general(
        left_side, right_side, (((0,), (0,)), ((), ())), preferred_element_type=jnp.float32
    )


def contract_cols(left_side, right_side):
    return lax.dot_general(
        left_side, right_side, (((1,), (1,)), ((), ())), preferred_element_type=jnp.float32
    )


def norm_forward(values, scale_row, shift_row):
    centred = values - jnp.mean(values, axis=1, keepdims=True)
    inverse = lax.rsqrt(jnp.mean(centred * centred, axis=1, keepdims=True) + EPSILON)
    normed = centred * inverse
    return (normed * scale_row + shift_row, normed, inverse)


def norm_backward(upstream, normed, inverse, scale_row):
    scale_grad = jnp.sum(upstream * normed, axis=0)
    shift_grad = jnp.sum(upstream, axis=0)
    scaled = upstream * scale_row
    centred = scaled - jnp.mean(scaled, axis=1, keepdims=True)
    centred = centred - normed * jnp.mean(scaled * normed, axis=1, keepdims=True)
    return (centred * inverse, scale_grad, shift_grad)


def block_scores(query_block, key_rows, segment_block, segments):
    scores = (
        jnp.einsum("qhe,khe->hqk", query_block, key_rows, preferred_element_type=jnp.float32)
        * SCORE_SCALE
    )
    same_segment = segment_block[:, None] == segments[None, :]
    return jnp.where(same_segment[None], scores, MASKED)


def per_device(
    tokens,
    cotangent,
    question_lengths,
    passage_lengths,
    attend_weight,
    query_bias,
    value_bias,
    output_weight,
    output_bias,
    first_gain,
    first_shift,
    expand_weight,
    expand_bias,
    reduce_weight,
    reduce_bias,
    second_gain,
    second_shift,
):
    inputs = tokens[0]
    attend_matrix = attend_weight[0]
    output_matrix = output_weight[0]
    expand_matrix = expand_weight[0]
    reduce_matrix = reduce_weight[0]
    first_scale = first_gain[0].astype(jnp.float32)
    second_scale = second_gain[0].astype(jnp.float32)
    slot_count = inputs.shape[0]
    window = min(512, slot_count)
    is_passage = lax.axis_index("enc") == 1
    lengths_here = jnp.where(is_passage, passage_lengths[0], question_lengths[0])
    order = jnp.arange(lengths_here.shape[0], dtype=jnp.int32)
    ends_here = jnp.sum(
        jnp.where(order[None, :] <= order[:, None], lengths_here[None, :], 0), axis=1
    )
    starts_here = ends_here - lengths_here
    slot_index = jnp.arange(slot_count, dtype=jnp.int32)
    segments = jnp.sum((slot_index[:, None] >= ends_here[None, :]).astype(jnp.int32), axis=1)
    live = (slot_index < ends_here[-1]).astype(jnp.float32)
    bias_full = jnp.concatenate(
        [
            query_bias[0].astype(jnp.float32),
            jnp.zeros((D,), jnp.float32),
            value_bias[0].astype(jnp.float32),
        ]
    )
    projected = (product(inputs, attend_matrix) + bias_full).astype(jnp.bfloat16)
    query_rows = projected[:, :D].reshape(slot_count, HEADS, HEAD_DIM)
    key_rows = projected[:, D : 2 * D].reshape(slot_count, HEADS, HEAD_DIM)
    value_rows = projected[:, 2 * D :].reshape(slot_count, HEADS, HEAD_DIM)
    contexts = []
    totals = []
    for number in range(slot_count // window):
        offset = number * window
        scores = block_scores(
            query_rows[offset : offset + window],
            key_rows,
            segments[offset : offset + window],
            segments,
        )
        highest = jnp.max(scores, axis=-1, keepdims=True)
        total_block = highest + jnp.log(jnp.sum(jnp.exp(scores - highest), axis=-1, keepdims=True))
        weights_soft = jnp.exp(scores - total_block).astype(jnp.bfloat16)
        contexts.append(
            jnp.einsum("hqk,khe->qhe", weights_soft, value_rows, preferred_element_type=jnp.float32)
        )
        totals.append(total_block)
    context = jnp.concatenate(contexts, axis=0).reshape(slot_count, D).astype(jnp.bfloat16)
    branch = product(context, output_matrix) + output_bias[0].astype(jnp.float32)
    hidden, normed_one, inverse_one = norm_forward(
        inputs.astype(jnp.float32) + branch, first_scale, first_shift[0].astype(jnp.float32)
    )
    hidden_low = hidden.astype(jnp.bfloat16)
    inner = product(hidden_low, expand_matrix) + expand_bias[0].astype(jnp.float32)
    normal_cdf = 0.5 * (1.0 + lax.erf(inner * INV_ROOT_TWO))
    active = (inner * normal_cdf).astype(jnp.bfloat16)
    second = product(active, reduce_matrix) + reduce_bias[0].astype(jnp.float32)
    result, normed_two, inverse_two = norm_forward(
        hidden + second, second_scale, second_shift[0].astype(jnp.float32)
    )
    chosen = (starts_here[:, None] == slot_index[None, :]).astype(jnp.bfloat16)
    summary = product(chosen, result.astype(jnp.bfloat16)).astype(jnp.bfloat16)
    mine, other, place = gathered_summaries(summary)
    seq_count = summary.shape[0]
    mine, other = mine.reshape(-1, D), other.reshape(-1, D)
    questions = jnp.where(is_passage, other, mine)
    passages = jnp.where(is_passage, mine, other)
    summary_scale = 2.0 / math.sqrt(D)
    total_seqs = questions.shape[0]
    logits = contract_cols(questions, passages) * summary_scale
    highest_logit = jnp.max(logits, axis=1, keepdims=True)
    logit_total = highest_logit + jnp.log(
        jnp.sum(jnp.exp(logits - highest_logit), axis=1, keepdims=True)
    )
    matches = jnp.eye(total_seqs, dtype=jnp.float32)
    score_grad = (LOSS_WEIGHT * (jnp.exp(logits - logit_total) - matches)).astype(jnp.bfloat16)
    own_rows = lax.dynamic_slice_in_dim(score_grad, place * seq_count, seq_count, 0)
    own_columns = lax.dynamic_slice_in_dim(score_grad, place * seq_count, seq_count, 1)
    question_term = (product(own_rows, passages) * summary_scale).astype(jnp.bfloat16)
    passage_term = contract_rows(own_columns, questions) * summary_scale
    summary_grad = jnp.where(is_passage, passage_term, question_term.astype(jnp.float32))
    upstream = cotangent[0].astype(jnp.float32) * live[:, None]
    upstream = upstream + lax.dot_general(
        chosen.astype(jnp.float32),
        summary_grad,
        (((0,), (0,)), ((), ())),
        precision=lax.Precision.HIGHEST,
        preferred_element_type=jnp.float32,
    )
    residual_two_grad, second_gain_grad, second_shift_grad = norm_backward(
        upstream, normed_two, inverse_two, second_scale
    )
    reduce_input = residual_two_grad.astype(jnp.bfloat16)
    reduce_grad = contract_rows(active, reduce_input)
    reduce_bias_grad = jnp.sum(reduce_input.astype(jnp.float32), axis=0)
    active_grad = contract_cols(reduce_input, reduce_matrix)
    slope = normal_cdf + inner * jnp.exp(-0.5 * inner * inner) * INV_ROOT_TAU
    inner_grad = (active_grad * slope).astype(jnp.bfloat16)
    expand_grad = contract_rows(hidden_low, inner_grad)
    expand_bias_grad = jnp.sum(inner_grad.astype(jnp.float32), axis=0)
    hidden_grad = residual_two_grad + contract_cols(inner_grad, expand_matrix)
    residual_one_grad, first_gain_grad, first_shift_grad = norm_backward(
        hidden_grad, normed_one, inverse_one, first_scale
    )
    branch_grad = residual_one_grad.astype(jnp.bfloat16)
    output_grad = contract_rows(context, branch_grad)
    output_bias_grad = jnp.sum(branch_grad.astype(jnp.float32), axis=0)
    context_grad = contract_cols(branch_grad, output_matrix).astype(jnp.bfloat16)
    context_grad = context_grad.reshape(slot_count, HEADS, HEAD_DIM)
    query_grads = []
    key_grad = jnp.zeros((slot_count, HEADS, HEAD_DIM), jnp.float32)
    value_grad = jnp.zeros((slot_count, HEADS, HEAD_DIM), jnp.float32)
    for number in range(slot_count // window):
        offset = number * window
        query_block = query_rows[offset : offset + window]
        scores = block_scores(query_block, key_rows, segments[offset : offset + window], segments)
        weights_soft = jnp.exp(scores - totals[number])
        context_block = context_grad[offset : offset + window]
        soft_grad = jnp.einsum(
            "qhe,khe->hqk", context_block, value_rows, preferred_element_type=jnp.float32
        )
        row_delta = jnp.sum(soft_grad * weights_soft, axis=-1, keepdims=True)
        attn_grad = (weights_soft * (soft_grad - row_delta)).astype(jnp.bfloat16)
        query_grads.append(
            jnp.einsum("hqk,khe->qhe", attn_grad, key_rows, preferred_element_type=jnp.float32)
            * SCORE_SCALE
        )
        key_grad = (
            key_grad
            + jnp.einsum("hqk,qhe->khe", attn_grad, query_block, preferred_element_type=jnp.float32)
            * SCORE_SCALE
        )
        value_grad = value_grad + jnp.einsum(
            "hqk,qhe->khe",
            weights_soft.astype(jnp.bfloat16),
            context_block,
            preferred_element_type=jnp.float32,
        )
    query_grad = jnp.concatenate(query_grads, axis=0)
    projected_grad = jnp.concatenate(
        [
            query_grad.reshape(slot_count, D),
            key_grad.reshape(slot_count, D),
            value_grad.reshape(slot_count, D),
        ],
        axis=1,
    ).astype(jnp.bfloat16)
    attend_grad = contract_rows(inputs, projected_grad)
    query_bias_grad = jnp.sum(projected_grad[:, :D].astype(jnp.float32), axis=0)
    value_bias_grad = jnp.sum(projected_grad[:, 2 * D :].astype(jnp.float32), axis=0)
    tokens_grad = (residual_one_grad + contract_cols(projected_grad, attend_matrix)).astype(
        jnp.bfloat16
    )
    count = lax.axis_size("batch")

    def share(gradient):
        return scattered_sum(
            gradient.astype(jnp.bfloat16).reshape(count, gradient.shape[0] // count, -1)
        )[None]

    vectors = (
        query_bias_grad,
        value_bias_grad,
        output_bias_grad,
        first_gain_grad,
        first_shift_grad,
        reduce_bias_grad,
        second_gain_grad,
        second_shift_grad,
        expand_bias_grad,
    )
    packed = jnp.concatenate([vector.reshape(count, -1) for vector in vectors], axis=1)
    small = scattered_sum(packed)
    width = D // count
    small_shares = [small[None, i * width : (i + 1) * width] for i in range(8)]
    small_shares.append(small[None, 8 * width :])
    return (
        result.astype(jnp.bfloat16)[None],
        tokens_grad[None],
        share(attend_grad),
        small_shares[0],
        small_shares[1],
        share(output_grad),
        small_shares[2],
        small_shares[3],
        small_shares[4],
        share(expand_grad),
        small_shares[8],
        share(reduce_grad),
        small_shares[5],
        small_shares[6],
        small_shares[7],
    )


def solution(mesh):
    in_specs = (
        P("enc", "batch", None),
        P("enc", "batch", None),
        P("batch", None),
        P("batch", None),
        P("enc", None, None),
        P("enc", None),
        P("enc", None),
        P("enc", None, None),
        P("enc", None),
        P("enc", None),
        P("enc", None),
        P("enc", None, None),
        P("enc", None),
        P("enc", None, None),
        P("enc", None),
        P("enc", None),
        P("enc", None),
    )
    out_specs = (
        P("enc", "batch", None),
        P("enc", "batch", None),
        P("enc", "batch", None),
        P("enc", "batch"),
        P("enc", "batch"),
        P("enc", "batch", None),
        P("enc", "batch"),
        P("enc", "batch"),
        P("enc", "batch"),
        P("enc", "batch", None),
        P("enc", "batch"),
        P("enc", "batch", None),
        P("enc", "batch"),
        P("enc", "batch"),
        P("enc", "batch"),
    )
    return jax.shard_map(
        per_device, mesh=mesh, in_specs=in_specs, out_specs=out_specs, check_vma=False
    )
```

```python
import math

import jax
import jax.numpy as jnp
from jax import lax
from jax.experimental import pallas as pl
from jax.experimental.pallas import tpu as pltpu
from jax.sharding import PartitionSpec as P

D = 768
HEADS = 12
HEAD_DIM = 64
TILE = 128
WIDE = 2 * TILE
PAIRS = HEADS // 2
ROWS = 16


EPSILON = 1e-12
SCORE_SCALE = 0.125
MASKED = -1000000000.0
LOSS_WEIGHT = 16.0
INV_ROOT_TWO = 0.7071067811865476
INV_ROOT_TAU = 0.3989422804014327


def exchanged(value, axes, distance):
    count = math.prod(lax.axis_size(axis) for axis in axes)
    return lax.ppermute(value, axes, [(source, source ^ distance) for source in range(count)])


def gathered_summaries(summary):
    count = lax.axis_size("batch")
    if count != 16:
        everything = lax.all_gather(summary, ("enc", "batch"), axis=0, tiled=False)
        own = lax.axis_index("enc")
        everything = everything.reshape((2, count) + summary.shape)
        mine = lax.dynamic_index_in_dim(everything, own, 0, keepdims=False)
        other = lax.dynamic_index_in_dim(everything, 1 - own, 0, keepdims=False)
        return mine, other, lax.axis_index("batch")
    both = ("enc", "batch")
    pair = jnp.stack([summary, exchanged(summary, both, 1)])
    mine = [pair, exchanged(pair, both, 2)]
    other = [exchanged(pair, both, 16), exchanged(pair, both, 18)]
    plane = jnp.concatenate(mine + other)
    parts = [plane] + [exchanged(plane, both, distance) for distance in (4, 8, 12)]
    size = plane.shape[0] // 2
    return (
        jnp.concatenate([part[:size] for part in parts]),
        jnp.concatenate([part[size:] for part in parts]),
        0,
    )


class Scatter:
    def __init__(self, pieces):
        self.count = lax.axis_size("batch")
        self.bits = self.count.bit_length() - 1
        self.kind = pieces.dtype
        self.stage = 0
        self.whole = pieces
        self.terms = [pieces.reshape((2,) * self.bits + pieces.shape[1:])]
        self.halving = not self.count & (self.count - 1)

    def outgoing(self):
        side = (lax.axis_index("batch") >> self.stage) & 1
        axis = self.bits - 1 - self.stage
        sent = sum(
            lax.dynamic_index_in_dim(term, 1 - side, axis, keepdims=False).astype(jnp.float32)
            for term in self.terms
        ).astype(self.kind)
        self.terms = [
            lax.dynamic_index_in_dim(term, side, axis, keepdims=False) for term in self.terms
        ]
        return sent

    def begin(self, since=None, ahead=None):
        if not self.halving or self.stage == self.bits:
            return ahead
        if since is not None:
            self.terms = list(lax.optimization_barrier((tuple(self.terms), since))[0])
        sent = self.outgoing()
        if ahead is not None:
            sent, ahead = lax.optimization_barrier((sent, ahead))
        self.terms.append(exchanged(sent, ("batch",), 1 << self.stage))
        self.stage += 1
        return ahead

    def result(self):
        if not self.halving:
            return lax.psum_scatter(
                self.whole.astype(jnp.float32), "batch", scatter_dimension=0, tiled=False
            )
        while self.stage < self.bits:
            self.begin()
        return sum(term.astype(jnp.float32) for term in self.terms)


def product(left_side, right_side):
    return jnp.dot(left_side, right_side, preferred_element_type=jnp.float32)


def contract_rows(left_side, right_side):
    return lax.dot_general(
        left_side, right_side, (((0,), (0,)), ((), ())), preferred_element_type=jnp.float32
    )


def contract_cols(left_side, right_side):
    return lax.dot_general(
        left_side, right_side, (((1,), (1,)), ((), ())), preferred_element_type=jnp.float32
    )


def norm_forward(values, scale_row, shift_row):
    centred = values - jnp.mean(values, axis=1, keepdims=True)
    inverse = lax.rsqrt(jnp.mean(centred * centred, axis=1, keepdims=True) + EPSILON)
    normed = centred * inverse
    return (normed * scale_row + shift_row, normed, inverse)


def norm_backward(upstream, normed, inverse, scale_row):
    scale_grad = jnp.sum(upstream * normed, axis=0)
    shift_grad = jnp.sum(upstream, axis=0)
    scaled = upstream * scale_row
    centred = scaled - jnp.mean(scaled, axis=1, keepdims=True)
    centred = centred - normed * jnp.mean(scaled * normed, axis=1, keepdims=True)
    return (centred * inverse, scale_grad, shift_grad)


def slot_segments(ends_ref, first, shape, axis):
    slots = lax.broadcasted_iota(jnp.int32, shape, axis) + first
    number = jnp.zeros(shape, jnp.int32)
    for j in range(ends_ref.shape[0]):
        number = number + (slots >= ends_ref[j]).astype(jnp.int32)
    return number

def key_tiles(ends_ref, first, last, slots):
    start, stop = jnp.int32(0), jnp.int32(slots)
    for j in reversed(range(ends_ref.shape[0])):
        end = ends_ref[j]
        start = jnp.maximum(start, jnp.where(end <= first, end, 0))
        stop = jnp.where(end > last, end, stop)
    return start // TILE, (stop + TILE - 1) // TILE

def head_masks(shape, axis):
    even = (lax.broadcasted_iota(jnp.int32, shape, axis) // HEAD_DIM) % 2 == 0
    return [m.astype(jnp.float32).astype(jnp.bfloat16) for m in (even, ~even)]

def columns(pair): return slice(pair * TILE, (pair + 1) * TILE)

def fill_stacks(projected_ref, column, tiles, stack=None, turned=None):
    across = head_masks((1, D), 1)
    down = head_masks((D, TILE), 0)
    def one(tile, _):
        rows = projected_ref[pl.ds(tile * TILE, TILE), column : column + D]
        if stack is not None:
            for side in range(2):
                stack[pl.ds(tile * WIDE + side * TILE, TILE), :] = rows * across[side]
        if turned is not None:
            flipped = rows.T
            for side in range(2):
                turned[tile, :, columns(side)] = flipped * down[side]
        return 0
    lax.fori_loop(0, tiles, one, 0)
    if stack is not None:
        stack[pl.ds(tiles * WIDE, WIDE), :] = jnp.zeros((WIDE, D), jnp.bfloat16)
    if turned is not None:
        turned[tiles] = jnp.zeros((D, WIDE), jnp.bfloat16)

def fill_segments(ends_ref, segments):
    def one(tile, _):
        segments[tile] = slot_segments(ends_ref, tile * TILE, (TILE, TILE), 0)
        return 0
    lax.fori_loop(0, segments.shape[0] - 1, one, 0)
    segments[segments.shape[0] - 1] = jnp.full((TILE, TILE), -1, jnp.int32)

def matching(segments, number, own):
    there = [segments[number], segments[number + 1]]
    return [jnp.concatenate([one, one], axis=1) == own for one in there]

def grouped(values): return values.reshape(TILE // 8, 8, WIDE)

def attention_kernel(ends_ref, projected_ref, context_ref, total_ref, keys, values, segments, queries, scores, highest, sums, out):
    tile = pl.program_id(0)
    slots = projected_ref.shape[0]
    tiles = slots // TILE
    @pl.when(tile == 0)
    def _():
        fill_stacks(projected_ref, D, tiles, stack=keys)
        fill_stacks(projected_ref, 2 * D, tiles, turned=values)
        fill_segments(ends_ref, segments)
    first = tile * WIDE
    low, high = key_tiles(ends_ref, first, first + WIDE - 1, slots)
    highest[...] = jnp.full_like(highest, -3e38)
    sums[...] = jnp.zeros_like(sums)
    out[...] = jnp.zeros_like(out)
    queries[...] = (projected_ref[pl.ds(first, WIDE), :D] * jnp.bfloat16(SCORE_SCALE)).T
    own = slot_segments(ends_ref, first, (1, WIDE), 1)
    windows = (high - low + 1) // 2
    def score(window, _):
        number = low + 2 * window
        same = matching(segments, number, own)
        for pair in range(PAIRS):
            both = product(keys[pl.ds(number * WIDE, 2 * WIDE), columns(pair)], queries[columns(pair), :])
            for place in range(4):
                half = jnp.where(same[place // 2], both[columns(place), :], MASKED)
                scores[pair, window, columns(place), :] = half
                head = 2 * pair + place % 2
                highest[head] = jnp.maximum(highest[head], jnp.max(grouped(half), axis=0))
        return 0
    lax.fori_loop(0, windows, score, 0)
    for head in range(HEADS):
        highest[head] = jnp.broadcast_to(jnp.max(highest[head], axis=0, keepdims=True), (8, WIDE))
    def weigh(window, _):
        number = low + 2 * window
        for pair in range(PAIRS):
            parts = []
            for place in range(4):
                head = 2 * pair + place % 2
                weights = jnp.exp(scores[pair, window, columns(place), :] - highest[head, :1, :])
                sums[head] += jnp.sum(grouped(weights), axis=0)
                parts.append(weights.astype(jnp.bfloat16))
            there = jnp.concatenate([values[number, columns(pair), :], values[number + 1, columns(pair), :]], axis=1)
            out[columns(pair), :] += product(there, jnp.concatenate(parts, axis=0))
        return 0
    lax.fori_loop(0, windows, weigh, 0)
    for head in range(HEADS):
        total = jnp.sum(sums[head], axis=0, keepdims=True)
        part = slice(head * HEAD_DIM, (head + 1) * HEAD_DIM)
        out[part, :] = out[part, :] * (1.0 / total)
        total_ref[head : head + 1, :] = highest[head, :1, :] + jnp.log(total)
    total_ref[HEADS:, :] = jnp.zeros((ROWS - HEADS, WIDE), jnp.float32)
    context_ref[...] = out[...].T.astype(jnp.bfloat16)

def attention(ends, projected):
    slots = projected.shape[0]; tiles = slots // TILE
    return pl.pallas_call(
        attention_kernel,
        grid_spec=pltpu.PrefetchScalarGridSpec(
            num_scalar_prefetch=1, grid=(slots // WIDE,),
            in_specs=[pl.BlockSpec((slots, 3 * D), lambda i, e: (0, 0), pipeline_mode=pl.Buffered(1))],
            out_specs=[pl.BlockSpec((WIDE, D), lambda i, e: (i, 0)), pl.BlockSpec((ROWS, WIDE), lambda i, e: (0, i))],
            scratch_shapes=[
                pltpu.VMEM(((tiles + 1) * WIDE, D), jnp.bfloat16), pltpu.VMEM((tiles + 1, D, WIDE), jnp.bfloat16),
                pltpu.VMEM((tiles + 1, TILE, TILE), jnp.int32),
                pltpu.VMEM((D, WIDE), jnp.bfloat16),
                pltpu.VMEM((PAIRS, (tiles + 1) // 2, 2 * WIDE, WIDE), jnp.float32),
                pltpu.VMEM((HEADS, 8, WIDE), jnp.float32), pltpu.VMEM((HEADS, 8, WIDE), jnp.float32),
                pltpu.VMEM((D, WIDE), jnp.float32)]),
        out_shape=[jax.ShapeDtypeStruct((slots, D), jnp.bfloat16), jax.ShapeDtypeStruct((ROWS, slots), jnp.float32)],
        compiler_params=pltpu.CompilerParams(vmem_limit_bytes=48 << 20),
        cost_estimate=pl.CostEstimate(flops=8 * 10**9, bytes_accessed=8 * 10**6, transcendentals=6 * 10**6),
        name="attention",
    )(ends, projected)

def attention_grad_kernel(ends_ref, projected_ref, outer_ref, context_ref, total_ref, out_ref, bias_ref, keys, values, turned, segments, queries, outers, query_sides, outer_sides, key_sum, value_sum, query_sum, deltas):
    tile = pl.program_id(0)
    slots = projected_ref.shape[0]; tiles = slots // TILE
    live = (ends_ref[ends_ref.shape[0] - 1] + TILE - 1) // TILE
    first = tile * WIDE
    rows = pl.ds(first, WIDE)
    @pl.when(tile == 0)
    def _():
        fill_stacks(projected_ref, D, tiles, stack=keys, turned=turned)
        fill_stacks(projected_ref, 2 * D, tiles, stack=values)
        fill_segments(ends_ref, segments)
        key_sum[...] = jnp.zeros_like(key_sum)
        value_sum[...] = jnp.zeros_like(value_sum)
        bias_ref[...] = jnp.zeros_like(bias_ref)
    @pl.when(first >= live * TILE)
    def _():
        out_ref[rows, :D] = jnp.zeros((WIDE, D), jnp.bfloat16)
    @pl.when(first < live * TILE)
    def _():
        low, high = key_tiles(ends_ref, first, first + WIDE - 1, slots)
        high = jnp.minimum(high, live)
        query_sum[...] = jnp.zeros_like(query_sum)
        across = head_masks((1, D), 1)
        scaled = projected_ref[rows, :D] * jnp.bfloat16(SCORE_SCALE)
        outer = outer_ref[...]
        queries[...] = scaled.T
        outers[...] = outer.T
        for side in range(2):
            query_sides[side] = scaled * across[side]
            outer_sides[side] = outer * across[side]
        both = (outer.astype(jnp.float32) * context_ref[...].astype(jnp.float32)).T
        for head in range(HEADS):
            deltas[head : head + 1, :] = jnp.sum(both[head * HEAD_DIM : (head + 1) * HEAD_DIM, :], axis=0, keepdims=True)
        own = slot_segments(ends_ref, first, (1, WIDE), 1)
        def visit(window, _):
            number = low + 2 * window
            same = matching(segments, number, own)
            there = pl.ds(number * WIDE, 2 * WIDE)
            where = pl.ds(number * TILE, WIDE)
            for pair in range(PAIRS):
                both = product(keys[there, columns(pair)], queries[columns(pair), :])
                grads = product(values[there, columns(pair)], outers[columns(pair), :])
                weights_parts, parts = [], []
                for place in range(4):
                    head = 2 * pair + place % 2
                    part = columns(place)
                    weights = jnp.where(same[place // 2], jnp.exp(both[part, :] - total_ref[head : head + 1, :]), 0.0)
                    parts.append((weights * (grads[part, :] - deltas[head : head + 1, :])).astype(jnp.bfloat16))
                    weights_parts.append(weights.astype(jnp.bfloat16))
                def folded(blocks, sides):
                    total = 0
                    for side in range(2):
                        total = total + product(jnp.concatenate(blocks[side::2], axis=0), sides[side, :, columns(pair)])
                    return total
                key_sum[where, columns(pair)] += folded(parts, query_sides)
                value_sum[where, columns(pair)] += folded(weights_parts, outer_sides)
                across = jnp.concatenate([turned[number, columns(pair), :], turned[number + 1, columns(pair), :]], axis=1)
                query_sum[columns(pair), :] += product(across, jnp.concatenate(parts, axis=0))
            return 0
        lax.fori_loop(0, (high - low + 1) // 2, visit, 0)
        done = (query_sum[...] * SCORE_SCALE).T.astype(jnp.bfloat16)
        out_ref[rows, :D] = done
        bias_ref[:, :D] += jnp.sum(done.astype(jnp.float32), axis=0, keepdims=True)
    @pl.when(tile == pl.num_programs(0) - 1)
    def _():
        def close(number, _):
            there = pl.ds(number * TILE, TILE)
            out_ref[there, D : 2 * D] = key_sum[there, :].astype(jnp.bfloat16)
            done = value_sum[there, :].astype(jnp.bfloat16)
            out_ref[there, 2 * D :] = done
            bias_ref[:, D:] += jnp.sum(done.astype(jnp.float32), axis=0, keepdims=True)
            return 0
        lax.fori_loop(0, tiles, close, 0)

def attention_grad(ends, projected, outer, context, total):
    slots = projected.shape[0]; tiles = slots // TILE
    whole = lambda i, e: (0, 0)
    return pl.pallas_call(
        attention_grad_kernel,
        grid_spec=pltpu.PrefetchScalarGridSpec(
            num_scalar_prefetch=1, grid=(slots // WIDE,),
            in_specs=[pl.BlockSpec((slots, 3 * D), whole, pipeline_mode=pl.Buffered(1)),
                pl.BlockSpec((WIDE, D), lambda i, e: (i, 0)), pl.BlockSpec((WIDE, D), lambda i, e: (i, 0)), pl.BlockSpec((ROWS, WIDE), lambda i, e: (0, i))],
            out_specs=[pl.BlockSpec((slots, 3 * D), whole), pl.BlockSpec((1, 2 * D), whole)],
            scratch_shapes=[
                pltpu.VMEM(((tiles + 1) * WIDE, D), jnp.bfloat16), pltpu.VMEM(((tiles + 1) * WIDE, D), jnp.bfloat16), pltpu.VMEM((tiles + 1, D, WIDE), jnp.bfloat16),
                pltpu.VMEM((tiles + 1, TILE, TILE), jnp.int32),
                pltpu.VMEM((D, WIDE), jnp.bfloat16), pltpu.VMEM((D, WIDE), jnp.bfloat16),
                pltpu.VMEM((2, WIDE, D), jnp.bfloat16), pltpu.VMEM((2, WIDE, D), jnp.bfloat16),
                pltpu.VMEM((slots + TILE, D), jnp.float32), pltpu.VMEM((slots + TILE, D), jnp.float32), pltpu.VMEM((D, WIDE), jnp.float32),
                pltpu.VMEM((ROWS, WIDE), jnp.float32)]),
        out_shape=[jax.ShapeDtypeStruct((slots, 3 * D), jnp.bfloat16), jax.ShapeDtypeStruct((1, 2 * D), jnp.float32)],
        compiler_params=pltpu.CompilerParams(vmem_limit_bytes=48 << 20),
        cost_estimate=pl.CostEstimate(flops=20 * 10**9, bytes_accessed=14 * 10**6, transcendentals=6 * 10**6),
        name="attention_grad",
    )(ends, projected, outer, context, total)


def per_device(
    tokens,
    cotangent,
    question_lengths,
    passage_lengths,
    attend_weight,
    query_bias,
    value_bias,
    output_weight,
    output_bias,
    first_gain,
    first_shift,
    expand_weight,
    expand_bias,
    reduce_weight,
    reduce_bias,
    second_gain,
    second_shift,
):
    inputs = tokens[0]
    attend_matrix = attend_weight[0]
    output_matrix = output_weight[0]
    expand_matrix = expand_weight[0]
    reduce_matrix = reduce_weight[0]
    first_scale = first_gain[0].astype(jnp.float32)
    second_scale = second_gain[0].astype(jnp.float32)
    slot_count = inputs.shape[0]
    is_passage = lax.axis_index("enc") == 1
    lengths_here = jnp.where(is_passage, passage_lengths[0], question_lengths[0])
    order = jnp.arange(lengths_here.shape[0], dtype=jnp.int32)
    ends_here = jnp.sum(
        jnp.where(order[None, :] <= order[:, None], lengths_here[None, :], 0), axis=1
    )
    starts_here = ends_here - lengths_here
    slot_index = jnp.arange(slot_count, dtype=jnp.int32)
    live = (slot_index < ends_here[-1]).astype(jnp.float32)
    bias_full = jnp.concatenate(
        [
            query_bias[0].astype(jnp.float32),
            jnp.zeros((D,), jnp.float32),
            value_bias[0].astype(jnp.float32),
        ]
    )
    projected = (product(inputs, attend_matrix) + bias_full).astype(jnp.bfloat16)
    context, total = attention(ends_here, projected)
    branch = product(context, output_matrix) + output_bias[0].astype(jnp.float32)
    hidden, normed_one, inverse_one = norm_forward(
        inputs.astype(jnp.float32) + branch, first_scale, first_shift[0].astype(jnp.float32)
    )
    hidden_low = hidden.astype(jnp.bfloat16)
    inner = product(hidden_low, expand_matrix) + expand_bias[0].astype(jnp.float32)
    normal_cdf = 0.5 * (1.0 + lax.erf(inner * INV_ROOT_TWO))
    active = (inner * normal_cdf).astype(jnp.bfloat16)
    second = product(active, reduce_matrix) + reduce_bias[0].astype(jnp.float32)
    result, normed_two, inverse_two = norm_forward(
        hidden + second, second_scale, second_shift[0].astype(jnp.float32)
    )
    chosen = (starts_here[:, None] == slot_index[None, :]).astype(jnp.bfloat16)
    summary = product(chosen, result.astype(jnp.bfloat16)).astype(jnp.bfloat16)
    mine, other, place = gathered_summaries(summary)
    seq_count = summary.shape[0]
    mine, other = mine.reshape(-1, D), other.reshape(-1, D)
    questions = jnp.where(is_passage, other, mine)
    passages = jnp.where(is_passage, mine, other)
    summary_scale = 2.0 / math.sqrt(D)
    total_seqs = questions.shape[0]
    logits = contract_cols(questions, passages) * summary_scale
    highest_logit = jnp.max(logits, axis=1, keepdims=True)
    logit_total = highest_logit + jnp.log(
        jnp.sum(jnp.exp(logits - highest_logit), axis=1, keepdims=True)
    )
    matches = jnp.eye(total_seqs, dtype=jnp.float32)
    score_grad = (LOSS_WEIGHT * (jnp.exp(logits - logit_total) - matches)).astype(jnp.bfloat16)
    own_rows = lax.dynamic_slice_in_dim(score_grad, place * seq_count, seq_count, 0)
    own_columns = lax.dynamic_slice_in_dim(score_grad, place * seq_count, seq_count, 1)
    question_term = (product(own_rows, passages) * summary_scale).astype(jnp.bfloat16)
    passage_term = contract_rows(own_columns, questions) * summary_scale
    summary_grad = jnp.where(is_passage, passage_term, question_term.astype(jnp.float32))
    upstream = cotangent[0].astype(jnp.float32) * live[:, None]
    upstream = upstream + lax.dot_general(
        chosen.astype(jnp.float32),
        summary_grad,
        (((0,), (0,)), ((), ())),
        precision=lax.Precision.HIGHEST,
        preferred_element_type=jnp.float32,
    )
    residual_two_grad, second_gain_grad, second_shift_grad = norm_backward(
        upstream, normed_two, inverse_two, second_scale
    )
    count = lax.axis_size("batch")

    def scatter(gradient):
        return Scatter(
            gradient.astype(jnp.bfloat16).reshape(count, gradient.shape[0] // count, -1)
        )

    reduce_input = residual_two_grad.astype(jnp.bfloat16)
    reduce_bias_grad = jnp.sum(reduce_input.astype(jnp.float32), axis=0)
    reduce_share = scatter(contract_rows(active, reduce_input))
    reduce_input = reduce_share.begin(ahead=reduce_input)
    active_grad = contract_cols(reduce_input, reduce_matrix)
    slope = normal_cdf + inner * jnp.exp(-0.5 * inner * inner) * INV_ROOT_TAU
    inner_grad = (active_grad * slope).astype(jnp.bfloat16)
    inner_grad = reduce_share.begin(since=inner_grad, ahead=inner_grad)
    expand_share = scatter(contract_rows(hidden_low, inner_grad))
    inner_grad = expand_share.begin(ahead=inner_grad)
    expand_bias_grad = jnp.sum(inner_grad.astype(jnp.float32), axis=0)
    hidden_grad = residual_two_grad + contract_cols(inner_grad, expand_matrix)
    residual_one_grad, first_gain_grad, first_shift_grad = norm_backward(
        hidden_grad, normed_one, inverse_one, first_scale
    )
    branch_grad = residual_one_grad.astype(jnp.bfloat16)
    output_bias_grad = jnp.sum(branch_grad.astype(jnp.float32), axis=0)
    output_share = scatter(contract_rows(context, branch_grad))
    branch_grad = output_share.begin(ahead=branch_grad)
    context_grad = contract_cols(branch_grad, output_matrix).astype(jnp.bfloat16)
    context_grad = expand_share.begin(since=context_grad, ahead=context_grad)
    context_grad = output_share.begin(since=context_grad, ahead=context_grad)
    projected_grad, bias_grads = attention_grad(
        ends_here, projected, context_grad, context, total
    )
    projected_grad = reduce_share.begin(since=projected_grad, ahead=projected_grad)
    projected_grad = output_share.begin(since=projected_grad, ahead=projected_grad)
    attend_share = scatter(contract_rows(inputs, projected_grad))
    projected_grad = attend_share.begin(ahead=projected_grad)
    projected_grad = expand_share.begin(since=attend_share.whole, ahead=projected_grad)
    tokens_grad = (residual_one_grad + contract_cols(projected_grad, attend_matrix)).astype(
        jnp.bfloat16
    )
    attend_share.begin(since=tokens_grad)
    reduce_share.begin(since=tokens_grad)
    output_share.begin(since=tokens_grad)
    vectors = (
        bias_grads[0, :D],
        bias_grads[0, D:],
        output_bias_grad,
        first_gain_grad,
        first_shift_grad,
        reduce_bias_grad,
        second_gain_grad,
        second_shift_grad,
        expand_bias_grad,
    )
    packed = jnp.concatenate([vector.reshape(count, -1) for vector in vectors], axis=1)
    small = Scatter(packed).result()
    width = D // count
    small_shares = [small[None, i * width : (i + 1) * width] for i in range(8)]
    small_shares.append(small[None, 8 * width :])
    return (
        result.astype(jnp.bfloat16)[None],
        tokens_grad[None],
        attend_share.result()[None],
        small_shares[0],
        small_shares[1],
        output_share.result()[None],
        small_shares[2],
        small_shares[3],
        small_shares[4],
        expand_share.result()[None],
        small_shares[8],
        reduce_share.result()[None],
        small_shares[5],
        small_shares[6],
        small_shares[7],
    )


def solution(mesh):
    in_specs = (
        P("enc", "batch", None),
        P("enc", "batch", None),
        P("batch", None),
        P("batch", None),
        P("enc", None, None),
        P("enc", None),
        P("enc", None),
        P("enc", None, None),
        P("enc", None),
        P("enc", None),
        P("enc", None),
        P("enc", None, None),
        P("enc", None),
        P("enc", None, None),
        P("enc", None),
        P("enc", None),
        P("enc", None),
    )
    out_specs = (
        P("enc", "batch", None),
        P("enc", "batch", None),
        P("enc", "batch", None),
        P("enc", "batch"),
        P("enc", "batch"),
        P("enc", "batch", None),
        P("enc", "batch"),
        P("enc", "batch"),
        P("enc", "batch"),
        P("enc", "batch", None),
        P("enc", "batch"),
        P("enc", "batch", None),
        P("enc", "batch"),
        P("enc", "batch"),
        P("enc", "batch"),
    )
    return jax.shard_map(
        per_device, mesh=mesh, in_specs=in_specs, out_specs=out_specs, check_vma=False
    )
```

```python
import functools
import math

import jax
import jax.numpy as jnp
from jax import lax
from jax.experimental import pallas as pl
from jax.experimental.pallas import tpu as pltpu
from jax.sharding import PartitionSpec as P

D = 768
HEADS = 12
HEAD_DIM = 64
TILE = 128
WIDE = 2 * TILE
PAIRS = HEADS // 2
ROWS = 16
FF_BLOCK = 512


def cost(weight):
    return pl.CostEstimate(flops=weight * 2 * 10**9, bytes_accessed=10**3, transcendentals=0)


COST = cost(1)


EPSILON = 1e-12
SCORE_SCALE = 0.125
MASKED = -1000000000.0
LOSS_WEIGHT = 16.0
INV_ROOT_TWO = 0.7071067811865476
INV_ROOT_TAU = 0.3989422804014327


def exchanged(value, axes, distance):
    count = math.prod(lax.axis_size(axis) for axis in axes)
    return lax.ppermute(value, axes, [(source, source ^ distance) for source in range(count)])


def gathered_summaries(summary):
    count = lax.axis_size("batch")
    if count != 16:
        everything = lax.all_gather(summary, ("enc", "batch"), axis=0, tiled=False)
        own = lax.axis_index("enc")
        everything = everything.reshape((2, count) + summary.shape)
        mine = lax.dynamic_index_in_dim(everything, own, 0, keepdims=False)
        other = lax.dynamic_index_in_dim(everything, 1 - own, 0, keepdims=False)
        return mine, other, lax.axis_index("batch")
    both = ("enc", "batch")
    pair = jnp.stack([summary, exchanged(summary, both, 1)])
    mine = [pair, exchanged(pair, both, 2)]
    other = [exchanged(pair, both, 16), exchanged(pair, both, 18)]
    plane = jnp.concatenate(mine + other)
    parts = [plane] + [exchanged(plane, both, distance) for distance in (4, 8, 12)]
    size = plane.shape[0] // 2
    return (
        jnp.concatenate([part[:size] for part in parts]),
        jnp.concatenate([part[size:] for part in parts]),
        0,
    )


def product(left_side, right_side):
    return jnp.dot(left_side, right_side, preferred_element_type=jnp.float32)


def contract_rows(left_side, right_side):
    return lax.dot_general(
        left_side, right_side, (((0,), (0,)), ((), ())), preferred_element_type=jnp.float32
    )


def contract_cols(left_side, right_side):
    return lax.dot_general(
        left_side, right_side, (((1,), (1,)), ((), ())), preferred_element_type=jnp.float32
    )


def norm_forward(values, scale_row, shift_row):
    centred = values - jnp.mean(values, axis=1, keepdims=True)
    inverse = lax.rsqrt(jnp.mean(centred * centred, axis=1, keepdims=True) + EPSILON)
    normed = centred * inverse
    return (normed * scale_row + shift_row, normed, inverse)


def norm_backward(upstream, normed, inverse, scale_row):
    scale_grad = jnp.sum(upstream * normed, axis=0)
    shift_grad = jnp.sum(upstream, axis=0)
    scaled = upstream * scale_row
    centred = scaled - jnp.mean(scaled, axis=1, keepdims=True)
    centred = centred - normed * jnp.mean(scaled * normed, axis=1, keepdims=True)
    return (centred * inverse, scale_grad, shift_grad)


def params(megabytes):
    return pltpu.CompilerParams(vmem_limit_bytes=max(megabytes, 64) << 20)


def constant(shape):
    return pl.BlockSpec(shape, lambda *_: (0,) * len(shape), pipeline_mode=pl.Buffered(1))


def slot_segments(ends_ref, first, shape, axis):
    slots = lax.broadcasted_iota(jnp.int32, shape, axis) + first
    number = jnp.zeros(shape, jnp.int32)
    for j in range(ends_ref.shape[0]):
        number = number + (slots >= ends_ref[j]).astype(jnp.int32)
    return number

def key_tiles(ends_ref, first, last, slots):
    start, stop = jnp.int32(0), jnp.int32(slots)
    for j in reversed(range(ends_ref.shape[0])):
        end = ends_ref[j]
        start = jnp.maximum(start, jnp.where(end <= first, end, 0))
        stop = jnp.where(end > last, end, stop)
    return start // TILE, (stop + TILE - 1) // TILE

def head_masks(shape, axis):
    even = (lax.broadcasted_iota(jnp.int32, shape, axis) // HEAD_DIM) % 2 == 0
    return [m.astype(jnp.float32).astype(jnp.bfloat16) for m in (even, ~even)]

def columns(pair): return slice(pair * TILE, (pair + 1) * TILE)

def fill_stacks(source_ref, tiles, stack=None, turned=None, column=0):
    width = (stack if stack is not None else turned).shape[1]
    across = head_masks((1, width), 1)
    down = head_masks((width, TILE), 0)
    def one(tile, _):
        rows = source_ref[pl.ds(tile * TILE, TILE), column : column + width]
        if stack is not None:
            for side in range(2):
                stack[pl.ds(tile * WIDE + side * TILE, TILE), :] = rows * across[side]
        if turned is not None:
            flipped = rows.T
            for side in range(2):
                turned[tile, :, columns(side)] = flipped * down[side]
        return 0
    lax.fori_loop(0, tiles, one, 0)
    if stack is not None:
        stack[pl.ds(tiles * WIDE, WIDE), :] = jnp.zeros((WIDE, width), jnp.bfloat16)
    if turned is not None:
        turned[tiles] = jnp.zeros((width, WIDE), jnp.bfloat16)

def fill_segments(ends_ref, segments):
    def one(tile, _):
        segments[tile] = slot_segments(ends_ref, tile * TILE, (TILE, TILE), 0)
        return 0
    lax.fori_loop(0, segments.shape[0] - 1, one, 0)
    segments[segments.shape[0] - 1] = jnp.full((TILE, TILE), -1, jnp.int32)

def matching(segments, number, own):
    there = [segments[number], segments[number + 1]]
    return [jnp.concatenate([one, one], axis=1) == own for one in there]

def grouped(values): return values.reshape(TILE // 8, 8, WIDE)

def attention_kernel(ends_ref, tokens_ref, attend_ref, query_bias_ref, value_bias_ref, output_ref, output_bias_ref, gain_ref, shift_ref, projected_ref, context_ref, total_ref, hidden_ref, normed_ref, inverse_ref, keys, values, segments, queries, scores, highest, sums, out):
    tile = pl.program_id(0)
    slots = projected_ref.shape[0]
    tiles = slots // TILE
    @pl.when(tile == 0)
    def _():
        for third, bias_ref in enumerate((query_bias_ref, None, value_bias_ref)):
            part = slice(third * D, (third + 1) * D)
            for block in range(slots // WIDE):
                rows = slice(block * WIDE, (block + 1) * WIDE)
                made = product(tokens_ref[rows, :], attend_ref[:, part])
                if bias_ref is not None:
                    made = made + bias_ref[...].astype(jnp.float32)
                projected_ref[rows, part] = made.astype(jnp.bfloat16)
        fill_stacks(projected_ref, tiles, stack=keys, column=D)
        fill_stacks(projected_ref, tiles, turned=values, column=2 * D)
        fill_segments(ends_ref, segments)
    first = tile * WIDE
    low, high = key_tiles(ends_ref, first, first + WIDE - 1, slots)
    highest[...] = jnp.full_like(highest, -3e38)
    sums[...] = jnp.zeros_like(sums)
    out[...] = jnp.zeros_like(out)
    queries[...] = (projected_ref[pl.ds(first, WIDE), :D] * jnp.bfloat16(SCORE_SCALE)).T
    own = slot_segments(ends_ref, first, (1, WIDE), 1)
    windows = (high - low + 1) // 2
    def score(window, _):
        number = low + 2 * window
        same = matching(segments, number, own)
        for pair in range(PAIRS):
            both = product(keys[pl.ds(number * WIDE, 2 * WIDE), columns(pair)], queries[columns(pair), :])
            for place in range(4):
                half = jnp.where(same[place // 2], both[columns(place), :], MASKED)
                scores[pair, window, columns(place), :] = half
                head = 2 * pair + place % 2
                highest[head] = jnp.maximum(highest[head], jnp.max(grouped(half), axis=0))
        return 0
    lax.fori_loop(0, windows, score, 0)
    for head in range(HEADS):
        highest[head] = jnp.broadcast_to(jnp.max(highest[head], axis=0, keepdims=True), (8, WIDE))
    def weigh(window, _):
        number = low + 2 * window
        for pair in range(PAIRS):
            parts = []
            for place in range(4):
                head = 2 * pair + place % 2
                weights = jnp.exp(scores[pair, window, columns(place), :] - highest[head, :1, :])
                sums[head] += jnp.sum(grouped(weights), axis=0)
                parts.append(weights.astype(jnp.bfloat16))
            there = jnp.concatenate([values[number, columns(pair), :], values[number + 1, columns(pair), :]], axis=1)
            out[columns(pair), :] += product(there, jnp.concatenate(parts, axis=0))
        return 0
    lax.fori_loop(0, windows, weigh, 0)
    for head in range(HEADS):
        total = jnp.sum(sums[head], axis=0, keepdims=True)
        part = slice(head * HEAD_DIM, (head + 1) * HEAD_DIM)
        out[part, :] = out[part, :] * (1.0 / total)
        total_ref[head : head + 1, :] = highest[head, :1, :] + jnp.log(total)
    total_ref[HEADS:, :] = jnp.zeros((ROWS - HEADS, WIDE), jnp.float32)
    context = out[...].T.astype(jnp.bfloat16)
    context_ref[...] = context
    branch = product(context, output_ref[...]) + output_bias_ref[...].astype(jnp.float32)
    hidden, normed, inverse = norm_forward(
        tokens_ref[pl.ds(first, WIDE), :].astype(jnp.float32) + branch,
        gain_ref[...].astype(jnp.float32),
        shift_ref[...].astype(jnp.float32),
    )
    hidden_ref[...] = hidden.astype(jnp.bfloat16)
    normed_ref[...] = normed
    inverse_ref[...] = inverse

def attention(ends, tokens, attend, query_bias, value_bias, output, output_bias, gain, shift):
    slots = tokens.shape[0]
    tiles = slots // TILE
    tile = pl.BlockSpec((WIDE, D), lambda i, e: (i, 0))
    return pl.pallas_call(
        attention_kernel,
        grid_spec=pltpu.PrefetchScalarGridSpec(
            num_scalar_prefetch=1,
            grid=(slots // WIDE,),
            in_specs=[
                constant(x.shape) for x in (tokens, attend, query_bias, value_bias, output)
            ]
            + [constant((1, D))] * 3,
            out_specs=[
                pl.BlockSpec((slots, 3 * D), lambda i, e: (0, 0)),
                tile,
                pl.BlockSpec((ROWS, WIDE), lambda i, e: (0, i)),
                tile,
                tile,
                pl.BlockSpec((WIDE, 1), lambda i, e: (i, 0)),
            ],
            scratch_shapes=[
                pltpu.VMEM(((tiles + 1) * WIDE, D), jnp.bfloat16),
                pltpu.VMEM((tiles + 1, D, WIDE), jnp.bfloat16),
                pltpu.VMEM((tiles + 1, TILE, TILE), jnp.int32),
                pltpu.VMEM((D, WIDE), jnp.bfloat16),
                pltpu.VMEM((PAIRS, (tiles + 1) // 2, 2 * WIDE, WIDE), jnp.float32),
                pltpu.VMEM((HEADS, 8, WIDE), jnp.float32),
                pltpu.VMEM((HEADS, 8, WIDE), jnp.float32),
                pltpu.VMEM((D, WIDE), jnp.float32),
            ],
        ),
        out_shape=[
            jax.ShapeDtypeStruct((slots, 3 * D), jnp.bfloat16),
            jax.ShapeDtypeStruct((slots, D), jnp.bfloat16),
            jax.ShapeDtypeStruct((ROWS, slots), jnp.float32),
            jax.ShapeDtypeStruct((slots, D), jnp.bfloat16),
            jax.ShapeDtypeStruct((slots, D), jnp.float32),
            jax.ShapeDtypeStruct((slots, 1), jnp.float32),
        ],
        compiler_params=params(42),
        cost_estimate=COST,
        name="attention",
    )(ends, tokens, attend, query_bias, value_bias, output, output_bias, gain, shift)


def attention_grad_kernel(ends_ref, queries_ref, keys_ref, values_ref, outer_ref, context_ref, total_ref, out_ref, bias_ref, keys, values, turned, segments, queries, outers, query_sides, outer_sides, key_sum, value_sum, query_sum, deltas):
    tile = pl.program_id(0)
    slots = keys_ref.shape[0]
    tiles = slots // TILE
    live = (ends_ref[ends_ref.shape[0] - 1] + TILE - 1) // TILE
    first = tile * WIDE
    rows = pl.ds(first, WIDE)
    @pl.when(tile == 0)
    def _():
        fill_stacks(keys_ref, tiles, stack=keys, turned=turned)
        fill_stacks(values_ref, tiles, stack=values)
        fill_segments(ends_ref, segments)
        key_sum[...] = jnp.zeros_like(key_sum)
        value_sum[...] = jnp.zeros_like(value_sum)
        bias_ref[...] = jnp.zeros_like(bias_ref)
    @pl.when(first >= live * TILE)
    def _():
        out_ref[rows, :D] = jnp.zeros((WIDE, D), jnp.bfloat16)
    @pl.when(first < live * TILE)
    def _():
        low, high = key_tiles(ends_ref, first, first + WIDE - 1, slots)
        high = jnp.minimum(high, live)
        query_sum[...] = jnp.zeros_like(query_sum)
        across = head_masks((1, D), 1)
        scaled = queries_ref[...] * jnp.bfloat16(SCORE_SCALE)
        outer = outer_ref[...]
        queries[...] = scaled.T
        outers[...] = outer.T
        for side in range(2):
            query_sides[side] = scaled * across[side]
            outer_sides[side] = outer * across[side]
        both = (outer.astype(jnp.float32) * context_ref[...].astype(jnp.float32)).T
        for head in range(HEADS):
            deltas[head : head + 1, :] = jnp.sum(both[head * HEAD_DIM : (head + 1) * HEAD_DIM, :], axis=0, keepdims=True)
        own = slot_segments(ends_ref, first, (1, WIDE), 1)
        def visit(window, _):
            number = low + 2 * window
            same = matching(segments, number, own)
            there = pl.ds(number * WIDE, 2 * WIDE)
            where = pl.ds(number * TILE, WIDE)
            for pair in range(PAIRS):
                both = product(keys[there, columns(pair)], queries[columns(pair), :])
                grads = product(values[there, columns(pair)], outers[columns(pair), :])
                weights_parts, parts = [], []
                for place in range(4):
                    head = 2 * pair + place % 2
                    part = columns(place)
                    weights = jnp.where(same[place // 2], jnp.exp(both[part, :] - total_ref[head : head + 1, :]), 0.0)
                    parts.append((weights * (grads[part, :] - deltas[head : head + 1, :])).astype(jnp.bfloat16))
                    weights_parts.append(weights.astype(jnp.bfloat16))
                def folded(blocks, sides):
                    total = 0
                    for side in range(2):
                        total = total + product(jnp.concatenate(blocks[side::2], axis=0), sides[side, :, columns(pair)])
                    return total
                key_sum[where, columns(pair)] += folded(parts, query_sides)
                value_sum[where, columns(pair)] += folded(weights_parts, outer_sides)
                across = jnp.concatenate([turned[number, columns(pair), :], turned[number + 1, columns(pair), :]], axis=1)
                query_sum[columns(pair), :] += product(across, jnp.concatenate(parts, axis=0))
            return 0
        lax.fori_loop(0, (high - low + 1) // 2, visit, 0)
        done = (query_sum[...] * SCORE_SCALE).T.astype(jnp.bfloat16)
        out_ref[rows, :D] = done
        bias_ref[:, :D] += jnp.sum(done.astype(jnp.float32), axis=0, keepdims=True)
    @pl.when(tile == pl.num_programs(0) - 1)
    def _():
        def close(number, _):
            there = pl.ds(number * TILE, TILE)
            out_ref[there, D : 2 * D] = key_sum[there, :].astype(jnp.bfloat16)
            done = value_sum[there, :].astype(jnp.bfloat16)
            out_ref[there, 2 * D :] = done
            bias_ref[:, D:] += jnp.sum(done.astype(jnp.float32), axis=0, keepdims=True)
            return 0
        lax.fori_loop(0, tiles, close, 0)

def attention_grad(ends, projected, outer, context, total):
    slots = projected.shape[0]; tiles = slots // TILE
    whole = lambda i, e: (0, 0)
    return pl.pallas_call(
        attention_grad_kernel,
        grid_spec=pltpu.PrefetchScalarGridSpec(
            num_scalar_prefetch=1, grid=(slots // WIDE,),
            in_specs=[
                pl.BlockSpec((WIDE, D), lambda i, e: (i, 0)),
                pl.BlockSpec((slots, D), lambda i, e: (0, 1), pipeline_mode=pl.Buffered(1)),
                pl.BlockSpec((slots, D), lambda i, e: (0, 2), pipeline_mode=pl.Buffered(1)),
                pl.BlockSpec((WIDE, D), lambda i, e: (i, 0)),
                pl.BlockSpec((WIDE, D), lambda i, e: (i, 0)), pl.BlockSpec((ROWS, WIDE), lambda i, e: (0, i))],
            out_specs=[pl.BlockSpec((slots, 3 * D), whole), pl.BlockSpec((1, 2 * D), whole)],
            scratch_shapes=[
                pltpu.VMEM(((tiles + 1) * WIDE, D), jnp.bfloat16), pltpu.VMEM(((tiles + 1) * WIDE, D), jnp.bfloat16), pltpu.VMEM((tiles + 1, D, WIDE), jnp.bfloat16),
                pltpu.VMEM((tiles + 1, TILE, TILE), jnp.int32),
                pltpu.VMEM((D, WIDE), jnp.bfloat16), pltpu.VMEM((D, WIDE), jnp.bfloat16),
                pltpu.VMEM((2, WIDE, D), jnp.bfloat16), pltpu.VMEM((2, WIDE, D), jnp.bfloat16),
                pltpu.VMEM((slots + TILE, D), jnp.float32), pltpu.VMEM((slots + TILE, D), jnp.float32), pltpu.VMEM((D, WIDE), jnp.float32),
                pltpu.VMEM((ROWS, WIDE), jnp.float32)]),
        out_shape=[jax.ShapeDtypeStruct((slots, 3 * D), jnp.bfloat16), jax.ShapeDtypeStruct((1, 2 * D), jnp.float32)],
        compiler_params=params(32),
        cost_estimate=COST,
        name="attention_grad",
    )(ends, projected, projected, projected, outer, context, total)


def feed_kernel(
    ends_ref, lengths_ref, hidden_ref, normed_one_ref, first_gain_ref, first_shift_ref, expand_ref, expand_bias_ref,
    reduce_ref, reduce_bias_ref, gain_ref, shift_ref, active_ref, slope_ref, out_ref, normed_ref, inverse_ref, summary_ref, total,
):
    step = pl.program_id(0)
    slots = hidden_ref.shape[0]

    @pl.when(step == 0)
    def _():
        total[...] = jnp.zeros_like(total)

    for block in range(slots // WIDE):
        rows = slice(block * WIDE, (block + 1) * WIDE)
        inner = product(hidden_ref[rows, :], expand_ref[...]) + expand_bias_ref[...].astype(
            jnp.float32
        )
        normal_cdf = 0.5 * (1.0 + lax.erf(inner * INV_ROOT_TWO))
        slope = normal_cdf + inner * jnp.exp(-0.5 * inner * inner) * INV_ROOT_TAU
        active = (inner * normal_cdf).astype(jnp.bfloat16)
        active_ref[rows, :] = active
        slope_ref[rows, :] = slope.astype(jnp.bfloat16)
        total[rows, :] += product(active, reduce_ref[...])

    @pl.when(step == pl.num_programs(0) - 1)
    def _():
        first_gain = first_gain_ref[...].astype(jnp.float32)
        first_shift = first_shift_ref[...].astype(jnp.float32)

        def close(block, _):
            rows = pl.ds(block * TILE, TILE)
            hidden = normed_one_ref[rows, :] * first_gain + first_shift
            second = total[rows, :] + reduce_bias_ref[...].astype(jnp.float32)
            result, normed, inverse = norm_forward(
                hidden + second,
                gain_ref[...].astype(jnp.float32),
                shift_ref[...].astype(jnp.float32),
            )
            total[rows, :] = result
            out_ref[rows, :] = result.astype(jnp.bfloat16)
            normed_ref[rows, :] = normed
            inverse_ref[rows, :] = inverse
            return 0

        lax.fori_loop(0, slots // TILE, close, 0)
        for number in range(ends_ref.shape[0]):
            begin = ends_ref[number] - lengths_ref[number]
            summary_ref[number : number + 1, :] = total[pl.ds(begin, 1), :].astype(jnp.bfloat16)


def feed(ends, lengths, hidden, normed_one, first_gain, first_shift, expand, expand_bias, reduce, reduce_bias, gain, shift):
    slots = hidden.shape[0]
    width = expand.shape[1]
    row = constant((1, D))
    return pl.pallas_call(
        feed_kernel,
        grid_spec=pltpu.PrefetchScalarGridSpec(
            num_scalar_prefetch=2,
            grid=(width // FF_BLOCK,),
            in_specs=[
                constant(hidden.shape),
                constant(normed_one.shape),
                row,
                row,
                pl.BlockSpec((D, FF_BLOCK), lambda i, *_: (0, i)),
                pl.BlockSpec((1, FF_BLOCK), lambda i, *_: (0, i)),
                pl.BlockSpec((FF_BLOCK, D), lambda i, *_: (i, 0)),
                row,
                row,
                row,
            ],
            out_specs=[
                pl.BlockSpec((slots, FF_BLOCK), lambda i, *_: (0, i)),
                pl.BlockSpec((slots, FF_BLOCK), lambda i, *_: (0, i)),
                pl.BlockSpec((slots, D), lambda i, *_: (0, 0)),
                pl.BlockSpec((slots, D), lambda i, *_: (0, 0)),
                pl.BlockSpec((slots, 1), lambda i, *_: (0, 0)),
                pl.BlockSpec((ends.shape[0], D), lambda i, *_: (0, 0)),
            ],
            scratch_shapes=[pltpu.VMEM((slots, D), jnp.float32)],
        ),
        out_shape=[
            jax.ShapeDtypeStruct((slots, width), jnp.bfloat16),
            jax.ShapeDtypeStruct((slots, width), jnp.bfloat16),
            jax.ShapeDtypeStruct((slots, D), jnp.bfloat16),
            jax.ShapeDtypeStruct((slots, D), jnp.float32),
            jax.ShapeDtypeStruct((slots, 1), jnp.float32),
            jax.ShapeDtypeStruct((ends.shape[0], D), jnp.bfloat16),
        ],
        compiler_params=params(30),
        cost_estimate=COST,
        name="feed",
    )(ends, lengths, hidden, normed_one, first_gain, first_shift, expand, expand_bias, reduce, reduce_bias, gain, shift)


def split_halves(made, own_ref, sent_ref, odd, piece):
    own_ref[...] = made
    if sent_ref is not None:
        pairs = made.shape[0] // (2 * piece)
        both = made.reshape(pairs, 2, piece, made.shape[1])
        sent_ref[...] = jnp.where(odd, both[:, 0], both[:, 1]).reshape(sent_ref.shape)


def reduce_grad_kernel(
    ends_ref, lengths_ref, index_ref, cotangent_ref, normed_ref, inverse_ref, gain_ref, summary_grad_ref, active_ref,
    residual_ref, low_out_ref, sums_ref, own_ref, *rest, piece, tiles,
):
    sent_ref = rest[0] if len(rest) == 2 else None
    low = rest[-1]
    step = pl.program_id(0)

    @pl.when(step == 0)
    def _():
        sums_ref[...] = jnp.zeros_like(sums_ref)

    @pl.when(step < tiles)
    def _():
        first = step * WIDE
        live = ends_ref[ends_ref.shape[0] - 1]
        slot = lax.broadcasted_iota(jnp.int32, (WIDE, 1), 0) + first
        residual_ref[...] = jnp.where(slot < live, cotangent_ref[...].astype(jnp.float32), 0.0)
        for number in range(ends_ref.shape[0]):
            begin = ends_ref[number] - lengths_ref[number] - first

            @pl.when((begin >= 0) & (begin < WIDE))
            def _():
                residual_ref[pl.ds(begin, 1), :] += summary_grad_ref[number : number + 1, :]

        residual, gain_sum, shift_sum = norm_backward(
            residual_ref[...], normed_ref[...], inverse_ref[...], gain_ref[...].astype(jnp.float32)
        )
        made = residual.astype(jnp.bfloat16)
        residual_ref[...] = residual
        low_out_ref[...] = made
        low[pl.ds(first, WIDE), :] = made
        sums_ref[0:1, :] += gain_sum[None]
        sums_ref[1:2, :] += shift_sum[None]
        sums_ref[2:3, :] += jnp.sum(made.astype(jnp.float32), axis=0, keepdims=True)

    @pl.when(step >= tiles)
    def _():
        made = contract_rows(active_ref[...], low[...]).astype(jnp.bfloat16)
        split_halves(made, own_ref, sent_ref, index_ref[0] % 2 == 1, piece)


def reduce_grad(ends, lengths, index, count, cotangent, normed, inverse, gain, summary_grad, active):
    slots, width = active.shape
    piece = width // count
    halves = count == 16
    tiles = slots // WIDE
    row = lambda columns: pl.BlockSpec(
        (WIDE, columns), lambda i, *_: (jnp.minimum(i, tiles - 1), 0)
    )
    later = lambda i: jnp.maximum(i - tiles, 0)
    out_specs = [
        row(D),
        row(D),
        pl.BlockSpec((8, D), lambda i, *_: (0, 0)),
        pl.BlockSpec((D, D), lambda i, *_: (later(i), 0)),
    ]
    out_shape = [
        jax.ShapeDtypeStruct((slots, D), jnp.float32),
        jax.ShapeDtypeStruct((slots, D), jnp.bfloat16),
        jax.ShapeDtypeStruct((8, D), jnp.float32),
        jax.ShapeDtypeStruct((width, D), jnp.bfloat16),
    ]
    if halves:
        out_specs.append(pl.BlockSpec((D // 2, D), lambda i, *_: (later(i), 0)))
        out_shape.append(jax.ShapeDtypeStruct((width // 2, D), jnp.bfloat16))
    return pl.pallas_call(
        functools.partial(reduce_grad_kernel, piece=piece, tiles=tiles),
        grid_spec=pltpu.PrefetchScalarGridSpec(
            num_scalar_prefetch=3,
            grid=(tiles + width // D,),
            in_specs=[
                row(D),
                row(D),
                row(1),
                constant(gain.shape),
                constant(summary_grad.shape),
                pl.BlockSpec((slots, D), lambda i, *_: (0, later(i))),
            ],
            out_specs=out_specs,
            scratch_shapes=[pltpu.VMEM((slots, D), jnp.bfloat16)],
        ),
        out_shape=out_shape,
        compiler_params=params(28),
        cost_estimate=COST,
        name="reduce_grad",
    )(ends, lengths, index, cotangent, normed, inverse, gain, summary_grad, active)


def feed_grad_kernel(
    index_ref, low_ref, hidden_ref, reduce_ref, slope_ref, expand_ref, inverse_ref, gain_ref,
    residual_two_any, normed_any, context_any, output_any,
    expand_sums_ref, residual_ref, context_grad_ref, sums_ref, own_ref, *rest, piece, blocks,
):
    sent_ref = rest[0] if len(rest) == 8 else None
    inner, total, residual_two, normed, context, output, arrived = rest[-7:]
    step = pl.program_id(0)
    slots = low_ref.shape[0]
    odd = index_ref[0] % 2 == 1
    copies = [
        pltpu.make_async_copy(source, target, arrived.at[number])
        for number, (source, target) in enumerate(
            (
                (residual_two_any, residual_two),
                (normed_any, normed),
                (context_any, context),
                (output_any, output),
            )
        )
    ]

    @pl.when(step == 0)
    def _():
        for copy in copies:
            copy.start()
        total[...] = jnp.zeros_like(total)

    @pl.when(step < blocks)
    def _():
        sums = jnp.zeros(expand_sums_ref.shape, jnp.float32)
        for block in range(slots // WIDE):
            rows = slice(block * WIDE, (block + 1) * WIDE)
            grad = contract_cols(low_ref[rows, :], reduce_ref[...])
            made = (grad * slope_ref[rows, :].astype(jnp.float32)).astype(jnp.bfloat16)
            inner[rows, :] = made
            sums = sums + jnp.sum(made.astype(jnp.float32), axis=0, keepdims=True)
            total[rows, :] += contract_cols(made, expand_ref[...])
        expand_sums_ref[...] = sums
        gradient = contract_rows(hidden_ref[...], inner[...]).astype(jnp.bfloat16)
        split_halves(gradient, own_ref, sent_ref, odd, piece)

    @pl.when(step == blocks)
    def _():
        for copy in copies:
            copy.wait()
        gain = gain_ref[...].astype(jnp.float32)
        sums_ref[...] = jnp.zeros_like(sums_ref)
        for block in range(slots // WIDE):
            rows = slice(block * WIDE, (block + 1) * WIDE)
            residual, gain_sum, shift_sum = norm_backward(
                residual_two[rows, :] + total[rows, :], normed[rows, :], inverse_ref[rows, :], gain
            )
            branch = residual.astype(jnp.bfloat16)
            residual_ref[rows, :] = residual
            inner[rows, :] = branch
            sums_ref[0:1, :] += gain_sum[None]
            sums_ref[1:2, :] += shift_sum[None]
            sums_ref[2:3, :] += jnp.sum(branch.astype(jnp.float32), axis=0, keepdims=True)
            context_grad_ref[rows, :] = contract_cols(branch, output[...]).astype(jnp.bfloat16)
        gradient = contract_rows(context[...], inner[...]).astype(jnp.bfloat16)
        split_halves(gradient, own_ref, sent_ref, odd, piece)


def feed_grad(index, count, low, hidden, reduce, slope, expand, residual_two, normed, inverse, gain, context, output):
    slots, width = slope.shape
    halves = count == 16
    blocks = width // D
    capped = lambda i: jnp.minimum(i, blocks - 1)
    whole = pl.BlockSpec((slots, D), lambda i, *_: (0, 0))
    out_specs = [
        pl.BlockSpec((1, D), lambda i, *_: (0, capped(i))),
        whole,
        whole,
        pl.BlockSpec((8, D), lambda i, *_: (0, 0)),
        pl.BlockSpec((D, D), lambda i, *_: (0, i)),
    ]
    out_shape = [
        jax.ShapeDtypeStruct((1, width), jnp.float32),
        jax.ShapeDtypeStruct((slots, D), jnp.float32),
        jax.ShapeDtypeStruct((slots, D), jnp.bfloat16),
        jax.ShapeDtypeStruct((8, D), jnp.float32),
        jax.ShapeDtypeStruct((D, width + D), jnp.bfloat16),
    ]
    if halves:
        out_specs.append(pl.BlockSpec((D // 2, D), lambda i, *_: (0, i)))
        out_shape.append(jax.ShapeDtypeStruct((D // 2, width + D), jnp.bfloat16))
    return pl.pallas_call(
        functools.partial(feed_grad_kernel, piece=D // count, blocks=blocks),
        grid_spec=pltpu.PrefetchScalarGridSpec(
            num_scalar_prefetch=1,
            grid=(blocks + 1,),
            in_specs=[
                constant(low.shape),
                constant(hidden.shape),
                pl.BlockSpec((D, D), lambda i, *_: (capped(i), 0)),
                pl.BlockSpec((slots, D), lambda i, *_: (0, capped(i))),
                pl.BlockSpec((D, D), lambda i, *_: (0, capped(i))),
                constant(inverse.shape),
                constant(gain.shape),
            ]
            + [pl.BlockSpec(memory_space=pl.ANY)] * 4,
            out_specs=out_specs,
            scratch_shapes=[
                pltpu.VMEM((slots, D), jnp.bfloat16),
                pltpu.VMEM((slots, D), jnp.float32),
                pltpu.VMEM((slots, D), jnp.float32),
                pltpu.VMEM((slots, D), jnp.float32),
                pltpu.VMEM((slots, D), jnp.bfloat16),
                pltpu.VMEM((D, D), jnp.bfloat16),
                pltpu.SemaphoreType.DMA((4,)),
            ],
        ),
        out_shape=out_shape,
        compiler_params=params(56),
        cost_estimate=COST,
        name="feed_grad",
    )(index, low, hidden, reduce, slope, expand, inverse, gain, residual_two, normed, context, output)


def attend_grad_kernel(index_ref, tokens_ref, projected_ref, own_ref, sent_ref=None, *, piece):
    made = contract_rows(tokens_ref[...], projected_ref[...]).astype(jnp.bfloat16)
    split_halves(made, own_ref, sent_ref, index_ref[0] % 2 == 1, piece)


def attend_grad(index, count, tokens, projected_grad):
    slots = tokens.shape[0]
    halves = count == 16
    extra = TILE if halves else 0
    out_specs = [pl.BlockSpec((D, D), lambda i, *_: (0, i))]
    out_shape = [jax.ShapeDtypeStruct((D, 3 * D + extra), jnp.bfloat16)]
    if halves:
        out_specs.append(pl.BlockSpec((D // 2, D), lambda i, *_: (0, i)))
        out_shape.append(jax.ShapeDtypeStruct((D // 2, 3 * D + extra), jnp.bfloat16))
    return pl.pallas_call(
        functools.partial(attend_grad_kernel, piece=D // count),
        grid_spec=pltpu.PrefetchScalarGridSpec(
            num_scalar_prefetch=1,
            grid=(3,),
            in_specs=[constant(tokens.shape)]
            + [pl.BlockSpec((slots, D), lambda i, *_: (0, i))],
            out_specs=out_specs,
        ),
        out_shape=out_shape,
        compiler_params=params(20),
        cost_estimate=COST,
        name="attend_grad",
    )(index, tokens, projected_grad)


def tokens_grad_kernel(projected_ref, attend_ref, residual_ref, out_ref):
    out_ref[...] = (
        residual_ref[...] + contract_cols(projected_ref[...], attend_ref[...])
    ).astype(jnp.bfloat16)


def tokens_grad_of(projected_grad, attend, residual):
    slots, width = projected_grad.shape
    tile = lambda columns: pl.BlockSpec((WIDE, columns), lambda i: (i, 0))
    return pl.pallas_call(
        tokens_grad_kernel,
        grid=(slots // WIDE,),
        in_specs=[tile(width), constant(attend.shape), tile(D)],
        out_specs=tile(D),
        out_shape=jax.ShapeDtypeStruct((slots, D), jnp.bfloat16),
        compiler_params=params(16),
        cost_estimate=COST,
        name="tokens_grad",
    )(projected_grad, attend, residual)


def pack_kernel(index_ref, second_ref, first_ref, bias_ref, expand_ref, own_any, sent_any, own_ref, sent_ref, rows, *, count):
    width = D // count
    rows[...] = jnp.zeros_like(rows)
    vectors = [bias_ref[0:1, :D], bias_ref[0:1, D:]]
    vectors += [first_ref[2:3, :], first_ref[0:1, :], first_ref[1:2, :]]
    vectors += [second_ref[2:3, :], second_ref[0:1, :], second_ref[1:2, :]]
    for number, vector in enumerate(vectors):
        rows[number : number + 1, :] = vector
    for number in range(count):
        for part in range(4):
            first = (number * 4 + part) * width
            rows[8 + part : 9 + part, number * width : (number + 1) * width] = expand_ref[
                0:1, first : first + width
            ]
    made = rows[...].T.astype(jnp.bfloat16)
    split_halves(made, own_ref, sent_ref, index_ref[0] % 2 == 1, width)


def pack(index, count, second, first, bias, expand, own, sent):
    whole = lambda shape: pl.BlockSpec(shape, lambda i, *_: (0,) * len(shape))
    place = own.shape[1] // TILE - 1
    return pl.pallas_call(
        functools.partial(pack_kernel, count=count),
        grid_spec=pltpu.PrefetchScalarGridSpec(
            num_scalar_prefetch=1,
            grid=(1,),
            in_specs=[whole(x.shape) for x in (second, first, bias, expand)]
            + [pl.BlockSpec(memory_space=pl.ANY)] * 2,
            out_specs=[
                pl.BlockSpec((D, TILE), lambda i, *_: (0, place)),
                pl.BlockSpec((D // 2, TILE), lambda i, *_: (0, place)),
            ],
            scratch_shapes=[pltpu.VMEM((TILE, D), jnp.float32)],
        ),
        out_shape=[jax.ShapeDtypeStruct(x.shape, x.dtype) for x in (own, sent)],
        input_output_aliases={5: 0, 6: 1},
        compiler_params=params(8),
        cost_estimate=COST,
        name="pack",
    )(index, second, first, bias, expand, own, sent)


def merge_kernel(index_ref, *refs):
    total = refs[0][...].astype(jnp.float32)
    for ref in refs[1:-1]:
        total = total + ref[...].astype(jnp.float32)
    refs[-1][...] = total.astype(refs[-1].dtype)


def merge(index, sources, stage, bits, kind, weight=1):
    rows, width = sources[0].shape[1:]
    made = 1 << max(bits - 1 - stage, 0)
    steps = min(made, 2)
    blocks = 3 if stage == bits and width % (3 * TILE) == 0 else 1
    block = (made // steps, 1, 1, rows, width // blocks)

    def spec(shift):
        def place(i, j, own):
            if stage == bits:
                return (0, 0, own[0] >> shift, 0, j)
            below = own[0] & ((1 << stage) - 1)
            return (i, 1 - ((own[0] >> stage) & 1), below >> shift, 0, j)

        return pl.BlockSpec(block, place)

    def view(source, shift):
        if stage == bits:
            source = source.reshape(1, 1, 1 << (bits - shift), rows, width)
        else:
            source = source.reshape(made, 2, 1 << (stage - shift), rows, width)
        return pltpu.with_memory_space_constraint(source, pltpu.HBM)

    return pl.pallas_call(
        merge_kernel,
        grid_spec=pltpu.PrefetchScalarGridSpec(
            num_scalar_prefetch=1,
            grid=(steps, blocks),
            in_specs=[spec(shift) for shift in range(len(sources))],
            out_specs=pl.BlockSpec(block, lambda i, j, own: (i, 0, 0, 0, j)),
        ),
        out_shape=jax.ShapeDtypeStruct((made, 1, 1, rows, width), kind),
        compiler_params=params(20),
        cost_estimate=cost(weight),
        name="merge",
    )(index, *[view(source, shift) for shift, source in enumerate(sources)]).reshape(made, rows, width)


class Scatter:
    def __init__(self, index, count, own, sent=None):
        self.index, self.count, self.own = index, count, own
        self.stage = 0
        self.bits = 4
        self.sent = sent
        self.terms = []
        if sent is not None:
            pieces = (count, own.shape[0] // count, own.shape[1])
            self.terms = [own.reshape(pieces)]
            self.sent = sent.reshape((count // 2,) + pieces[1:])

    def settle(self, since):
        if since is not None:
            self.terms[-1] = lax.optimization_barrier((self.terms[-1], since))[0]

    def begin(self, since=None, ahead=None, weight=1):
        if self.sent is None:
            return since, ahead
        if self.stage == 0:
            sent = self.sent
        else:
            self.settle(since)
            sent = merge(
                self.index, self.terms, self.stage, self.bits, self.own.dtype, weight
            )
        if ahead is not None:
            sent, ahead = lax.optimization_barrier((sent, ahead))
        self.terms.append(exchanged(sent, ("batch",), 1 << self.stage))
        self.stage += 1
        return sent, ahead

    def result(self, since=None):
        if self.sent is None:
            return lax.psum_scatter(
                self.own.astype(jnp.float32), "batch", scatter_dimension=0, tiled=True
            )
        self.settle(since)
        return merge(self.index, self.terms, self.stage, self.bits, jnp.float32)[0]


def per_device(
    tokens,
    cotangent,
    question_lengths,
    passage_lengths,
    attend_weight,
    query_bias,
    value_bias,
    output_weight,
    output_bias,
    first_gain,
    first_shift,
    expand_weight,
    expand_bias,
    reduce_weight,
    reduce_bias,
    second_gain,
    second_shift,
):
    inputs = tokens[0]
    is_passage = lax.axis_index("enc") == 1
    count = lax.axis_size("batch")
    index = lax.axis_index("batch").astype(jnp.int32).reshape(1)
    lengths_here = jnp.where(is_passage, passage_lengths[0], question_lengths[0])
    order = jnp.arange(lengths_here.shape[0], dtype=jnp.int32)
    ends_here = jnp.sum(
        jnp.where(order[None, :] <= order[:, None], lengths_here[None, :], 0), axis=1
    )
    projected, context, total, hidden_low, normed_one, inverse_one = attention(
        ends_here,
        inputs,
        attend_weight[0],
        query_bias,
        value_bias,
        output_weight[0],
        output_bias,
        first_gain,
        first_shift,
    )
    active, slope, result, normed_two, inverse_two, summary = feed(
        ends_here,
        lengths_here,
        hidden_low,
        normed_one,
        first_gain,
        first_shift,
        expand_weight[0],
        expand_bias,
        reduce_weight[0],
        reduce_bias,
        second_gain,
        second_shift,
    )
    mine, other, place = gathered_summaries(summary)
    seq_count = summary.shape[0]
    mine, other = mine.reshape(-1, D), other.reshape(-1, D)
    questions = jnp.where(is_passage, other, mine)
    passages = jnp.where(is_passage, mine, other)
    summary_scale = 2.0 / math.sqrt(D)
    total_seqs = questions.shape[0]
    logits = contract_cols(questions, passages) * summary_scale
    highest_logit = jnp.max(logits, axis=1, keepdims=True)
    logit_total = highest_logit + jnp.log(
        jnp.sum(jnp.exp(logits - highest_logit), axis=1, keepdims=True)
    )
    matches = jnp.eye(total_seqs, dtype=jnp.float32)
    score_grad = (LOSS_WEIGHT * (jnp.exp(logits - logit_total) - matches)).astype(jnp.bfloat16)
    own_rows = lax.dynamic_slice_in_dim(score_grad, place * seq_count, seq_count, 0)
    own_columns = lax.dynamic_slice_in_dim(score_grad, place * seq_count, seq_count, 1)
    question_term = (product(own_rows, passages) * summary_scale).astype(jnp.bfloat16)
    passage_term = contract_rows(own_columns, questions) * summary_scale
    summary_grad = jnp.where(is_passage, passage_term, question_term.astype(jnp.float32))
    residual_two, reduce_input, second_sums, *reduce_parts = reduce_grad(
        ends_here,
        lengths_here,
        index,
        count,
        cotangent[0],
        normed_two,
        inverse_two,
        second_gain,
        summary_grad,
        active,
    )
    reduce_share = Scatter(index, count, *reduce_parts)
    _, reduce_input = reduce_share.begin(ahead=reduce_input)
    expand_sums, residual_one, context_grad, first_sums, *expand_parts = feed_grad(
        index,
        count,
        reduce_input,
        hidden_low,
        reduce_weight[0],
        slope,
        expand_weight[0],
        residual_two,
        normed_one,
        inverse_one,
        first_gain,
        context,
        output_weight[0],
    )
    _, context_grad = reduce_share.begin(since=context_grad, ahead=context_grad)
    expand_share = Scatter(index, count, *expand_parts)
    _, context_grad = expand_share.begin(ahead=context_grad)
    projected_grad, bias_sums = attention_grad(ends_here, projected, context_grad, context, total)
    _, projected_grad = expand_share.begin(since=projected_grad, ahead=projected_grad)
    _, projected_grad = reduce_share.begin(since=projected_grad, ahead=projected_grad)
    attend_parts = attend_grad(index, count, inputs, projected_grad)
    if count == 16:
        attend_parts = pack(
            index, count, second_sums, first_sums, bias_sums, expand_sums, *attend_parts
        )
    attend_share = Scatter(index, count, *attend_parts)
    _, projected_grad = attend_share.begin(ahead=projected_grad)
    tokens_grad = tokens_grad_of(projected_grad, attend_weight[0], residual_one)
    token, _ = reduce_share.begin(since=tokens_grad, weight=3)
    token, _ = expand_share.begin(since=token, weight=6)
    token, _ = attend_share.begin(since=token)
    reduced = reduce_share.result(since=token)
    token, _ = expand_share.begin(since=reduced)
    token, _ = attend_share.begin(since=token)
    expanded = expand_share.result(since=token)
    token, _ = attend_share.begin(since=expanded)
    attended = attend_share.result(since=token)
    width = D // count
    if count == 16:
        packed = attended[:, 3 * D :].T
        shares = [packed[i][None] for i in range(8)]
        expand_bias_share = packed[8:12].reshape(1, -1)
    else:
        vectors = [bias_sums[0, :D], bias_sums[0, D:]]
        vectors += [first_sums[2], first_sums[0], first_sums[1]]
        vectors += [second_sums[2], second_sums[0], second_sums[1], expand_sums[0]]
        flat = jnp.concatenate([vector.reshape(count, -1) for vector in vectors], axis=1)
        packed = lax.psum_scatter(flat, "batch", scatter_dimension=0, tiled=True)[0]
        shares = [packed[None, i * width : (i + 1) * width] for i in range(8)]
        expand_bias_share = packed[None, 8 * width :]
    wide = expand_weight.shape[2]
    return (
        result[None],
        tokens_grad[None],
        attended[None, :, : 3 * D],
        shares[0],
        shares[1],
        expanded[None, :, wide:],
        shares[2],
        shares[3],
        shares[4],
        expanded[None, :, :wide],
        expand_bias_share,
        reduced[None],
        shares[5],
        shares[6],
        shares[7],
    )


def solution(mesh):
    in_specs = (
        P("enc", "batch", None),
        P("enc", "batch", None),
        P("batch", None),
        P("batch", None),
        P("enc", None, None),
        P("enc", None),
        P("enc", None),
        P("enc", None, None),
        P("enc", None),
        P("enc", None),
        P("enc", None),
        P("enc", None, None),
        P("enc", None),
        P("enc", None, None),
        P("enc", None),
        P("enc", None),
        P("enc", None),
    )
    out_specs = (
        P("enc", "batch", None),
        P("enc", "batch", None),
        P("enc", "batch", None),
        P("enc", "batch"),
        P("enc", "batch"),
        P("enc", "batch", None),
        P("enc", "batch"),
        P("enc", "batch"),
        P("enc", "batch"),
        P("enc", "batch", None),
        P("enc", "batch"),
        P("enc", "batch", None),
        P("enc", "batch"),
        P("enc", "batch"),
        P("enc", "batch"),
    )
    return jax.shard_map(
        per_device, mesh=mesh, in_specs=in_specs, out_specs=out_specs, check_vma=False
    )
```

```python
import functools
import math

import jax
import jax.numpy as jnp
from jax import lax
from jax.experimental import pallas as pl
from jax.experimental.pallas import tpu as pltpu
from jax.sharding import PartitionSpec as P

D = 768
HEADS = 12
HEAD_DIM = 64
TILE = 128
WIDE = 2 * TILE
PAIRS = HEADS // 2
ROWS = 16
FF_BLOCK = 512
EARLY = 4


def cost(weight):
    return pl.CostEstimate(flops=int(weight * 2 * 10**9), bytes_accessed=10**3, transcendentals=0)


COST = cost(1)


EPSILON = 1e-12
SCORE_SCALE = 0.125
MASKED = -1000000000.0
LOSS_WEIGHT = 16.0
INV_ROOT_TWO = 0.7071067811865476
INV_ROOT_TAU = 0.3989422804014327


def exchanged(value, axes, distance):
    count = math.prod(lax.axis_size(axis) for axis in axes)
    return lax.ppermute(value, axes, [(source, source ^ distance) for source in range(count)])


def gathered_summaries(summary):
    count = lax.axis_size("batch")
    if count != 16:
        everything = lax.all_gather(summary, ("enc", "batch"), axis=0, tiled=False)
        own = lax.axis_index("enc")
        everything = everything.reshape((2, count) + summary.shape)
        mine = lax.dynamic_index_in_dim(everything, own, 0, keepdims=False)
        other = lax.dynamic_index_in_dim(everything, 1 - own, 0, keepdims=False)
        return mine, other, lax.axis_index("batch")
    both = ("enc", "batch")
    pair = jnp.stack([summary, exchanged(summary, both, 1)])
    mine = [pair, exchanged(pair, both, 2)]
    other = [exchanged(pair, both, 16), exchanged(pair, both, 18)]
    plane = jnp.concatenate(mine + other)
    parts = [plane] + [exchanged(plane, both, distance) for distance in (4, 8, 12)]
    size = plane.shape[0] // 2
    return (
        jnp.concatenate([part[:size] for part in parts]),
        jnp.concatenate([part[size:] for part in parts]),
        0,
    )


def product(left_side, right_side):
    return jnp.dot(left_side, right_side, preferred_element_type=jnp.float32)


def contract_rows(left_side, right_side):
    return lax.dot_general(
        left_side, right_side, (((0,), (0,)), ((), ())), preferred_element_type=jnp.float32
    )


def contract_cols(left_side, right_side):
    return lax.dot_general(
        left_side, right_side, (((1,), (1,)), ((), ())), preferred_element_type=jnp.float32
    )


def norm_forward(values, scale_row, shift_row):
    centred = values - jnp.mean(values, axis=1, keepdims=True)
    inverse = lax.rsqrt(jnp.mean(centred * centred, axis=1, keepdims=True) + EPSILON)
    normed = centred * inverse
    return (normed * scale_row + shift_row, normed, inverse)


def norm_backward(upstream, normed, inverse, scale_row):
    scale_grad = jnp.sum(upstream * normed, axis=0)
    shift_grad = jnp.sum(upstream, axis=0)
    scaled = upstream * scale_row
    centred = scaled - jnp.mean(scaled, axis=1, keepdims=True)
    centred = centred - normed * jnp.mean(scaled * normed, axis=1, keepdims=True)
    return (centred * inverse, scale_grad, shift_grad)


def params(megabytes):
    return pltpu.CompilerParams(vmem_limit_bytes=max(megabytes, 64) << 20)


def constant(shape):
    return pl.BlockSpec(shape, lambda *_: (0,) * len(shape), pipeline_mode=pl.Buffered(1))


def slot_segments(ends_ref, first, shape, axis):
    slots = lax.broadcasted_iota(jnp.int32, shape, axis) + first
    number = jnp.zeros(shape, jnp.int32)
    for j in range(ends_ref.shape[0]):
        number = number + (slots >= ends_ref[j]).astype(jnp.int32)
    return number

def key_tiles(ends_ref, first, last, slots):
    start, stop = jnp.int32(0), jnp.int32(slots)
    for j in reversed(range(ends_ref.shape[0])):
        end = ends_ref[j]
        start = jnp.maximum(start, jnp.where(end <= first, end, 0))
        stop = jnp.where(end > last, end, stop)
    return start // TILE, (stop + TILE - 1) // TILE

def head_masks(shape, axis):
    even = (lax.broadcasted_iota(jnp.int32, shape, axis) // HEAD_DIM) % 2 == 0
    return [m.astype(jnp.float32).astype(jnp.bfloat16) for m in (even, ~even)]

def columns(pair): return slice(pair * TILE, (pair + 1) * TILE)

def fill_stacks(source_ref, tiles, stack=None, turned=None):
    width = (stack if stack is not None else turned).shape[1]
    across = head_masks((1, width), 1)
    down = head_masks((width, TILE), 0)
    def one(tile, _):
        rows = source_ref[pl.ds(tile * TILE, TILE), :]
        if stack is not None:
            for side in range(2):
                stack[pl.ds(tile * WIDE + side * TILE, TILE), :] = rows * across[side]
        if turned is not None:
            flipped = rows.T
            for side in range(2):
                turned[tile, :, columns(side)] = flipped * down[side]
        return 0
    lax.fori_loop(0, tiles, one, 0)
    if stack is not None:
        stack[pl.ds(tiles * WIDE, WIDE), :] = jnp.zeros((WIDE, width), jnp.bfloat16)
    if turned is not None:
        turned[tiles] = jnp.zeros((width, WIDE), jnp.bfloat16)

def fill_segments(ends_ref, segments):
    def one(tile, _):
        segments[tile] = slot_segments(ends_ref, tile * TILE, (TILE, TILE), 0)
        return 0
    lax.fori_loop(0, segments.shape[0] - 1, one, 0)
    segments[segments.shape[0] - 1] = jnp.full((TILE, TILE), -1, jnp.int32)

def matching(segments, number, own):
    there = [segments[number], segments[number + 1]]
    return [jnp.concatenate([one, one], axis=1) == own for one in there]

def grouped(values): return values.reshape(TILE // 8, 8, WIDE)

def attention_kernel(ends_ref, tokens_ref, attend_any, query_bias_ref, value_bias_ref, output_ref, output_bias_ref, gain_ref, shift_ref, queries_any, keys_any, values_any, context_ref, total_ref, hidden_ref, normed_ref, inverse_ref, keys, values, segments, queries, scores, highest, sums, out, weights_in, queries_ref, keys_ref, values_ref, moved):
    tile = pl.program_id(0)
    slots = tokens_ref.shape[0]
    tiles = slots // TILE
    leaving = [
        pltpu.make_async_copy(source, target, moved.at[3 + third])
        for third, (source, target) in enumerate(
            ((queries_ref, queries_any), (keys_ref, keys_any), (values_ref, values_any))
        )
    ]
    @pl.when(tile == 0)
    def _():
        thirds = (
            (queries_ref, query_bias_ref),
            (keys_ref, None),
            (values_ref, value_bias_ref),
        )
        parts = [slice(third * D, (third + 1) * D) for third in range(3)]
        for third, part in enumerate(parts):
            pltpu.make_async_copy(
                attend_any.at[:, part], weights_in.at[third], moved.at[third]
            ).start()
        for third, (made_ref, bias_ref) in enumerate(thirds):
            pltpu.make_async_copy(
                attend_any.at[:, parts[third]], weights_in.at[third], moved.at[third]
            ).wait()
            for block in range(slots // WIDE):
                rows = slice(block * WIDE, (block + 1) * WIDE)
                made = product(tokens_ref[rows, :], weights_in[third])
                if bias_ref is not None:
                    made = made + bias_ref[...].astype(jnp.float32)
                made_ref[rows, :] = made.astype(jnp.bfloat16)
            leaving[third].start()
        fill_stacks(keys_ref, tiles, stack=keys)
        fill_stacks(values_ref, tiles, turned=values)
        fill_segments(ends_ref, segments)
    first = tile * WIDE
    low, high = key_tiles(ends_ref, first, first + WIDE - 1, slots)
    highest[...] = jnp.full_like(highest, -3e38)
    sums[...] = jnp.zeros_like(sums)
    out[...] = jnp.zeros_like(out)
    queries[...] = (queries_ref[pl.ds(first, WIDE), :] * jnp.bfloat16(SCORE_SCALE)).T
    own = slot_segments(ends_ref, first, (1, WIDE), 1)
    windows = (high - low + 1) // 2
    def score(window, _):
        number = low + 2 * window
        same = matching(segments, number, own)
        for pair in range(PAIRS):
            both = product(keys[pl.ds(number * WIDE, 2 * WIDE), columns(pair)], queries[columns(pair), :])
            for place in range(4):
                half = jnp.where(same[place // 2], both[columns(place), :], MASKED)
                scores[pair, window, columns(place), :] = half
                head = 2 * pair + place % 2
                highest[head] = jnp.maximum(highest[head], jnp.max(grouped(half), axis=0))
        return 0
    lax.fori_loop(0, windows, score, 0)
    for head in range(HEADS):
        highest[head] = jnp.broadcast_to(jnp.max(highest[head], axis=0, keepdims=True), (8, WIDE))
    def weigh(window, _):
        number = low + 2 * window
        for pair in range(PAIRS):
            parts = []
            for place in range(4):
                head = 2 * pair + place % 2
                weights = jnp.exp(scores[pair, window, columns(place), :] - highest[head, :1, :])
                sums[head] += jnp.sum(grouped(weights), axis=0)
                parts.append(weights.astype(jnp.bfloat16))
            there = jnp.concatenate([values[number, columns(pair), :], values[number + 1, columns(pair), :]], axis=1)
            out[columns(pair), :] += product(there, jnp.concatenate(parts, axis=0))
        return 0
    lax.fori_loop(0, windows, weigh, 0)
    for head in range(HEADS):
        total = jnp.sum(sums[head], axis=0, keepdims=True)
        part = slice(head * HEAD_DIM, (head + 1) * HEAD_DIM)
        out[part, :] = out[part, :] * (1.0 / total)
        total_ref[head : head + 1, :] = highest[head, :1, :] + jnp.log(total)
    total_ref[HEADS:, :] = jnp.zeros((ROWS - HEADS, WIDE), jnp.float32)
    context = out[...].T.astype(jnp.bfloat16)
    context_ref[...] = context
    branch = product(context, output_ref[...]) + output_bias_ref[...].astype(jnp.float32)
    hidden, normed, inverse = norm_forward(
        tokens_ref[pl.ds(first, WIDE), :].astype(jnp.float32) + branch,
        gain_ref[...].astype(jnp.float32),
        shift_ref[...].astype(jnp.float32),
    )
    hidden_ref[...] = hidden.astype(jnp.bfloat16)
    normed_ref[...] = normed
    inverse_ref[...] = inverse
    @pl.when(tile == pl.num_programs(0) - 1)
    def _():
        for copy in leaving:
            copy.wait()

def attention(ends, tokens, attend, query_bias, value_bias, output, output_bias, gain, shift):
    slots = tokens.shape[0]
    tiles = slots // TILE
    tile = pl.BlockSpec((WIDE, D), lambda i, e: (i, 0))
    return pl.pallas_call(
        attention_kernel,
        grid_spec=pltpu.PrefetchScalarGridSpec(
            num_scalar_prefetch=1,
            grid=(slots // WIDE,),
            in_specs=[
                constant(tokens.shape),
                pl.BlockSpec(memory_space=pl.ANY),
            ]
            + [constant(x.shape) for x in (query_bias, value_bias, output)]
            + [constant((1, D))] * 3,
            out_specs=[
            ]
            + [pl.BlockSpec(memory_space=pl.ANY)] * 3
            + [
                tile,
                pl.BlockSpec((ROWS, WIDE), lambda i, e: (0, i)),
                tile,
                tile,
                pl.BlockSpec((WIDE, 1), lambda i, e: (i, 0)),
            ],
            scratch_shapes=[
                pltpu.VMEM(((tiles + 1) * WIDE, D), jnp.bfloat16),
                pltpu.VMEM((tiles + 1, D, WIDE), jnp.bfloat16),
                pltpu.VMEM((tiles + 1, TILE, TILE), jnp.int32),
                pltpu.VMEM((D, WIDE), jnp.bfloat16),
                pltpu.VMEM((PAIRS, (tiles + 1) // 2, 2 * WIDE, WIDE), jnp.float32),
                pltpu.VMEM((HEADS, 8, WIDE), jnp.float32),
                pltpu.VMEM((HEADS, 8, WIDE), jnp.float32),
                pltpu.VMEM((D, WIDE), jnp.float32),
                pltpu.VMEM((3, D, D), jnp.bfloat16),
            ]
            + [pltpu.VMEM((slots, D), jnp.bfloat16)] * 3
            + [pltpu.SemaphoreType.DMA((6,))],
        ),
        out_shape=[
        ]
        + [jax.ShapeDtypeStruct((slots, D), jnp.bfloat16)] * 4
        + [
            jax.ShapeDtypeStruct((ROWS, slots), jnp.float32),
            jax.ShapeDtypeStruct((slots, D), jnp.bfloat16),
            jax.ShapeDtypeStruct((slots, D), jnp.float32),
            jax.ShapeDtypeStruct((slots, 1), jnp.float32),
        ],
        compiler_params=params(42),
        cost_estimate=COST,
        name="attention",
    )(ends, tokens, attend, query_bias, value_bias, output, output_bias, gain, shift)


def attention_grad_kernel(ends_ref, queries_ref, keys_ref, values_ref, outer_ref, context_ref, total_ref, out_ref, bias_ref, keys, values, turned, segments, queries, outers, query_sides, outer_sides, key_sum, value_sum, query_sum, deltas, *, first_head):
    tile = pl.program_id(0)
    slots, width = keys_ref.shape
    tiles = slots // TILE
    heads = width // HEAD_DIM
    live = (ends_ref[ends_ref.shape[0] - 1] + TILE - 1) // TILE
    first = tile * WIDE
    rows = pl.ds(first, WIDE)
    @pl.when(tile == 0)
    def _():
        fill_stacks(keys_ref, tiles, stack=keys, turned=turned)
        fill_stacks(values_ref, tiles, stack=values)
        fill_segments(ends_ref, segments)
        key_sum[...] = jnp.zeros_like(key_sum)
        value_sum[...] = jnp.zeros_like(value_sum)
        bias_ref[...] = jnp.zeros_like(bias_ref)
    @pl.when(first >= live * TILE)
    def _():
        out_ref[rows, :width] = jnp.zeros((WIDE, width), jnp.bfloat16)
    @pl.when(first < live * TILE)
    def _():
        low, high = key_tiles(ends_ref, first, first + WIDE - 1, slots)
        high = jnp.minimum(high, live)
        query_sum[...] = jnp.zeros_like(query_sum)
        across = head_masks((1, width), 1)
        scaled = queries_ref[...] * jnp.bfloat16(SCORE_SCALE)
        outer = outer_ref[...]
        queries[...] = scaled.T
        outers[...] = outer.T
        for side in range(2):
            query_sides[side] = scaled * across[side]
            outer_sides[side] = outer * across[side]
        both = (outer.astype(jnp.float32) * context_ref[...].astype(jnp.float32)).T
        for head in range(heads):
            deltas[head : head + 1, :] = jnp.sum(both[head * HEAD_DIM : (head + 1) * HEAD_DIM, :], axis=0, keepdims=True)
        own = slot_segments(ends_ref, first, (1, WIDE), 1)
        def visit(window, _):
            number = low + 2 * window
            same = matching(segments, number, own)
            there = pl.ds(number * WIDE, 2 * WIDE)
            where = pl.ds(number * TILE, WIDE)
            for pair in range(heads // 2):
                both = product(keys[there, columns(pair)], queries[columns(pair), :])
                grads = product(values[there, columns(pair)], outers[columns(pair), :])
                weights_parts, parts = [], []
                for place in range(4):
                    head = 2 * pair + place % 2
                    part = columns(place)
                    weights = jnp.where(same[place // 2], jnp.exp(both[part, :] - total_ref[first_head + head : first_head + head + 1, :]), 0.0)
                    parts.append((weights * (grads[part, :] - deltas[head : head + 1, :])).astype(jnp.bfloat16))
                    weights_parts.append(weights.astype(jnp.bfloat16))
                def folded(blocks, sides):
                    total = 0
                    for side in range(2):
                        total = total + product(jnp.concatenate(blocks[side::2], axis=0), sides[side, :, columns(pair)])
                    return total
                key_sum[where, columns(pair)] += folded(parts, query_sides)
                value_sum[where, columns(pair)] += folded(weights_parts, outer_sides)
                across = jnp.concatenate([turned[number, columns(pair), :], turned[number + 1, columns(pair), :]], axis=1)
                query_sum[columns(pair), :] += product(across, jnp.concatenate(parts, axis=0))
            return 0
        lax.fori_loop(0, (high - low + 1) // 2, visit, 0)
        done = (query_sum[...] * SCORE_SCALE).T.astype(jnp.bfloat16)
        out_ref[rows, :width] = done
        bias_ref[:, :width] += jnp.sum(done.astype(jnp.float32), axis=0, keepdims=True)
    @pl.when(tile == pl.num_programs(0) - 1)
    def _():
        def close(number, _):
            there = pl.ds(number * TILE, TILE)
            out_ref[there, width : 2 * width] = key_sum[there, :].astype(jnp.bfloat16)
            done = value_sum[there, :].astype(jnp.bfloat16)
            out_ref[there, 2 * width :] = done
            bias_ref[:, width:] += jnp.sum(done.astype(jnp.float32), axis=0, keepdims=True)
            return 0
        lax.fori_loop(0, tiles, close, 0)

def attention_grad(first_pair, pairs, ends, queries, keys, values, outer, context, total):
    slots = queries.shape[0]
    tiles = slots // TILE
    width = pairs * TILE
    place = first_pair // pairs
    whole = lambda i, e: (0, 0)
    return pl.pallas_call(
        functools.partial(attention_grad_kernel, first_head=2 * first_pair),
        grid_spec=pltpu.PrefetchScalarGridSpec(
            num_scalar_prefetch=1, grid=(slots // WIDE,),
            in_specs=[
                pl.BlockSpec((WIDE, width), lambda i, e: (i, place)),
                pl.BlockSpec((slots, width), lambda i, e: (0, place), pipeline_mode=pl.Buffered(1)),
                pl.BlockSpec((slots, width), lambda i, e: (0, place), pipeline_mode=pl.Buffered(1)),
                pl.BlockSpec((WIDE, width), lambda i, e: (i, place)),
                pl.BlockSpec((WIDE, width), lambda i, e: (i, place)),
                pl.BlockSpec((ROWS, WIDE), lambda i, e: (0, i)),
            ],
            out_specs=[pl.BlockSpec((slots, 3 * width), whole), pl.BlockSpec((1, 2 * width), whole)],
            scratch_shapes=[
                pltpu.VMEM(((tiles + 1) * WIDE, width), jnp.bfloat16), pltpu.VMEM(((tiles + 1) * WIDE, width), jnp.bfloat16), pltpu.VMEM((tiles + 1, width, WIDE), jnp.bfloat16),
                pltpu.VMEM((tiles + 1, TILE, TILE), jnp.int32),
                pltpu.VMEM((width, WIDE), jnp.bfloat16), pltpu.VMEM((width, WIDE), jnp.bfloat16),
                pltpu.VMEM((2, WIDE, width), jnp.bfloat16), pltpu.VMEM((2, WIDE, width), jnp.bfloat16),
                pltpu.VMEM((slots + TILE, width), jnp.float32), pltpu.VMEM((slots + TILE, width), jnp.float32), pltpu.VMEM((width, WIDE), jnp.float32),
                pltpu.VMEM((ROWS, WIDE), jnp.float32)]),
        out_shape=[jax.ShapeDtypeStruct((slots, 3 * width), jnp.bfloat16), jax.ShapeDtypeStruct((1, 2 * width), jnp.float32)],
        compiler_params=params(32),
        cost_estimate=cost(0),
        name="attention_grad",
    )(ends, queries, keys, values, outer, context, total)


def feed_kernel(
    ends_ref, hidden_ref, normed_one_any, first_gain_ref, first_shift_ref, expand_ref, expand_bias_ref,
    reduce_ref, reduce_bias_ref, gain_ref, shift_ref, active_ref, slope_ref, out_any, normed_any, inverse_ref, summary_ref, total, normed_one, normed, out, moved,
):
    step = pl.program_id(0)
    slots = hidden_ref.shape[0]

    arrive = pltpu.make_async_copy(normed_one_any, normed_one, moved.at[0])
    leave = [
        pltpu.make_async_copy(normed, normed_any, moved.at[1]),
        pltpu.make_async_copy(out, out_any, moved.at[2]),
    ]

    @pl.when(step == 0)
    def _():
        arrive.start()
        total[...] = jnp.zeros_like(total)

    for block in range(slots // WIDE):
        rows = slice(block * WIDE, (block + 1) * WIDE)
        inner = product(hidden_ref[rows, :], expand_ref[...]) + expand_bias_ref[...].astype(
            jnp.float32
        )
        normal_cdf = 0.5 * (1.0 + lax.erf(inner * INV_ROOT_TWO))
        slope = normal_cdf + inner * jnp.exp(-0.5 * inner * inner) * INV_ROOT_TAU
        active = (inner * normal_cdf).astype(jnp.bfloat16)
        active_ref[rows, :] = active
        slope_ref[rows, :] = slope.astype(jnp.bfloat16)
        total[rows, :] += product(active, reduce_ref[...])

    @pl.when(step == pl.num_programs(0) - 1)
    def _():
        arrive.wait()
        first_gain = first_gain_ref[...].astype(jnp.float32)
        first_shift = first_shift_ref[...].astype(jnp.float32)

        for block in range(slots // WIDE):
            rows = slice(block * WIDE, (block + 1) * WIDE)
            hidden = normed_one[rows, :] * first_gain + first_shift
            second = total[rows, :] + reduce_bias_ref[...].astype(jnp.float32)
            result, made, inverse = norm_forward(
                hidden + second,
                gain_ref[...].astype(jnp.float32),
                shift_ref[...].astype(jnp.float32),
            )
            total[rows, :] = result
            out[rows, :] = result.astype(jnp.bfloat16)
            normed[rows, :] = made
            inverse_ref[rows, :] = inverse
            pltpu.make_async_copy(normed.at[rows], normed_any.at[rows], moved.at[1]).start()
            pltpu.make_async_copy(out.at[rows], out_any.at[rows], moved.at[2]).start()
        for number in range(ends_ref.shape[0]):
            begin = ends_ref[number - 1] if number else 0
            summary_ref[number : number + 1, :] = total[pl.ds(begin, 1), :].astype(jnp.bfloat16)
        for copy in leave:
            copy.wait()


def feed(ends, hidden, normed_one, first_gain, first_shift, expand, expand_bias, reduce, reduce_bias, gain, shift):
    slots = hidden.shape[0]
    width = expand.shape[1]
    row = constant((1, D))
    return pl.pallas_call(
        feed_kernel,
        grid_spec=pltpu.PrefetchScalarGridSpec(
            num_scalar_prefetch=1,
            grid=(width // FF_BLOCK,),
            in_specs=[
                constant(hidden.shape),
                pl.BlockSpec(memory_space=pl.ANY),
                row,
                row,
                pl.BlockSpec((D, FF_BLOCK), lambda i, *_: (0, i)),
                pl.BlockSpec((1, FF_BLOCK), lambda i, *_: (0, i)),
                pl.BlockSpec((FF_BLOCK, D), lambda i, *_: (i, 0)),
                row,
                row,
                row,
            ],
            out_specs=[
                pl.BlockSpec((slots, FF_BLOCK), lambda i, *_: (0, i)),
                pl.BlockSpec((slots, FF_BLOCK), lambda i, *_: (0, i)),
                pl.BlockSpec(memory_space=pl.ANY),
                pl.BlockSpec(memory_space=pl.ANY),
                pl.BlockSpec((slots, 1), lambda i, *_: (0, 0)),
                pl.BlockSpec((ends.shape[0], D), lambda i, *_: (0, 0)),
            ],
            scratch_shapes=[pltpu.VMEM((slots, D), jnp.float32)] * 3
            + [pltpu.VMEM((slots, D), jnp.bfloat16), pltpu.SemaphoreType.DMA((3,))],
        ),
        out_shape=[
            jax.ShapeDtypeStruct((slots, width), jnp.bfloat16),
            jax.ShapeDtypeStruct((slots, width), jnp.bfloat16),
            jax.ShapeDtypeStruct((slots, D), jnp.bfloat16),
            jax.ShapeDtypeStruct((slots, D), jnp.float32),
            jax.ShapeDtypeStruct((slots, 1), jnp.float32),
            jax.ShapeDtypeStruct((ends.shape[0], D), jnp.bfloat16),
        ],
        compiler_params=params(30),
        cost_estimate=COST,
        name="feed",
    )(ends, hidden, normed_one, first_gain, first_shift, expand, expand_bias, reduce, reduce_bias, gain, shift)


def split_halves(made, own_ref, sent_ref, odd, piece):
    own_ref[...] = made
    if sent_ref is not None:
        pairs = made.shape[0] // (2 * piece)
        both = made.reshape(pairs, 2, piece, made.shape[1])
        sent_ref[...] = jnp.where(odd, both[:, 0], both[:, 1]).reshape(sent_ref.shape)


def reduce_grad_kernel(
    ends_ref, index_ref, cotangent_ref, normed_ref, inverse_ref, gain_ref, summary_grad_ref, active_ref,
    residual_ref, low_out_ref, sums_ref, own_ref, *rest, piece, tiles,
):
    sent_ref = rest[0] if len(rest) == 2 else None
    low = rest[-1]
    step = pl.program_id(0)

    @pl.when(step == 0)
    def _():
        sums_ref[...] = jnp.zeros_like(sums_ref)

    @pl.when(step < tiles)
    def _():
        first = step * WIDE
        live = ends_ref[ends_ref.shape[0] - 1]
        slot = lax.broadcasted_iota(jnp.int32, (WIDE, 1), 0) + first
        residual_ref[...] = jnp.where(slot < live, cotangent_ref[...].astype(jnp.float32), 0.0)
        for number in range(ends_ref.shape[0]):
            begin = (ends_ref[number - 1] if number else 0) - first

            @pl.when((begin >= 0) & (begin < WIDE))
            def _():
                residual_ref[pl.ds(begin, 1), :] += summary_grad_ref[number : number + 1, :]

        residual, gain_sum, shift_sum = norm_backward(
            residual_ref[...], normed_ref[...], inverse_ref[...], gain_ref[...].astype(jnp.float32)
        )
        made = residual.astype(jnp.bfloat16)
        residual_ref[...] = residual
        low_out_ref[...] = made
        low[pl.ds(first, WIDE), :] = made
        sums_ref[0:1, :] += gain_sum[None]
        sums_ref[1:2, :] += shift_sum[None]
        sums_ref[2:3, :] += jnp.sum(made.astype(jnp.float32), axis=0, keepdims=True)

    @pl.when(step >= tiles)
    def _():
        made = contract_rows(active_ref[...], low[...]).astype(jnp.bfloat16)
        split_halves(made, own_ref, sent_ref, index_ref[0] % 2 == 1, piece)


def reduce_grad(ends, index, count, cotangent, normed, inverse, gain, summary_grad, active):
    slots, width = active.shape
    piece = width // count
    halves = count == 16
    tiles = slots // WIDE
    row = lambda columns: pl.BlockSpec(
        (WIDE, columns), lambda i, *_: (jnp.minimum(i, tiles - 1), 0)
    )
    later = lambda i: jnp.maximum(i - tiles, 0)
    out_specs = [
        row(D),
        row(D),
        pl.BlockSpec((8, D), lambda i, *_: (0, 0)),
        pl.BlockSpec((D, D), lambda i, *_: (later(i), 0)),
    ]
    out_shape = [
        jax.ShapeDtypeStruct((slots, D), jnp.float32),
        jax.ShapeDtypeStruct((slots, D), jnp.bfloat16),
        jax.ShapeDtypeStruct((8, D), jnp.float32),
        jax.ShapeDtypeStruct((width, D), jnp.bfloat16),
    ]
    if halves:
        out_specs.append(pl.BlockSpec((D // 2, D), lambda i, *_: (later(i), 0)))
        out_shape.append(jax.ShapeDtypeStruct((width // 2, D), jnp.bfloat16))
    return pl.pallas_call(
        functools.partial(reduce_grad_kernel, piece=piece, tiles=tiles),
        grid_spec=pltpu.PrefetchScalarGridSpec(
            num_scalar_prefetch=2,
            grid=(tiles + width // D,),
            in_specs=[
                row(D),
                row(D),
                row(1),
                constant(gain.shape),
                constant(summary_grad.shape),
                pl.BlockSpec((slots, D), lambda i, *_: (0, later(i))),
            ],
            out_specs=out_specs,
            scratch_shapes=[pltpu.VMEM((slots, D), jnp.bfloat16)],
        ),
        out_shape=out_shape,
        compiler_params=params(28),
        cost_estimate=COST,
        name="reduce_grad",
    )(ends, index, cotangent, normed, inverse, gain, summary_grad, active)


def feed_grad_kernel(
    index_ref, low_ref, hidden_ref, reduce_ref, slope_ref, expand_ref, residual_any,
    expand_sums_ref, total_any, own_ref, *rest, piece, blocks,
):
    sent_ref = rest[0] if len(rest) == 5 else None
    inner, total, residual, moved = rest[-4:]
    step = pl.program_id(0)
    slots = low_ref.shape[0]
    arrive = pltpu.make_async_copy(residual_any, residual, moved.at[0])

    @pl.when(step == 0)
    def _():
        arrive.start()
        total[...] = jnp.zeros_like(total)

    sums = jnp.zeros(expand_sums_ref.shape, jnp.float32)
    for block in range(slots // WIDE):
        rows = slice(block * WIDE, (block + 1) * WIDE)
        grad = contract_cols(low_ref[rows, :], reduce_ref[...])
        made = (grad * slope_ref[rows, :].astype(jnp.float32)).astype(jnp.bfloat16)
        inner[rows, :] = made
        sums = sums + jnp.sum(made.astype(jnp.float32), axis=0, keepdims=True)
        total[rows, :] += contract_cols(made, expand_ref[...])
    expand_sums_ref[...] = sums

    @pl.when(step == blocks - 1)
    def _():
        arrive.wait()
        total[...] += residual[...]
        pltpu.make_async_copy(total, total_any, moved.at[1]).start()

    gradient = contract_rows(hidden_ref[...], inner[...]).astype(jnp.bfloat16)
    split_halves(gradient, own_ref, sent_ref, index_ref[0] % 2 == 1, piece)

    @pl.when(step == blocks - 1)
    def _():
        pltpu.make_async_copy(total, total_any, moved.at[1]).wait()


def feed_grad(index, count, low, hidden, reduce, slope, expand, residual):
    slots, width = slope.shape
    halves = count == 16
    blocks = width // D
    out_specs = [
        pl.BlockSpec((1, D), lambda i, *_: (0, i)),
        pl.BlockSpec(memory_space=pl.ANY),
        pl.BlockSpec((D, D), lambda i, *_: (0, i)),
    ]
    out_shape = [
        jax.ShapeDtypeStruct((1, width), jnp.float32),
        jax.ShapeDtypeStruct((slots, D), jnp.float32),
        jax.ShapeDtypeStruct((D, width), jnp.bfloat16),
    ]
    if halves:
        out_specs.append(pl.BlockSpec((D // 2, D), lambda i, *_: (0, i)))
        out_shape.append(jax.ShapeDtypeStruct((D // 2, width), jnp.bfloat16))
    return pl.pallas_call(
        functools.partial(feed_grad_kernel, piece=D // count, blocks=blocks),
        grid_spec=pltpu.PrefetchScalarGridSpec(
            num_scalar_prefetch=1,
            grid=(blocks,),
            in_specs=[
                constant(low.shape),
                constant(hidden.shape),
                pl.BlockSpec((D, D), lambda i, *_: (i, 0)),
                pl.BlockSpec((slots, D), lambda i, *_: (0, i)),
                pl.BlockSpec((D, D), lambda i, *_: (0, i)),
                pl.BlockSpec(memory_space=pl.ANY),
            ],
            out_specs=out_specs,
            scratch_shapes=[
                pltpu.VMEM((slots, D), jnp.bfloat16),
                pltpu.VMEM((slots, D), jnp.float32),
                pltpu.VMEM((slots, D), jnp.float32),
                pltpu.SemaphoreType.DMA((2,)),
            ],
        ),
        out_shape=out_shape,
        compiler_params=params(56),
        cost_estimate=COST,
        name="feed_grad",
    )(index, low, hidden, reduce, slope, expand, residual)


def output_grad_kernel(
    index_ref, hidden_grad_ref, normed_ref, inverse_ref, context_ref, gain_ref, output_ref,
    residual_ref, context_grad_ref, sums_ref, own_ref, *rest, piece,
):
    sent_ref = rest[0] if len(rest) == 2 else None
    total = rest[-1]
    step = pl.program_id(0)

    @pl.when(step == 0)
    def _():
        sums_ref[...] = jnp.zeros_like(sums_ref)
        total[...] = jnp.zeros_like(total)

    residual, gain_sum, shift_sum = norm_backward(
        hidden_grad_ref[...],
        normed_ref[...],
        inverse_ref[...],
        gain_ref[...].astype(jnp.float32),
    )
    branch = residual.astype(jnp.bfloat16)
    residual_ref[...] = residual
    sums_ref[0:1, :] += gain_sum[None]
    sums_ref[1:2, :] += shift_sum[None]
    sums_ref[2:3, :] += jnp.sum(branch.astype(jnp.float32), axis=0, keepdims=True)
    context_grad_ref[...] = contract_cols(branch, output_ref[...]).astype(jnp.bfloat16)
    total[...] += contract_rows(context_ref[...], branch)

    @pl.when(step == pl.num_programs(0) - 1)
    def _():
        split_halves(
            total[...].astype(jnp.bfloat16), own_ref, sent_ref, index_ref[0] % 2 == 1, piece
        )


def output_grad(index, count, width, hidden_grad, normed, inverse, context, gain, output):
    slots = hidden_grad.shape[0]
    halves = count == 16
    place = width // D - 1
    tile = lambda columns: pl.BlockSpec((WIDE, columns), lambda i, *_: (i, 0))
    out_specs = [
        tile(D),
        tile(D),
        pl.BlockSpec((8, D), lambda i, *_: (0, 0)),
        pl.BlockSpec((D, D), lambda i, *_: (0, place)),
    ]
    out_shape = [
        jax.ShapeDtypeStruct((slots, D), jnp.float32),
        jax.ShapeDtypeStruct((slots, D), jnp.bfloat16),
        jax.ShapeDtypeStruct((8, D), jnp.float32),
        jax.ShapeDtypeStruct((D, width), jnp.bfloat16),
    ]
    if halves:
        out_specs.append(pl.BlockSpec((D // 2, D), lambda i, *_: (0, place)))
        out_shape.append(jax.ShapeDtypeStruct((D // 2, width), jnp.bfloat16))
    return pl.pallas_call(
        functools.partial(output_grad_kernel, piece=D // count),
        grid_spec=pltpu.PrefetchScalarGridSpec(
            num_scalar_prefetch=1,
            grid=(slots // WIDE,),
            in_specs=[tile(D), tile(D), tile(1), tile(D), constant(gain.shape), constant(output.shape)],
            out_specs=out_specs,
            scratch_shapes=[pltpu.VMEM((D, D), jnp.float32)],
        ),
        out_shape=out_shape,
        compiler_params=params(32),
        cost_estimate=COST,
        name="output_grad",
    )(index, hidden_grad, normed, inverse, context, gain, output)


def attend_grad_kernel(index_ref, tokens_ref, projected_ref, *rest, piece, halves):
    own_ref, sent_ref = rest[-2:] if halves else (rest[-1], None)
    made = contract_rows(tokens_ref[...], projected_ref[...]).astype(jnp.bfloat16)
    split_halves(made, own_ref, sent_ref, index_ref[0] % 2 == 1, piece)


def attend_grad(index, count, tokens, projected_grad, extra=0, carried=()):
    slots, width = projected_grad.shape
    halves = count == 16
    heights = (D, D // 2) if halves else (D,)
    block = width // 3
    shapes = [jax.ShapeDtypeStruct(x.shape, x.dtype) for x in carried] or [
        jax.ShapeDtypeStruct((height, width + extra), jnp.bfloat16) for height in heights
    ]
    return pl.pallas_call(
        functools.partial(attend_grad_kernel, piece=D // count, halves=halves),
        grid_spec=pltpu.PrefetchScalarGridSpec(
            num_scalar_prefetch=1,
            grid=(3,),
            in_specs=[
                constant(tokens.shape),
                pl.BlockSpec((slots, block), lambda i, *_: (0, i)),
            ]
            + [pl.BlockSpec(memory_space=pl.ANY)] * len(carried),
            out_specs=[pl.BlockSpec((height, block), lambda i, *_: (0, i)) for height in heights],
        ),
        out_shape=shapes,
        input_output_aliases={3 + i: i for i in range(len(carried))},
        compiler_params=params(20),
        cost_estimate=cost(0),
        name="attend_grad",
    )(index, tokens, projected_grad, *carried)


def joined(refs, part):
    return jnp.concatenate(
        [
            ref[:, part * (ref.shape[1] // 3) : (part + 1) * (ref.shape[1] // 3)]
            for ref in refs
        ],
        axis=1,
    )


def tokens_grad_kernel(early_ref, late_ref, attend_ref, residual_ref, out_ref):
    total = residual_ref[...]
    for third in range(3):
        total = total + contract_cols(
            joined((early_ref, late_ref), third), attend_ref[:, third * D : (third + 1) * D]
        )
    out_ref[...] = total.astype(jnp.bfloat16)


def tokens_grad_of(early, late, attend, residual):
    slots = early.shape[0]
    tile = lambda columns: pl.BlockSpec((WIDE, columns), lambda i: (i, 0))
    return pl.pallas_call(
        tokens_grad_kernel,
        grid=(slots // WIDE,),
        in_specs=[tile(early.shape[1]), tile(late.shape[1]), constant(attend.shape), tile(D)],
        out_specs=tile(D),
        out_shape=jax.ShapeDtypeStruct((slots, D), jnp.bfloat16),
        compiler_params=params(16),
        cost_estimate=cost(0),
        name="tokens_grad",
    )(early, late, attend, residual)


def pack_kernel(index_ref, second_ref, first_ref, early_ref, late_ref, expand_ref, own_any, sent_any, own_ref, sent_ref, rows, *, count):
    width = D // count
    rows[...] = jnp.zeros_like(rows)
    vectors = [
        jnp.concatenate(
            [
                ref[0:1, part * (ref.shape[1] // 2) : (part + 1) * (ref.shape[1] // 2)]
                for ref in (early_ref, late_ref)
            ],
            axis=1,
        )
        for part in range(2)
    ]
    vectors += [first_ref[2:3, :], first_ref[0:1, :], first_ref[1:2, :]]
    vectors += [second_ref[2:3, :], second_ref[0:1, :], second_ref[1:2, :]]
    for number, vector in enumerate(vectors):
        rows[number : number + 1, :] = vector
    for number in range(count):
        for part in range(4):
            first = (number * 4 + part) * width
            rows[8 + part : 9 + part, number * width : (number + 1) * width] = expand_ref[
                0:1, first : first + width
            ]
    made = rows[...].T.astype(jnp.bfloat16)
    split_halves(made, own_ref, sent_ref, index_ref[0] % 2 == 1, width)


def pack(index, count, second, first, early, late, expand, own, sent):
    whole = lambda shape: pl.BlockSpec(shape, lambda i, *_: (0,) * len(shape))
    place = own.shape[1] // TILE - 1
    return pl.pallas_call(
        functools.partial(pack_kernel, count=count),
        grid_spec=pltpu.PrefetchScalarGridSpec(
            num_scalar_prefetch=1,
            grid=(1,),
            in_specs=[whole(x.shape) for x in (second, first, early, late, expand)]
            + [pl.BlockSpec(memory_space=pl.ANY)] * 2,
            out_specs=[
                pl.BlockSpec((D, TILE), lambda i, *_: (0, place)),
                pl.BlockSpec((D // 2, TILE), lambda i, *_: (0, place)),
            ],
            scratch_shapes=[pltpu.VMEM((TILE, D), jnp.float32)],
        ),
        out_shape=[jax.ShapeDtypeStruct(x.shape, x.dtype) for x in (own, sent)],
        input_output_aliases={6: 0, 7: 1},
        compiler_params=params(8),
        cost_estimate=cost(0),
        name="pack",
    )(index, second, first, early, late, expand, own, sent)


def merge_kernel(index_ref, *refs, count):
    total = refs[0][...].astype(jnp.float32)
    for ref in refs[1:count]:
        total = total + ref[...].astype(jnp.float32)
    refs[-1][...] = total.astype(refs[-1].dtype)


def merge(index, sources, stage, bits, kind, since, weight=1):
    rows, width = sources[0].shape[1:]
    made = 1 << max(bits - 1 - stage, 0)
    steps = min(made, 2)
    blocks = 3 if stage == bits and width % (3 * TILE) == 0 else 1
    block = (made // steps, 1, 1, rows, width // blocks)

    def spec(shift):
        def place(i, j, own):
            if stage == bits:
                return (0, 0, own[0] >> shift, 0, j)
            below = own[0] & ((1 << stage) - 1)
            return (i, 1 - ((own[0] >> stage) & 1), below >> shift, 0, j)

        return pl.BlockSpec(block, place)

    def view(source, shift):
        if stage == bits:
            source = source.reshape(1, 1, 1 << (bits - shift), rows, width)
        else:
            source = source.reshape(made, 2, 1 << (stage - shift), rows, width)
        return pltpu.with_memory_space_constraint(source, pltpu.HBM)

    return pl.pallas_call(
        functools.partial(merge_kernel, count=len(sources)),
        grid_spec=pltpu.PrefetchScalarGridSpec(
            num_scalar_prefetch=1,
            grid=(steps, blocks),
            in_specs=[spec(shift) for shift in range(len(sources))]
            + [pl.BlockSpec(memory_space=pl.ANY)] * len(since),
            out_specs=pl.BlockSpec(block, lambda i, j, own: (i, 0, 0, 0, j)),
        ),
        out_shape=jax.ShapeDtypeStruct((made, 1, 1, rows, width), kind),
        compiler_params=params(20),
        cost_estimate=cost(weight),
        name="merge",
    )(index, *[view(source, shift) for shift, source in enumerate(sources)], *since).reshape(made, rows, width)


def finish_kernel(index_ref, *refs, count):
    for sources, target in ((refs[:count], refs[-2]), (refs[count : 2 * count], refs[-1])):
        total = sources[0][...].astype(jnp.float32)
        for ref in sources[1:]:
            total = total + ref[...].astype(jnp.float32)
        target[...] = total


def finish(share, since, width, blocks, place, carried=()):
    rows, columns = share.terms[0].shape[1:]
    steps = 3 * blocks
    rest = (columns - steps * width) // TILE

    def view(source, shift):
        return source.reshape(1 << (share.bits - shift), rows, columns)

    def spec(shift, size, at):
        return pl.BlockSpec((1, rows, size), lambda j, own: (own[0] >> shift, 0, at(j)))

    following = lambda j: jnp.minimum(j, rest - 1)
    sources = [view(source, shift) for shift, source in enumerate(share.terms)]
    shifts = range(len(sources))
    out = pl.pallas_call(
        functools.partial(finish_kernel, count=len(sources)),
        grid_spec=pltpu.PrefetchScalarGridSpec(
            num_scalar_prefetch=1,
            grid=(steps,),
            in_specs=[spec(shift, width, lambda j: j) for shift in shifts]
            + [
                spec(shift, TILE, lambda j: steps * width // TILE + following(j))
                for shift in shifts
            ]
            + [pl.BlockSpec(memory_space=pl.ANY)] * (1 + len(carried)),
            out_specs=[
                pl.BlockSpec((1, rows, width), lambda j, own: (0, 0, place(j))),
                pl.BlockSpec((1, rows, TILE), lambda j, own: (0, 0, following(j))),
            ],
        ),
        out_shape=[
            jax.ShapeDtypeStruct((1, rows, 3 * D), jnp.float32),
            jax.ShapeDtypeStruct((1, rows, rest * TILE), jnp.float32),
        ],
        input_output_aliases={2 + 2 * len(sources): 0} if carried else {},
        compiler_params=params(20),
        cost_estimate=COST,
        name="finish",
    )(share.index, *sources, *sources, since, *carried)
    return out[0], out[1][0]


class Scatter:
    def __init__(self, index, count, own, sent=None):
        self.index, self.count, self.own = index, count, own
        self.stage = 0
        self.bits = 4
        self.sent = sent
        self.terms = []
        if sent is not None:
            pieces = (count, own.shape[0] // count, own.shape[1])
            self.terms = [own.reshape(pieces)]
            self.sent = sent.reshape((count // 2,) + pieces[1:])

    def begin(self, since=None, ahead=None, weight=1):
        if self.sent is None:
            return since, ahead
        if self.stage == 0:
            sent = self.sent
        else:
            sent = merge(
                self.index,
                self.terms,
                self.stage,
                self.bits,
                self.own.dtype,
                () if since is None else (since,),
                weight,
            )
        if ahead is not None:
            sent, ahead = lax.optimization_barrier((sent, ahead))
        self.terms.append(exchanged(sent, ("batch",), 1 << self.stage))
        self.stage += 1
        return sent, ahead

    def result(self, since=None, weight=1):
        if self.sent is None:
            return lax.psum_scatter(
                self.own.astype(jnp.float32), "batch", scatter_dimension=0, tiled=True
            )
        since = () if since is None else (since,)
        return merge(
            self.index, self.terms, self.stage, self.bits, jnp.float32, since, weight
        )[0]


def per_device(
    tokens,
    cotangent,
    question_lengths,
    passage_lengths,
    attend_weight,
    query_bias,
    value_bias,
    output_weight,
    output_bias,
    first_gain,
    first_shift,
    expand_weight,
    expand_bias,
    reduce_weight,
    reduce_bias,
    second_gain,
    second_shift,
):
    inputs = tokens[0]
    is_passage = lax.axis_index("enc") == 1
    count = lax.axis_size("batch")
    index = lax.axis_index("batch").astype(jnp.int32).reshape(1)
    lengths_here = jnp.where(is_passage, passage_lengths[0], question_lengths[0])
    order = jnp.arange(lengths_here.shape[0], dtype=jnp.int32)
    ends_here = jnp.sum(
        jnp.where(order[None, :] <= order[:, None], lengths_here[None, :], 0), axis=1
    )
    queries, keys, values, context, total, hidden_low, normed_one, inverse_one = attention(
        ends_here,
        inputs,
        attend_weight[0],
        query_bias,
        value_bias,
        output_weight[0],
        output_bias,
        first_gain,
        first_shift,
    )
    active, slope, result, normed_two, inverse_two, summary = feed(
        ends_here,
        hidden_low,
        normed_one,
        first_gain,
        first_shift,
        expand_weight[0],
        expand_bias,
        reduce_weight[0],
        reduce_bias,
        second_gain,
        second_shift,
    )
    mine, other, place = gathered_summaries(summary)
    seq_count = summary.shape[0]
    mine, other = mine.reshape(-1, D), other.reshape(-1, D)
    questions = jnp.where(is_passage, other, mine)
    passages = jnp.where(is_passage, mine, other)
    summary_scale = 2.0 / math.sqrt(D)
    total_seqs = questions.shape[0]
    logits = contract_cols(questions, passages) * summary_scale
    highest_logit = jnp.max(logits, axis=1, keepdims=True)
    logit_total = highest_logit + jnp.log(
        jnp.sum(jnp.exp(logits - highest_logit), axis=1, keepdims=True)
    )
    matches = jnp.eye(total_seqs, dtype=jnp.float32)
    score_grad = (LOSS_WEIGHT * (jnp.exp(logits - logit_total) - matches)).astype(jnp.bfloat16)
    own_rows = lax.dynamic_slice_in_dim(score_grad, place * seq_count, seq_count, 0)
    own_columns = lax.dynamic_slice_in_dim(score_grad, place * seq_count, seq_count, 1)
    question_term = (product(own_rows, passages) * summary_scale).astype(jnp.bfloat16)
    passage_term = contract_rows(own_columns, questions) * summary_scale
    summary_grad = jnp.where(is_passage, passage_term, question_term.astype(jnp.float32))
    residual_two, reduce_input, second_sums, *reduce_parts = reduce_grad(
        ends_here,
        index,
        count,
        cotangent[0],
        normed_two,
        inverse_two,
        second_gain,
        summary_grad,
        active,
    )
    reduce_share = Scatter(index, count, *reduce_parts)
    _, reduce_input = reduce_share.begin(ahead=reduce_input)
    expand_sums, hidden_grad, *expand_parts = feed_grad(
        index,
        count,
        reduce_input,
        hidden_low,
        reduce_weight[0],
        slope,
        expand_weight[0],
        residual_two,
    )
    _, hidden_grad = reduce_share.begin(since=hidden_grad, ahead=hidden_grad)
    expand_share = Scatter(index, count, *expand_parts)
    _, hidden_grad = expand_share.begin(ahead=hidden_grad)
    residual_one, context_grad, first_sums, *early_parts = output_grad(
        index,
        count,
        2 * EARLY * TILE + EARLY * TILE + D,
        hidden_grad,
        normed_one,
        inverse_one,
        context,
        first_gain,
        output_weight[0],
    )
    _, context_grad = expand_share.begin(since=context_grad, ahead=context_grad)
    projected = (ends_here, queries, keys, values)
    early_grad, early_bias = attention_grad(0, EARLY, *projected, context_grad, context, total)
    _, early_grad = reduce_share.begin(since=early_grad, ahead=early_grad, weight=3.541)
    early_parts = attend_grad(index, count, inputs, early_grad, carried=early_parts)
    early_share = Scatter(index, count, *early_parts)
    _, context_grad = early_share.begin(ahead=context_grad)
    _, context_grad = expand_share.begin(since=early_parts[0], ahead=context_grad, weight=5.880)
    late_grad, late_bias = attention_grad(
        EARLY, PAIRS - EARLY, *projected, context_grad, context, total
    )
    token, _ = early_share.begin(since=late_grad, weight=0.128)
    token, _ = reduce_share.begin(since=token, weight=0.949)
    token, late_grad = expand_share.begin(since=token, ahead=late_grad, weight=4.313)
    late_parts = attend_grad(
        index, count, inputs, late_grad, extra=TILE if count == 16 else 0
    )
    if count == 16:
        late_parts = pack(
            index,
            count,
            second_sums,
            first_sums,
            early_bias,
            late_bias,
            expand_sums,
            *late_parts,
        )
    late_share = Scatter(index, count, *late_parts)
    _, late_grad = late_share.begin(ahead=late_grad)
    tokens_grad = tokens_grad_of(early_grad, late_grad, attend_weight[0], residual_one)
    token, _ = early_share.begin(since=tokens_grad, weight=9.831)
    token, _ = late_share.begin(since=token, weight=1.601)
    reduced = reduce_share.result(since=token, weight=0.587)
    expanded = expand_share.result(since=reduced, weight=1.341)
    token, _ = early_share.begin(since=expanded, weight=1.345)
    token, _ = late_share.begin(since=token, weight=1.253)
    width = D // count
    wide, narrow = EARLY * TILE, (PAIRS - EARLY) * TILE
    if count == 16:
        token, _ = late_share.begin(since=token, weight=0.084)
        attended, output_share = finish(
            early_share, token, narrow, 2, lambda j: j // 2 * 3 + j % 2
        )
        attended, small = finish(
            late_share, output_share, narrow, 1, lambda j: j * 3 + 2, (attended,)
        )
    else:
        early, late = early_share.result(), late_share.result()
        output_share = early[:, 3 * wide :]
        attended = jnp.concatenate(
            [
                part
                for third in range(3)
                for part in (
                    early[:, third * wide : (third + 1) * wide],
                    late[:, third * narrow : (third + 1) * narrow],
                )
            ],
            axis=1,
        )[None]
    if count == 16:
        packed = small.T
        shares = [packed[i][None] for i in range(8)]
        expand_bias_share = packed[8:12].reshape(1, -1)
    else:
        vectors = [
            jnp.concatenate([early_bias[0, :wide], late_bias[0, :narrow]]),
            jnp.concatenate([early_bias[0, wide:], late_bias[0, narrow:]]),
        ]
        vectors += [first_sums[2], first_sums[0], first_sums[1]]
        vectors += [second_sums[2], second_sums[0], second_sums[1], expand_sums[0]]
        flat = jnp.concatenate([vector.reshape(count, -1) for vector in vectors], axis=1)
        packed = lax.psum_scatter(flat, "batch", scatter_dimension=0, tiled=True)[0]
        shares = [packed[None, i * width : (i + 1) * width] for i in range(8)]
        expand_bias_share = packed[None, 8 * width :]
    return (
        result[None],
        tokens_grad[None],
        attended,
        shares[0],
        shares[1],
        output_share[None],
        shares[2],
        shares[3],
        shares[4],
        expanded[None],
        expand_bias_share,
        reduced[None],
        shares[5],
        shares[6],
        shares[7],
    )


def solution(mesh):
    in_specs = (
        P("enc", "batch", None),
        P("enc", "batch", None),
        P("batch", None),
        P("batch", None),
        P("enc", None, None),
        P("enc", None),
        P("enc", None),
        P("enc", None, None),
        P("enc", None),
        P("enc", None),
        P("enc", None),
        P("enc", None, None),
        P("enc", None),
        P("enc", None, None),
        P("enc", None),
        P("enc", None),
        P("enc", None),
    )
    out_specs = (
        P("enc", "batch", None),
        P("enc", "batch", None),
        P("enc", "batch", None),
        P("enc", "batch"),
        P("enc", "batch"),
        P("enc", "batch", None),
        P("enc", "batch"),
        P("enc", "batch"),
        P("enc", "batch"),
        P("enc", "batch", None),
        P("enc", "batch"),
        P("enc", "batch", None),
        P("enc", "batch"),
        P("enc", "batch"),
        P("enc", "batch"),
    )
    return jax.shard_map(
        per_device, mesh=mesh, in_specs=in_specs, out_specs=out_specs, check_vma=False
    )
```

```python
import functools
import math

import jax
import jax.numpy as jnp
from jax import lax
from jax.experimental import pallas as pl
from jax.experimental.pallas import tpu as pltpu
from jax.sharding import PartitionSpec as P

D = 768
HEADS = 12
HEAD_DIM = 64
TILE = 128
WIDE = 2 * TILE
PAIRS = HEADS // 2
ROWS = 16
FF_BLOCK = 768
EARLY = 4


def cost(weight):
    return pl.CostEstimate(flops=int(weight * 2 * 10**9), bytes_accessed=10**3, transcendentals=0)


COST = cost(1)


EPSILON = 1e-12
SCORE_SCALE = 0.125
MASKED = -1000000000.0
LOSS_WEIGHT = 16.0
INV_ROOT_TWO = 0.7071067811865476
INV_ROOT_TAU = 0.3989422804014327


def exchanged(value, axes, distance):
    count = math.prod(lax.axis_size(axis) for axis in axes)
    return lax.ppermute(value, axes, [(source, source ^ distance) for source in range(count)])


def gathered_summaries(summary):
    count = lax.axis_size("batch")
    if count != 16:
        everything = lax.all_gather(summary, ("enc", "batch"), axis=0, tiled=False)
        own = lax.axis_index("enc")
        everything = everything.reshape((2, count) + summary.shape)
        mine = lax.dynamic_index_in_dim(everything, own, 0, keepdims=False)
        other = lax.dynamic_index_in_dim(everything, 1 - own, 0, keepdims=False)
        return mine, other, lax.axis_index("batch")
    both = ("enc", "batch")
    pair = jnp.stack([summary, exchanged(summary, both, 1)])
    mine = [pair, exchanged(pair, both, 2)]
    other = [exchanged(pair, both, 16), exchanged(pair, both, 18)]
    plane = jnp.concatenate(mine + other)
    parts = [plane] + [exchanged(plane, both, distance) for distance in (4, 8, 12)]
    size = plane.shape[0] // 2
    return (
        jnp.concatenate([part[:size] for part in parts]),
        jnp.concatenate([part[size:] for part in parts]),
        0,
    )


def product(left_side, right_side):
    return jnp.dot(left_side, right_side, preferred_element_type=jnp.float32)


def contract_rows(left_side, right_side):
    return lax.dot_general(
        left_side, right_side, (((0,), (0,)), ((), ())), preferred_element_type=jnp.float32
    )


def contract_cols(left_side, right_side):
    return lax.dot_general(
        left_side, right_side, (((1,), (1,)), ((), ())), preferred_element_type=jnp.float32
    )


def norm_forward(values, scale_row, shift_row):
    centred = values - jnp.mean(values, axis=1, keepdims=True)
    inverse = lax.rsqrt(jnp.mean(centred * centred, axis=1, keepdims=True) + EPSILON)
    normed = centred * inverse
    return (normed * scale_row + shift_row, normed, inverse)


def norm_backward(upstream, normed, inverse, scale_row):
    scale_grad = jnp.sum(upstream * normed, axis=0)
    shift_grad = jnp.sum(upstream, axis=0)
    scaled = upstream * scale_row
    centred = scaled - jnp.mean(scaled, axis=1, keepdims=True)
    centred = centred - normed * jnp.mean(scaled * normed, axis=1, keepdims=True)
    return (centred * inverse, scale_grad, shift_grad)


def params(megabytes):
    return pltpu.CompilerParams(vmem_limit_bytes=max(megabytes, 64) << 20)


def constant(shape):
    return pl.BlockSpec(shape, lambda *_: (0,) * len(shape), pipeline_mode=pl.Buffered(1))


def slot_segments(ends_ref, first, shape, axis):
    slots = lax.broadcasted_iota(jnp.int32, shape, axis) + first
    number = jnp.zeros(shape, jnp.int32)
    for j in range(ends_ref.shape[0]):
        number = number + (slots >= ends_ref[j]).astype(jnp.int32)
    return number

def key_tiles(ends_ref, first, last, slots):
    start, stop = jnp.int32(0), jnp.int32(slots)
    for j in reversed(range(ends_ref.shape[0])):
        end = ends_ref[j]
        start = jnp.maximum(start, jnp.where(end <= first, end, 0))
        stop = jnp.where(end > last, end, stop)
    return start // TILE, (stop + TILE - 1) // TILE

def head_masks(shape, axis):
    even = (lax.broadcasted_iota(jnp.int32, shape, axis) // HEAD_DIM) % 2 == 0
    return [m.astype(jnp.float32).astype(jnp.bfloat16) for m in (even, ~even)]

def columns(pair): return slice(pair * TILE, (pair + 1) * TILE)

def fill_stacks(source_ref, tiles, stack=None, turned=None):
    width = (stack if stack is not None else turned).shape[1]
    across = head_masks((1, width), 1)
    down = head_masks((width, TILE), 0)
    def one(tile, _):
        rows = source_ref[pl.ds(tile * TILE, TILE), :]
        if stack is not None:
            for side in range(2):
                stack[pl.ds(tile * WIDE + side * TILE, TILE), :] = rows * across[side]
        if turned is not None:
            flipped = rows.T
            for side in range(2):
                turned[tile, :, columns(side)] = flipped * down[side]
        return 0
    lax.fori_loop(0, tiles, one, 0)
    if stack is not None:
        stack[pl.ds(tiles * WIDE, WIDE), :] = jnp.zeros((WIDE, width), jnp.bfloat16)
    if turned is not None:
        turned[tiles] = jnp.zeros((width, WIDE), jnp.bfloat16)

def fill_segments(ends_ref, segments):
    def one(tile, _):
        segments[tile] = slot_segments(ends_ref, tile * TILE, (TILE, TILE), 0)
        return 0
    lax.fori_loop(0, segments.shape[0] - 1, one, 0)
    segments[segments.shape[0] - 1] = jnp.full((TILE, TILE), -1, jnp.int32)

def matching(segments, number, own):
    there = [segments[number], segments[number + 1]]
    return [jnp.concatenate([one, one], axis=1) == own for one in there]

def grouped(values): return values.reshape(TILE // 8, 8, WIDE)

def attention_kernel(ends_ref, tokens_ref, attend_any, query_bias_ref, value_bias_ref, output_ref, output_bias_ref, gain_ref, shift_ref, queries_any, keys_any, values_any, context_ref, total_ref, hidden_ref, normed_ref, inverse_ref, keys, values, segments, queries, scores, highest, sums, out, weights_in, queries_ref, keys_ref, values_ref, moved):
    tile = pl.program_id(0)
    slots = tokens_ref.shape[0]
    tiles = slots // TILE
    leaving = [
        pltpu.make_async_copy(source, target, moved.at[3 + third])
        for third, (source, target) in enumerate(
            ((queries_ref, queries_any), (keys_ref, keys_any), (values_ref, values_any))
        )
    ]
    @pl.when(tile == 0)
    def _():
        thirds = (
            (queries_ref, query_bias_ref),
            (keys_ref, None),
            (values_ref, value_bias_ref),
        )
        parts = [slice(third * D, (third + 1) * D) for third in range(3)]
        for third, part in enumerate(parts):
            pltpu.make_async_copy(
                attend_any.at[:, part], weights_in.at[third], moved.at[third]
            ).start()
        for third, (made_ref, bias_ref) in enumerate(thirds):
            pltpu.make_async_copy(
                attend_any.at[:, parts[third]], weights_in.at[third], moved.at[third]
            ).wait()
            for block in range(slots // WIDE):
                rows = slice(block * WIDE, (block + 1) * WIDE)
                made = product(tokens_ref[rows, :], weights_in[third])
                if bias_ref is not None:
                    made = made + bias_ref[...].astype(jnp.float32)
                made_ref[rows, :] = made.astype(jnp.bfloat16)
            leaving[third].start()
        fill_stacks(keys_ref, tiles, stack=keys)
        fill_stacks(values_ref, tiles, turned=values)
        fill_segments(ends_ref, segments)
    first = tile * WIDE
    low, high = key_tiles(ends_ref, first, first + WIDE - 1, slots)
    highest[...] = jnp.full_like(highest, -3e38)
    sums[...] = jnp.zeros_like(sums)
    out[...] = jnp.zeros_like(out)
    queries[...] = (queries_ref[pl.ds(first, WIDE), :] * jnp.bfloat16(SCORE_SCALE)).T
    own = slot_segments(ends_ref, first, (1, WIDE), 1)
    windows = (high - low + 1) // 2
    def score(window, _):
        number = low + 2 * window
        same = matching(segments, number, own)
        for pair in range(PAIRS):
            both = product(keys[pl.ds(number * WIDE, 2 * WIDE), columns(pair)], queries[columns(pair), :])
            for place in range(4):
                half = jnp.where(same[place // 2], both[columns(place), :], MASKED)
                scores[pair, window, columns(place), :] = half
                head = 2 * pair + place % 2
                highest[head] = jnp.maximum(highest[head], jnp.max(grouped(half), axis=0))
        return 0
    lax.fori_loop(0, windows, score, 0)
    for head in range(HEADS):
        highest[head] = jnp.broadcast_to(jnp.max(highest[head], axis=0, keepdims=True), (8, WIDE))
    def weigh(window, _):
        number = low + 2 * window
        for pair in range(PAIRS):
            parts = []
            for place in range(4):
                head = 2 * pair + place % 2
                weights = jnp.exp(scores[pair, window, columns(place), :] - highest[head, :1, :])
                sums[head] += jnp.sum(grouped(weights), axis=0)
                parts.append(weights.astype(jnp.bfloat16))
            there = jnp.concatenate([values[number, columns(pair), :], values[number + 1, columns(pair), :]], axis=1)
            out[columns(pair), :] += product(there, jnp.concatenate(parts, axis=0))
        return 0
    lax.fori_loop(0, windows, weigh, 0)
    for head in range(HEADS):
        total = jnp.sum(sums[head], axis=0, keepdims=True)
        part = slice(head * HEAD_DIM, (head + 1) * HEAD_DIM)
        out[part, :] = out[part, :] * (1.0 / total)
        total_ref[head : head + 1, :] = highest[head, :1, :] + jnp.log(total)
    total_ref[HEADS:, :] = jnp.zeros((ROWS - HEADS, WIDE), jnp.float32)
    context = out[...].T.astype(jnp.bfloat16)
    context_ref[...] = context
    branch = product(context, output_ref[...]) + output_bias_ref[...].astype(jnp.float32)
    hidden, normed, inverse = norm_forward(
        tokens_ref[pl.ds(first, WIDE), :].astype(jnp.float32) + branch,
        gain_ref[...].astype(jnp.float32),
        shift_ref[...].astype(jnp.float32),
    )
    hidden_ref[...] = hidden.astype(jnp.bfloat16)
    normed_ref[...] = normed
    inverse_ref[...] = inverse
    @pl.when(tile == pl.num_programs(0) - 1)
    def _():
        for copy in leaving:
            copy.wait()

def attention(ends, tokens, attend, query_bias, value_bias, output, output_bias, gain, shift):
    slots = tokens.shape[0]
    tiles = slots // TILE
    tile = pl.BlockSpec((WIDE, D), lambda i, e: (i, 0))
    return pl.pallas_call(
        attention_kernel,
        grid_spec=pltpu.PrefetchScalarGridSpec(
            num_scalar_prefetch=1,
            grid=(slots // WIDE,),
            in_specs=[
                constant(tokens.shape),
                pl.BlockSpec(memory_space=pl.ANY),
            ]
            + [constant(x.shape) for x in (query_bias, value_bias, output)]
            + [constant((1, D))] * 3,
            out_specs=[
            ]
            + [pl.BlockSpec(memory_space=pl.ANY)] * 3
            + [
                tile,
                pl.BlockSpec((ROWS, WIDE), lambda i, e: (0, i)),
                tile,
                tile,
                pl.BlockSpec((WIDE, 1), lambda i, e: (i, 0)),
            ],
            scratch_shapes=[
                pltpu.VMEM(((tiles + 1) * WIDE, D), jnp.bfloat16),
                pltpu.VMEM((tiles + 1, D, WIDE), jnp.bfloat16),
                pltpu.VMEM((tiles + 1, TILE, TILE), jnp.int32),
                pltpu.VMEM((D, WIDE), jnp.bfloat16),
                pltpu.VMEM((PAIRS, (tiles + 1) // 2, 2 * WIDE, WIDE), jnp.float32),
                pltpu.VMEM((HEADS, 8, WIDE), jnp.float32),
                pltpu.VMEM((HEADS, 8, WIDE), jnp.float32),
                pltpu.VMEM((D, WIDE), jnp.float32),
                pltpu.VMEM((3, D, D), jnp.bfloat16),
            ]
            + [pltpu.VMEM((slots, D), jnp.bfloat16)] * 3
            + [pltpu.SemaphoreType.DMA((6,))],
        ),
        out_shape=[
        ]
        + [jax.ShapeDtypeStruct((slots, D), jnp.bfloat16)] * 4
        + [
            jax.ShapeDtypeStruct((ROWS, slots), jnp.float32),
            jax.ShapeDtypeStruct((slots, D), jnp.bfloat16),
            jax.ShapeDtypeStruct((slots, D), jnp.float32),
            jax.ShapeDtypeStruct((slots, 1), jnp.float32),
        ],
        compiler_params=params(42),
        cost_estimate=COST,
        name="attention",
    )(ends, tokens, attend, query_bias, value_bias, output, output_bias, gain, shift)


def attention_grad_kernel(ends_ref, queries_ref, keys_ref, values_ref, outer_ref, context_ref, total_ref, out_ref, bias_ref, keys, values, turned, segments, queries, outers, query_sides, outer_sides, key_sum, value_sum, query_sum, deltas, *, first_head):
    tile = pl.program_id(0)
    slots, width = keys_ref.shape
    tiles = slots // TILE
    heads = width // HEAD_DIM
    live = (ends_ref[ends_ref.shape[0] - 1] + TILE - 1) // TILE
    first = tile * WIDE
    rows = pl.ds(first, WIDE)
    @pl.when(tile == 0)
    def _():
        fill_stacks(keys_ref, tiles, stack=keys, turned=turned)
        fill_stacks(values_ref, tiles, stack=values)
        fill_segments(ends_ref, segments)
        key_sum[...] = jnp.zeros_like(key_sum)
        value_sum[...] = jnp.zeros_like(value_sum)
        bias_ref[...] = jnp.zeros_like(bias_ref)
    @pl.when(first >= live * TILE)
    def _():
        out_ref[rows, :width] = jnp.zeros((WIDE, width), jnp.bfloat16)
    @pl.when(first < live * TILE)
    def _():
        low, high = key_tiles(ends_ref, first, first + WIDE - 1, slots)
        high = jnp.minimum(high, live)
        query_sum[...] = jnp.zeros_like(query_sum)
        across = head_masks((1, width), 1)
        scaled = queries_ref[...] * jnp.bfloat16(SCORE_SCALE)
        outer = outer_ref[...]
        queries[...] = scaled.T
        outers[...] = outer.T
        for side in range(2):
            query_sides[side] = scaled * across[side]
            outer_sides[side] = outer * across[side]
        both = (outer.astype(jnp.float32) * context_ref[...].astype(jnp.float32)).T
        for head in range(heads):
            deltas[head : head + 1, :] = jnp.sum(both[head * HEAD_DIM : (head + 1) * HEAD_DIM, :], axis=0, keepdims=True)
        own = slot_segments(ends_ref, first, (1, WIDE), 1)
        def visit(window, _):
            number = low + 2 * window
            same = matching(segments, number, own)
            there = pl.ds(number * WIDE, 2 * WIDE)
            where = pl.ds(number * TILE, WIDE)
            for pair in range(heads // 2):
                both = product(keys[there, columns(pair)], queries[columns(pair), :])
                grads = product(values[there, columns(pair)], outers[columns(pair), :])
                weights_parts, parts = [], []
                for place in range(4):
                    head = 2 * pair + place % 2
                    part = columns(place)
                    weights = jnp.where(same[place // 2], jnp.exp(both[part, :] - total_ref[first_head + head : first_head + head + 1, :]), 0.0)
                    parts.append((weights * (grads[part, :] - deltas[head : head + 1, :])).astype(jnp.bfloat16))
                    weights_parts.append(weights.astype(jnp.bfloat16))
                def folded(blocks, sides):
                    total = 0
                    for side in range(2):
                        total = total + product(jnp.concatenate(blocks[side::2], axis=0), sides[side, :, columns(pair)])
                    return total
                key_sum[where, columns(pair)] += folded(parts, query_sides)
                value_sum[where, columns(pair)] += folded(weights_parts, outer_sides)
                across = jnp.concatenate([turned[number, columns(pair), :], turned[number + 1, columns(pair), :]], axis=1)
                query_sum[columns(pair), :] += product(across, jnp.concatenate(parts, axis=0))
            return 0
        lax.fori_loop(0, (high - low + 1) // 2, visit, 0)
        done = (query_sum[...] * SCORE_SCALE).T.astype(jnp.bfloat16)
        out_ref[rows, :width] = done
        bias_ref[:, :width] += jnp.sum(done.astype(jnp.float32), axis=0, keepdims=True)
    @pl.when(tile == pl.num_programs(0) - 1)
    def _():
        def close(number, _):
            there = pl.ds(number * TILE, TILE)
            out_ref[there, width : 2 * width] = key_sum[there, :].astype(jnp.bfloat16)
            done = value_sum[there, :].astype(jnp.bfloat16)
            out_ref[there, 2 * width :] = done
            bias_ref[:, width:] += jnp.sum(done.astype(jnp.float32), axis=0, keepdims=True)
            return 0
        lax.fori_loop(0, tiles, close, 0)

def attention_grad(first_pair, pairs, ends, queries, keys, values, outer, context, total):
    slots = queries.shape[0]
    tiles = slots // TILE
    width = pairs * TILE
    place = first_pair // pairs
    whole = lambda i, e: (0, 0)
    return pl.pallas_call(
        functools.partial(attention_grad_kernel, first_head=2 * first_pair),
        grid_spec=pltpu.PrefetchScalarGridSpec(
            num_scalar_prefetch=1, grid=(slots // WIDE,),
            in_specs=[
                pl.BlockSpec((WIDE, width), lambda i, e: (i, place)),
                pl.BlockSpec((slots, width), lambda i, e: (0, place), pipeline_mode=pl.Buffered(1)),
                pl.BlockSpec((slots, width), lambda i, e: (0, place), pipeline_mode=pl.Buffered(1)),
                pl.BlockSpec((WIDE, width), lambda i, e: (i, place)),
                pl.BlockSpec((WIDE, width), lambda i, e: (i, place)),
                pl.BlockSpec((ROWS, WIDE), lambda i, e: (0, i)),
            ],
            out_specs=[pl.BlockSpec((slots, 3 * width), whole), pl.BlockSpec((1, 2 * width), whole)],
            scratch_shapes=[
                pltpu.VMEM(((tiles + 1) * WIDE, width), jnp.bfloat16), pltpu.VMEM(((tiles + 1) * WIDE, width), jnp.bfloat16), pltpu.VMEM((tiles + 1, width, WIDE), jnp.bfloat16),
                pltpu.VMEM((tiles + 1, TILE, TILE), jnp.int32),
                pltpu.VMEM((width, WIDE), jnp.bfloat16), pltpu.VMEM((width, WIDE), jnp.bfloat16),
                pltpu.VMEM((2, WIDE, width), jnp.bfloat16), pltpu.VMEM((2, WIDE, width), jnp.bfloat16),
                pltpu.VMEM((slots + TILE, width), jnp.float32), pltpu.VMEM((slots + TILE, width), jnp.float32), pltpu.VMEM((width, WIDE), jnp.float32),
                pltpu.VMEM((ROWS, WIDE), jnp.float32)]),
        out_shape=[jax.ShapeDtypeStruct((slots, 3 * width), jnp.bfloat16), jax.ShapeDtypeStruct((1, 2 * width), jnp.float32)],
        compiler_params=params(32),
        cost_estimate=cost(0),
        name="attention_grad",
    )(ends, queries, keys, values, outer, context, total)


def feed_kernel(
    ends_ref, hidden_ref, normed_one_any, first_gain_ref, first_shift_ref, expand_ref, expand_bias_ref,
    reduce_ref, reduce_bias_ref, gain_ref, shift_ref, active_ref, slope_ref, out_any, normed_any, inverse_ref, summary_ref, total, normed_one, normed, out, moved,
):
    step = pl.program_id(0)
    slots = hidden_ref.shape[0]

    arrive = pltpu.make_async_copy(normed_one_any, normed_one, moved.at[0])
    leave = [
        pltpu.make_async_copy(normed, normed_any, moved.at[1]),
        pltpu.make_async_copy(out, out_any, moved.at[2]),
    ]

    @pl.when(step == 0)
    def _():
        arrive.start()
        total[...] = jnp.zeros_like(total)

    for block in range(slots // WIDE):
        rows = slice(block * WIDE, (block + 1) * WIDE)
        inner = product(hidden_ref[rows, :], expand_ref[...]) + expand_bias_ref[...].astype(
            jnp.float32
        )
        normal_cdf = 0.5 * (1.0 + lax.erf(inner * INV_ROOT_TWO))
        slope = normal_cdf + inner * jnp.exp(-0.5 * inner * inner) * INV_ROOT_TAU
        active = (inner * normal_cdf).astype(jnp.bfloat16)
        active_ref[rows, :] = active
        slope_ref[rows, :] = slope.astype(jnp.bfloat16)
        total[rows, :] += product(active, reduce_ref[...])

    @pl.when(step == pl.num_programs(0) - 1)
    def _():
        arrive.wait()
        first_gain = first_gain_ref[...].astype(jnp.float32)
        first_shift = first_shift_ref[...].astype(jnp.float32)

        for block in range(slots // WIDE):
            rows = slice(block * WIDE, (block + 1) * WIDE)
            hidden = normed_one[rows, :] * first_gain + first_shift
            second = total[rows, :] + reduce_bias_ref[...].astype(jnp.float32)
            result, made, inverse = norm_forward(
                hidden + second,
                gain_ref[...].astype(jnp.float32),
                shift_ref[...].astype(jnp.float32),
            )
            total[rows, :] = result
            out[rows, :] = result.astype(jnp.bfloat16)
            normed[rows, :] = made
            inverse_ref[rows, :] = inverse
            pltpu.make_async_copy(normed.at[rows], normed_any.at[rows], moved.at[1]).start()
            pltpu.make_async_copy(out.at[rows], out_any.at[rows], moved.at[2]).start()
        for number in range(ends_ref.shape[0]):
            begin = ends_ref[number - 1] if number else 0
            summary_ref[number : number + 1, :] = total[pl.ds(begin, 1), :].astype(jnp.bfloat16)
        for copy in leave:
            copy.wait()


def feed(ends, hidden, normed_one, first_gain, first_shift, expand, expand_bias, reduce, reduce_bias, gain, shift):
    slots = hidden.shape[0]
    width = expand.shape[1]
    row = constant((1, D))
    return pl.pallas_call(
        feed_kernel,
        grid_spec=pltpu.PrefetchScalarGridSpec(
            num_scalar_prefetch=1,
            grid=(width // FF_BLOCK,),
            in_specs=[
                constant(hidden.shape),
                pl.BlockSpec(memory_space=pl.ANY),
                row,
                row,
                pl.BlockSpec((D, FF_BLOCK), lambda i, *_: (0, i)),
                pl.BlockSpec((1, FF_BLOCK), lambda i, *_: (0, i)),
                pl.BlockSpec((FF_BLOCK, D), lambda i, *_: (i, 0)),
                row,
                row,
                row,
            ],
            out_specs=[
                pl.BlockSpec((slots, FF_BLOCK), lambda i, *_: (0, i)),
                pl.BlockSpec((slots, FF_BLOCK), lambda i, *_: (0, i)),
                pl.BlockSpec(memory_space=pl.ANY),
                pl.BlockSpec(memory_space=pl.ANY),
                pl.BlockSpec((slots, 1), lambda i, *_: (0, 0)),
                pl.BlockSpec((ends.shape[0], D), lambda i, *_: (0, 0)),
            ],
            scratch_shapes=[pltpu.VMEM((slots, D), jnp.float32)] * 3
            + [pltpu.VMEM((slots, D), jnp.bfloat16), pltpu.SemaphoreType.DMA((3,))],
        ),
        out_shape=[
            jax.ShapeDtypeStruct((slots, width), jnp.bfloat16),
            jax.ShapeDtypeStruct((slots, width), jnp.bfloat16),
            jax.ShapeDtypeStruct((slots, D), jnp.bfloat16),
            jax.ShapeDtypeStruct((slots, D), jnp.float32),
            jax.ShapeDtypeStruct((slots, 1), jnp.float32),
            jax.ShapeDtypeStruct((ends.shape[0], D), jnp.bfloat16),
        ],
        compiler_params=params(30),
        cost_estimate=COST,
        name="feed",
    )(ends, hidden, normed_one, first_gain, first_shift, expand, expand_bias, reduce, reduce_bias, gain, shift)


def split_halves(made, own_ref, sent_ref, odd, piece):
    own_ref[...] = made
    if sent_ref is not None:
        pairs = made.shape[0] // (2 * piece)
        both = made.reshape(pairs, 2, piece, made.shape[1])
        sent_ref[...] = jnp.where(odd, both[:, 0], both[:, 1]).reshape(sent_ref.shape)


def reduce_grad_kernel(
    ends_ref, index_ref, cotangent_ref, normed_ref, inverse_ref, gain_ref, summary_grad_ref, active_ref,
    residual_ref, low_out_ref, sums_ref, own_ref, *rest, piece, tiles,
):
    sent_ref = rest[0] if len(rest) == 2 else None
    low = rest[-1]
    step = pl.program_id(0)

    @pl.when(step == 0)
    def _():
        sums_ref[...] = jnp.zeros_like(sums_ref)

    @pl.when(step < tiles)
    def _():
        first = step * WIDE
        live = ends_ref[ends_ref.shape[0] - 1]
        slot = lax.broadcasted_iota(jnp.int32, (WIDE, 1), 0) + first
        residual_ref[...] = jnp.where(slot < live, cotangent_ref[...].astype(jnp.float32), 0.0)
        for number in range(ends_ref.shape[0]):
            begin = (ends_ref[number - 1] if number else 0) - first

            @pl.when((begin >= 0) & (begin < WIDE))
            def _():
                residual_ref[pl.ds(begin, 1), :] += summary_grad_ref[number : number + 1, :]

        residual, gain_sum, shift_sum = norm_backward(
            residual_ref[...], normed_ref[...], inverse_ref[...], gain_ref[...].astype(jnp.float32)
        )
        made = residual.astype(jnp.bfloat16)
        residual_ref[...] = residual
        low_out_ref[...] = made
        low[pl.ds(first, WIDE), :] = made
        sums_ref[0:1, :] += gain_sum[None]
        sums_ref[1:2, :] += shift_sum[None]
        sums_ref[2:3, :] += jnp.sum(made.astype(jnp.float32), axis=0, keepdims=True)

    @pl.when(step >= tiles)
    def _():
        made = contract_rows(active_ref[...], low[...]).astype(jnp.bfloat16)
        split_halves(made, own_ref, sent_ref, index_ref[0] % 2 == 1, piece)


def reduce_grad(ends, index, count, cotangent, normed, inverse, gain, summary_grad, active):
    slots, width = active.shape
    piece = width // count
    halves = count == 16
    tiles = slots // WIDE
    row = lambda columns: pl.BlockSpec(
        (WIDE, columns), lambda i, *_: (jnp.minimum(i, tiles - 1), 0)
    )
    later = lambda i: jnp.maximum(i - tiles, 0)
    out_specs = [
        row(D),
        row(D),
        pl.BlockSpec((8, D), lambda i, *_: (0, 0)),
        pl.BlockSpec((D, D), lambda i, *_: (later(i), 0)),
    ]
    out_shape = [
        jax.ShapeDtypeStruct((slots, D), jnp.float32),
        jax.ShapeDtypeStruct((slots, D), jnp.bfloat16),
        jax.ShapeDtypeStruct((8, D), jnp.float32),
        jax.ShapeDtypeStruct((width, D), jnp.bfloat16),
    ]
    if halves:
        out_specs.append(pl.BlockSpec((D // 2, D), lambda i, *_: (later(i), 0)))
        out_shape.append(jax.ShapeDtypeStruct((width // 2, D), jnp.bfloat16))
    return pl.pallas_call(
        functools.partial(reduce_grad_kernel, piece=piece, tiles=tiles),
        grid_spec=pltpu.PrefetchScalarGridSpec(
            num_scalar_prefetch=2,
            grid=(tiles + width // D,),
            in_specs=[
                row(D),
                row(D),
                row(1),
                constant(gain.shape),
                constant(summary_grad.shape),
                pl.BlockSpec((slots, D), lambda i, *_: (0, later(i))),
            ],
            out_specs=out_specs,
            scratch_shapes=[pltpu.VMEM((slots, D), jnp.bfloat16)],
        ),
        out_shape=out_shape,
        compiler_params=params(28),
        cost_estimate=COST,
        name="reduce_grad",
    )(ends, index, cotangent, normed, inverse, gain, summary_grad, active)


def feed_grad_kernel(
    index_ref, low_ref, hidden_ref, reduce_ref, slope_ref, expand_ref, residual_any,
    expand_sums_ref, total_any, own_ref, *rest, piece, blocks,
):
    sent_ref = rest[0] if len(rest) == 5 else None
    inner, total, residual, moved = rest[-4:]
    step = pl.program_id(0)
    slots = low_ref.shape[0]
    arrive = pltpu.make_async_copy(residual_any, residual, moved.at[0])

    @pl.when(step == 0)
    def _():
        arrive.start()
        total[...] = jnp.zeros_like(total)

    sums = jnp.zeros(expand_sums_ref.shape, jnp.float32)
    for block in range(slots // WIDE):
        rows = slice(block * WIDE, (block + 1) * WIDE)
        grad = contract_cols(low_ref[rows, :], reduce_ref[...])
        made = (grad * slope_ref[rows, :].astype(jnp.float32)).astype(jnp.bfloat16)
        inner[rows, :] = made
        sums = sums + jnp.sum(made.astype(jnp.float32), axis=0, keepdims=True)
        total[rows, :] += contract_cols(made, expand_ref[...])
    expand_sums_ref[...] = sums

    @pl.when(step == blocks - 1)
    def _():
        arrive.wait()
        total[...] += residual[...]
        pltpu.make_async_copy(total, total_any, moved.at[1]).start()

    gradient = contract_rows(hidden_ref[...], inner[...]).astype(jnp.bfloat16)
    split_halves(gradient, own_ref, sent_ref, index_ref[0] % 2 == 1, piece)

    @pl.when(step == blocks - 1)
    def _():
        pltpu.make_async_copy(total, total_any, moved.at[1]).wait()


def feed_grad(index, count, low, hidden, reduce, slope, expand, residual):
    slots, width = slope.shape
    halves = count == 16
    blocks = width // D
    out_specs = [
        pl.BlockSpec((1, D), lambda i, *_: (0, i)),
        pl.BlockSpec(memory_space=pl.ANY),
        pl.BlockSpec((D, D), lambda i, *_: (0, i)),
    ]
    out_shape = [
        jax.ShapeDtypeStruct((1, width), jnp.float32),
        jax.ShapeDtypeStruct((slots, D), jnp.float32),
        jax.ShapeDtypeStruct((D, width), jnp.bfloat16),
    ]
    if halves:
        out_specs.append(pl.BlockSpec((D // 2, D), lambda i, *_: (0, i)))
        out_shape.append(jax.ShapeDtypeStruct((D // 2, width), jnp.bfloat16))
    return pl.pallas_call(
        functools.partial(feed_grad_kernel, piece=D // count, blocks=blocks),
        grid_spec=pltpu.PrefetchScalarGridSpec(
            num_scalar_prefetch=1,
            grid=(blocks,),
            in_specs=[
                constant(low.shape),
                constant(hidden.shape),
                pl.BlockSpec((D, D), lambda i, *_: (i, 0)),
                pl.BlockSpec((slots, D), lambda i, *_: (0, i)),
                pl.BlockSpec((D, D), lambda i, *_: (0, i)),
                pl.BlockSpec(memory_space=pl.ANY),
            ],
            out_specs=out_specs,
            scratch_shapes=[
                pltpu.VMEM((slots, D), jnp.bfloat16),
                pltpu.VMEM((slots, D), jnp.float32),
                pltpu.VMEM((slots, D), jnp.float32),
                pltpu.SemaphoreType.DMA((2,)),
            ],
        ),
        out_shape=out_shape,
        compiler_params=params(56),
        cost_estimate=COST,
        name="feed_grad",
    )(index, low, hidden, reduce, slope, expand, residual)


def output_grad_kernel(
    index_ref, hidden_grad_ref, normed_ref, inverse_ref, context_ref, gain_ref, output_ref,
    residual_ref, context_grad_ref, sums_ref, own_ref, *rest, piece,
):
    sent_ref = rest[0] if len(rest) == 2 else None
    total = rest[-1]
    step = pl.program_id(0)

    @pl.when(step == 0)
    def _():
        sums_ref[...] = jnp.zeros_like(sums_ref)
        total[...] = jnp.zeros_like(total)

    residual, gain_sum, shift_sum = norm_backward(
        hidden_grad_ref[...],
        normed_ref[...],
        inverse_ref[...],
        gain_ref[...].astype(jnp.float32),
    )
    branch = residual.astype(jnp.bfloat16)
    residual_ref[...] = residual
    sums_ref[0:1, :] += gain_sum[None]
    sums_ref[1:2, :] += shift_sum[None]
    sums_ref[2:3, :] += jnp.sum(branch.astype(jnp.float32), axis=0, keepdims=True)
    context_grad_ref[...] = contract_cols(branch, output_ref[...]).astype(jnp.bfloat16)
    total[...] += contract_rows(context_ref[...], branch)

    @pl.when(step == pl.num_programs(0) - 1)
    def _():
        split_halves(
            total[...].astype(jnp.bfloat16), own_ref, sent_ref, index_ref[0] % 2 == 1, piece
        )


def output_grad(index, count, width, hidden_grad, normed, inverse, context, gain, output):
    slots = hidden_grad.shape[0]
    halves = count == 16
    place = width // D - 1
    tile = lambda columns: pl.BlockSpec((WIDE, columns), lambda i, *_: (i, 0))
    out_specs = [
        tile(D),
        tile(D),
        pl.BlockSpec((8, D), lambda i, *_: (0, 0)),
        pl.BlockSpec((D, D), lambda i, *_: (0, place)),
    ]
    out_shape = [
        jax.ShapeDtypeStruct((slots, D), jnp.float32),
        jax.ShapeDtypeStruct((slots, D), jnp.bfloat16),
        jax.ShapeDtypeStruct((8, D), jnp.float32),
        jax.ShapeDtypeStruct((D, width), jnp.bfloat16),
    ]
    if halves:
        out_specs.append(pl.BlockSpec((D // 2, D), lambda i, *_: (0, place)))
        out_shape.append(jax.ShapeDtypeStruct((D // 2, width), jnp.bfloat16))
    return pl.pallas_call(
        functools.partial(output_grad_kernel, piece=D // count),
        grid_spec=pltpu.PrefetchScalarGridSpec(
            num_scalar_prefetch=1,
            grid=(slots // WIDE,),
            in_specs=[tile(D), tile(D), tile(1), tile(D), constant(gain.shape), constant(output.shape)],
            out_specs=out_specs,
            scratch_shapes=[pltpu.VMEM((D, D), jnp.float32)],
        ),
        out_shape=out_shape,
        compiler_params=params(32),
        cost_estimate=COST,
        name="output_grad",
    )(index, hidden_grad, normed, inverse, context, gain, output)


def attend_grad_kernel(index_ref, tokens_ref, projected_ref, *rest, piece, halves):
    own_ref, sent_ref = rest[-2:] if halves else (rest[-1], None)
    made = contract_rows(tokens_ref[...], projected_ref[...]).astype(jnp.bfloat16)
    split_halves(made, own_ref, sent_ref, index_ref[0] % 2 == 1, piece)


def attend_grad(index, count, tokens, projected_grad, extra=0, carried=()):
    slots, width = projected_grad.shape
    halves = count == 16
    heights = (D, D // 2) if halves else (D,)
    block = width // 3
    shapes = [jax.ShapeDtypeStruct(x.shape, x.dtype) for x in carried] or [
        jax.ShapeDtypeStruct((height, width + extra), jnp.bfloat16) for height in heights
    ]
    return pl.pallas_call(
        functools.partial(attend_grad_kernel, piece=D // count, halves=halves),
        grid_spec=pltpu.PrefetchScalarGridSpec(
            num_scalar_prefetch=1,
            grid=(3,),
            in_specs=[
                constant(tokens.shape),
                pl.BlockSpec((slots, block), lambda i, *_: (0, i)),
            ]
            + [pl.BlockSpec(memory_space=pl.ANY)] * len(carried),
            out_specs=[pl.BlockSpec((height, block), lambda i, *_: (0, i)) for height in heights],
        ),
        out_shape=shapes,
        input_output_aliases={3 + i: i for i in range(len(carried))},
        compiler_params=params(20),
        cost_estimate=cost(0),
        name="attend_grad",
    )(index, tokens, projected_grad, *carried)


def joined(refs, part):
    return jnp.concatenate(
        [
            ref[:, part * (ref.shape[1] // 3) : (part + 1) * (ref.shape[1] // 3)]
            for ref in refs
        ],
        axis=1,
    )


def tokens_grad_kernel(early_ref, late_ref, attend_ref, residual_ref, out_ref):
    total = residual_ref[...]
    for third in range(3):
        total = total + contract_cols(
            joined((early_ref, late_ref), third), attend_ref[:, third * D : (third + 1) * D]
        )
    out_ref[...] = total.astype(jnp.bfloat16)


def tokens_grad_of(early, late, attend, residual):
    slots = early.shape[0]
    tile = lambda columns: pl.BlockSpec((WIDE, columns), lambda i: (i, 0))
    return pl.pallas_call(
        tokens_grad_kernel,
        grid=(slots // WIDE,),
        in_specs=[tile(early.shape[1]), tile(late.shape[1]), constant(attend.shape), tile(D)],
        out_specs=tile(D),
        out_shape=jax.ShapeDtypeStruct((slots, D), jnp.bfloat16),
        compiler_params=params(16),
        cost_estimate=cost(0),
        name="tokens_grad",
    )(early, late, attend, residual)


def pack_kernel(index_ref, second_ref, first_ref, early_ref, late_ref, expand_ref, own_any, sent_any, own_ref, sent_ref, rows, *, count):
    width = D // count
    rows[...] = jnp.zeros_like(rows)
    vectors = [
        jnp.concatenate(
            [
                ref[0:1, part * (ref.shape[1] // 2) : (part + 1) * (ref.shape[1] // 2)]
                for ref in (early_ref, late_ref)
            ],
            axis=1,
        )
        for part in range(2)
    ]
    vectors += [first_ref[2:3, :], first_ref[0:1, :], first_ref[1:2, :]]
    vectors += [second_ref[2:3, :], second_ref[0:1, :], second_ref[1:2, :]]
    for number, vector in enumerate(vectors):
        rows[number : number + 1, :] = vector
    for number in range(count):
        for part in range(4):
            first = (number * 4 + part) * width
            rows[8 + part : 9 + part, number * width : (number + 1) * width] = expand_ref[
                0:1, first : first + width
            ]
    made = rows[...].T.astype(jnp.bfloat16)
    split_halves(made, own_ref, sent_ref, index_ref[0] % 2 == 1, width)


def pack(index, count, second, first, early, late, expand, own, sent):
    whole = lambda shape: pl.BlockSpec(shape, lambda i, *_: (0,) * len(shape))
    place = own.shape[1] // TILE - 1
    return pl.pallas_call(
        functools.partial(pack_kernel, count=count),
        grid_spec=pltpu.PrefetchScalarGridSpec(
            num_scalar_prefetch=1,
            grid=(1,),
            in_specs=[whole(x.shape) for x in (second, first, early, late, expand)]
            + [pl.BlockSpec(memory_space=pl.ANY)] * 2,
            out_specs=[
                pl.BlockSpec((D, TILE), lambda i, *_: (0, place)),
                pl.BlockSpec((D // 2, TILE), lambda i, *_: (0, place)),
            ],
            scratch_shapes=[pltpu.VMEM((TILE, D), jnp.float32)],
        ),
        out_shape=[jax.ShapeDtypeStruct(x.shape, x.dtype) for x in (own, sent)],
        input_output_aliases={6: 0, 7: 1},
        compiler_params=params(8),
        cost_estimate=cost(0),
        name="pack",
    )(index, second, first, early, late, expand, own, sent)


def merge_kernel(index_ref, *refs, count):
    total = refs[0][...].astype(jnp.float32)
    for ref in refs[1:count]:
        total = total + ref[...].astype(jnp.float32)
    refs[-1][...] = total.astype(refs[-1].dtype)


def merge(index, sources, stage, bits, kind, since, weight=1):
    rows, width = sources[0].shape[1:]
    made = 1 << max(bits - 1 - stage, 0)
    steps = min(made, 2)
    blocks = 3 if stage == bits and width % (3 * TILE) == 0 else 1
    block = (made // steps, 1, 1, rows, width // blocks)

    def spec(shift):
        def place(i, j, own):
            if stage == bits:
                return (0, 0, own[0] >> shift, 0, j)
            below = own[0] & ((1 << stage) - 1)
            return (i, 1 - ((own[0] >> stage) & 1), below >> shift, 0, j)

        return pl.BlockSpec(block, place)

    def view(source, shift):
        if stage == bits:
            source = source.reshape(1, 1, 1 << (bits - shift), rows, width)
        else:
            source = source.reshape(made, 2, 1 << (stage - shift), rows, width)
        return pltpu.with_memory_space_constraint(source, pltpu.HBM)

    return pl.pallas_call(
        functools.partial(merge_kernel, count=len(sources)),
        grid_spec=pltpu.PrefetchScalarGridSpec(
            num_scalar_prefetch=1,
            grid=(steps, blocks),
            in_specs=[spec(shift) for shift in range(len(sources))]
            + [pl.BlockSpec(memory_space=pl.ANY)] * len(since),
            out_specs=pl.BlockSpec(block, lambda i, j, own: (i, 0, 0, 0, j)),
        ),
        out_shape=jax.ShapeDtypeStruct((made, 1, 1, rows, width), kind),
        compiler_params=params(20),
        cost_estimate=cost(weight),
        name="merge",
    )(index, *[view(source, shift) for shift, source in enumerate(sources)], *since).reshape(made, rows, width)


def finish_kernel(index_ref, *refs, count):
    for sources, target in ((refs[:count], refs[-2]), (refs[count : 2 * count], refs[-1])):
        total = sources[0][...].astype(jnp.float32)
        for ref in sources[1:]:
            total = total + ref[...].astype(jnp.float32)
        target[...] = total


def finish(share, since, width, blocks, place, carried=()):
    rows, columns = share.terms[0].shape[1:]
    steps = 3 * blocks
    rest = (columns - steps * width) // TILE

    def view(source, shift):
        return source.reshape(1 << (share.bits - shift), rows, columns)

    def spec(shift, size, at):
        return pl.BlockSpec((1, rows, size), lambda j, own: (own[0] >> shift, 0, at(j)))

    following = lambda j: jnp.minimum(j, rest - 1)
    sources = [view(source, shift) for shift, source in enumerate(share.terms)]
    shifts = range(len(sources))
    out = pl.pallas_call(
        functools.partial(finish_kernel, count=len(sources)),
        grid_spec=pltpu.PrefetchScalarGridSpec(
            num_scalar_prefetch=1,
            grid=(steps,),
            in_specs=[spec(shift, width, lambda j: j) for shift in shifts]
            + [
                spec(shift, TILE, lambda j: steps * width // TILE + following(j))
                for shift in shifts
            ]
            + [pl.BlockSpec(memory_space=pl.ANY)] * (1 + len(carried)),
            out_specs=[
                pl.BlockSpec((1, rows, width), lambda j, own: (0, 0, place(j))),
                pl.BlockSpec((1, rows, TILE), lambda j, own: (0, 0, following(j))),
            ],
        ),
        out_shape=[
            jax.ShapeDtypeStruct((1, rows, 3 * D), jnp.float32),
            jax.ShapeDtypeStruct((1, rows, rest * TILE), jnp.float32),
        ],
        input_output_aliases={2 + 2 * len(sources): 0} if carried else {},
        compiler_params=params(20),
        cost_estimate=COST,
        name="finish",
    )(share.index, *sources, *sources, since, *carried)
    return out[0], out[1][0]


class Scatter:
    def __init__(self, index, count, own, sent=None):
        self.index, self.count, self.own = index, count, own
        self.stage = 0
        self.bits = 4
        self.sent = sent
        self.terms = []
        if sent is not None:
            pieces = (count, own.shape[0] // count, own.shape[1])
            self.terms = [own.reshape(pieces)]
            self.sent = sent.reshape((count // 2,) + pieces[1:])

    def begin(self, since=None, ahead=None, weight=1):
        if self.sent is None:
            return since, ahead
        if self.stage == 0:
            sent = self.sent
        else:
            sent = merge(
                self.index,
                self.terms,
                self.stage,
                self.bits,
                self.own.dtype,
                () if since is None else (since,),
                weight,
            )
        if ahead is not None:
            sent, ahead = lax.optimization_barrier((sent, ahead))
        self.terms.append(exchanged(sent, ("batch",), 1 << self.stage))
        self.stage += 1
        return sent, ahead

    def result(self, since=None, weight=1):
        if self.sent is None:
            return lax.psum_scatter(
                self.own.astype(jnp.float32), "batch", scatter_dimension=0, tiled=True
            )
        since = () if since is None else (since,)
        return merge(
            self.index, self.terms, self.stage, self.bits, jnp.float32, since, weight
        )[0]


def per_device(
    tokens,
    cotangent,
    question_lengths,
    passage_lengths,
    attend_weight,
    query_bias,
    value_bias,
    output_weight,
    output_bias,
    first_gain,
    first_shift,
    expand_weight,
    expand_bias,
    reduce_weight,
    reduce_bias,
    second_gain,
    second_shift,
):
    inputs = tokens[0]
    is_passage = lax.axis_index("enc") == 1
    count = lax.axis_size("batch")
    index = lax.axis_index("batch").astype(jnp.int32).reshape(1)
    lengths_here = jnp.where(is_passage, passage_lengths[0], question_lengths[0])
    order = jnp.arange(lengths_here.shape[0], dtype=jnp.int32)
    ends_here = jnp.sum(
        jnp.where(order[None, :] <= order[:, None], lengths_here[None, :], 0), axis=1
    )
    queries, keys, values, context, total, hidden_low, normed_one, inverse_one = attention(
        ends_here,
        inputs,
        attend_weight[0],
        query_bias,
        value_bias,
        output_weight[0],
        output_bias,
        first_gain,
        first_shift,
    )
    active, slope, result, normed_two, inverse_two, summary = feed(
        ends_here,
        hidden_low,
        normed_one,
        first_gain,
        first_shift,
        expand_weight[0],
        expand_bias,
        reduce_weight[0],
        reduce_bias,
        second_gain,
        second_shift,
    )
    mine, other, place = gathered_summaries(summary)
    seq_count = summary.shape[0]
    mine, other = mine.reshape(-1, D), other.reshape(-1, D)
    questions = jnp.where(is_passage, other, mine)
    passages = jnp.where(is_passage, mine, other)
    summary_scale = 2.0 / math.sqrt(D)
    total_seqs = questions.shape[0]
    logits = contract_cols(questions, passages) * summary_scale
    highest_logit = jnp.max(logits, axis=1, keepdims=True)
    logit_total = highest_logit + jnp.log(
        jnp.sum(jnp.exp(logits - highest_logit), axis=1, keepdims=True)
    )
    matches = jnp.eye(total_seqs, dtype=jnp.float32)
    score_grad = (LOSS_WEIGHT * (jnp.exp(logits - logit_total) - matches)).astype(jnp.bfloat16)
    own_rows = lax.dynamic_slice_in_dim(score_grad, place * seq_count, seq_count, 0)
    own_columns = lax.dynamic_slice_in_dim(score_grad, place * seq_count, seq_count, 1)
    question_term = (product(own_rows, passages) * summary_scale).astype(jnp.bfloat16)
    passage_term = contract_rows(own_columns, questions) * summary_scale
    summary_grad = jnp.where(is_passage, passage_term, question_term.astype(jnp.float32))
    residual_two, reduce_input, second_sums, *reduce_parts = reduce_grad(
        ends_here,
        index,
        count,
        cotangent[0],
        normed_two,
        inverse_two,
        second_gain,
        summary_grad,
        active,
    )
    reduce_share = Scatter(index, count, *reduce_parts)
    _, reduce_input = reduce_share.begin(ahead=reduce_input)
    expand_sums, hidden_grad, *expand_parts = feed_grad(
        index,
        count,
        reduce_input,
        hidden_low,
        reduce_weight[0],
        slope,
        expand_weight[0],
        residual_two,
    )
    _, hidden_grad = reduce_share.begin(since=hidden_grad, ahead=hidden_grad)
    expand_share = Scatter(index, count, *expand_parts)
    _, hidden_grad = expand_share.begin(ahead=hidden_grad)
    residual_one, context_grad, first_sums, *early_parts = output_grad(
        index,
        count,
        2 * EARLY * TILE + EARLY * TILE + D,
        hidden_grad,
        normed_one,
        inverse_one,
        context,
        first_gain,
        output_weight[0],
    )
    _, context_grad = expand_share.begin(since=context_grad, ahead=context_grad)
    projected = (ends_here, queries, keys, values)
    early_grad, early_bias = attention_grad(0, EARLY, *projected, context_grad, context, total)
    _, early_grad = reduce_share.begin(since=early_grad, ahead=early_grad, weight=3.541)
    early_parts = attend_grad(index, count, inputs, early_grad, carried=early_parts)
    early_share = Scatter(index, count, *early_parts)
    _, context_grad = early_share.begin(ahead=context_grad)
    _, context_grad = expand_share.begin(since=early_parts[0], ahead=context_grad, weight=5.880)
    late_grad, late_bias = attention_grad(
        EARLY, PAIRS - EARLY, *projected, context_grad, context, total
    )
    token, _ = early_share.begin(since=late_grad, weight=0.128)
    token, _ = reduce_share.begin(since=token, weight=0.949)
    token, late_grad = expand_share.begin(since=token, ahead=late_grad, weight=4.313)
    late_parts = attend_grad(
        index, count, inputs, late_grad, extra=TILE if count == 16 else 0
    )
    if count == 16:
        late_parts = pack(
            index,
            count,
            second_sums,
            first_sums,
            early_bias,
            late_bias,
            expand_sums,
            *late_parts,
        )
    late_share = Scatter(index, count, *late_parts)
    _, late_grad = late_share.begin(ahead=late_grad)
    tokens_grad = tokens_grad_of(early_grad, late_grad, attend_weight[0], residual_one)
    token, _ = early_share.begin(since=tokens_grad, weight=9.831)
    token, _ = late_share.begin(since=token, weight=1.601)
    reduced = reduce_share.result(since=token, weight=0.587)
    expanded = expand_share.result(since=reduced, weight=1.341)
    token, _ = early_share.begin(since=expanded, weight=1.345)
    token, _ = late_share.begin(since=token, weight=1.253)
    width = D // count
    wide, narrow = EARLY * TILE, (PAIRS - EARLY) * TILE
    if count == 16:
        token, _ = late_share.begin(since=token, weight=0.084)
        attended, output_share = finish(
            early_share, token, narrow, 2, lambda j: j // 2 * 3 + j % 2
        )
        attended, small = finish(
            late_share, output_share, narrow, 1, lambda j: j * 3 + 2, (attended,)
        )
    else:
        early, late = early_share.result(), late_share.result()
        output_share = early[:, 3 * wide :]
        attended = jnp.concatenate(
            [
                part
                for third in range(3)
                for part in (
                    early[:, third * wide : (third + 1) * wide],
                    late[:, third * narrow : (third + 1) * narrow],
                )
            ],
            axis=1,
        )[None]
    if count == 16:
        packed = small.T
        shares = [packed[i][None] for i in range(8)]
        expand_bias_share = packed[8:12].reshape(1, -1)
    else:
        vectors = [
            jnp.concatenate([early_bias[0, :wide], late_bias[0, :narrow]]),
            jnp.concatenate([early_bias[0, wide:], late_bias[0, narrow:]]),
        ]
        vectors += [first_sums[2], first_sums[0], first_sums[1]]
        vectors += [second_sums[2], second_sums[0], second_sums[1], expand_sums[0]]
        flat = jnp.concatenate([vector.reshape(count, -1) for vector in vectors], axis=1)
        packed = lax.psum_scatter(flat, "batch", scatter_dimension=0, tiled=True)[0]
        shares = [packed[None, i * width : (i + 1) * width] for i in range(8)]
        expand_bias_share = packed[None, 8 * width :]
    return (
        result[None],
        tokens_grad[None],
        attended,
        shares[0],
        shares[1],
        output_share[None],
        shares[2],
        shares[3],
        shares[4],
        expanded[None],
        expand_bias_share,
        reduced[None],
        shares[5],
        shares[6],
        shares[7],
    )


def solution(mesh):
    in_specs = (
        P("enc", "batch", None),
        P("enc", "batch", None),
        P("batch", None),
        P("batch", None),
        P("enc", None, None),
        P("enc", None),
        P("enc", None),
        P("enc", None, None),
        P("enc", None),
        P("enc", None),
        P("enc", None),
        P("enc", None, None),
        P("enc", None),
        P("enc", None, None),
        P("enc", None),
        P("enc", None),
        P("enc", None),
    )
    out_specs = (
        P("enc", "batch", None),
        P("enc", "batch", None),
        P("enc", "batch", None),
        P("enc", "batch"),
        P("enc", "batch"),
        P("enc", "batch", None),
        P("enc", "batch"),
        P("enc", "batch"),
        P("enc", "batch"),
        P("enc", "batch", None),
        P("enc", "batch"),
        P("enc", "batch", None),
        P("enc", "batch"),
        P("enc", "batch"),
        P("enc", "batch"),
    )
    return jax.shard_map(
        per_device, mesh=mesh, in_specs=in_specs, out_specs=out_specs, check_vma=False
    )
```
